256 devices in a mesh: gx: 32 (over z_lo, x, y), gy: 8 (over z_hi, core).
Axes of the slice: x: 4, y: 4, z: 8 (z_hi: 4, z_lo: 2; z = z_hi * 2 + z_lo), core: 2. Of those that a mesh axis runs over, the one named last changes fastest.
Arguments:
- background_sample: float32 [64, 2, 4, 512, 1024], P(None, None, None, 'gx', 'gy'), may hold values from -6 to 6
- courant_eastward: float32 [2, 512, 1024], P(None, 'gx', 'gy'), may hold values from -0.3 to 0.3
- courant_northward: float32 [2, 512, 1024], P(None, 'gx', 'gy'), may hold values from -0.3 to 0.3
- diffusivity: float32 [512, 1024], P('gx', 'gy'), may hold values from 0.02 to 0.1
- sample_site: int32 [32, 8, 4, 128], P('gx', 'gy'), may hold values from 0 to 16383
- live_count: int32 [32, 8, 4], P('gx', 'gy'), may hold values from 1 to 128, as said below
- observed: float32 [32, 8, 4, 128], P('gx', 'gy'), may hold values from -8 to 8
- error_variance: float32 [32, 8, 4, 128], P('gx', 'gy'), may hold values from 4 to 40
- reach_mask: int32 [32, 8, 5, 5], P('gx', 'gy'), may hold values 0 or 1
Outputs:
- analysis: float32 [64, 2, 4, 512, 1024], P(None, None, None, 'gx', 'gy')
The draws below stay inside these ranges and needn't reach their ends.
Inputs may be any that keep to these rules, and one draw needn't show every extreme that they name: Slots 0 to live_count - 1 of a tile's batch hold its observations, the rest are unused; in every batch some tile has 128 of them.
All inputs are finite; a program needn't handle non-finite values. No bound on the sum of `reach_mask` on one device may be relied on, other than what follows from the above.
Results may differ from the reference program's by a relative error of at most 0.00015.
Values sent between devices are 32-bit elements; how exact they have to be, the bound alone decides.
A program may use at most 128 MiB of HBM per device.

```python
import math
import jax
import jax.numpy as jnp
from jax import lax

MEMBERS = 64
PROGNOSTIC_VARS = 4
VERTICAL_LAYERS = 2
PATCH_WIDTH_ZON = 16
PATCH_WIDTH_MER = 128
QMAX = 128
BATCHES = 4
RAD = 2
NS_STEPS = 6
PATCHES_ZONAL = 32
PATCHES_MERIDION = 8
NX = 512
NY = 1024


def draw_live_count(key, part):
    first_key, second_key = jax.random.split(jax.random.fold_in(key, 17))
    raw_draw = jax.random.randint(first_key, (PATCHES_ZONAL * PATCHES_MERIDION, BATCHES), 0, 64)
    base_count = 1 + raw_draw * (QMAX - 1) // 63
    busiest = jax.random.randint(second_key, (BATCHES,), 0, PATCHES_ZONAL * PATCHES_MERIDION)
    tile_index = jnp.arange(PATCHES_ZONAL * PATCHES_MERIDION)[:, None]
    filled = jnp.where(tile_index == busiest[None, :], QMAX, base_count)
    return filled.reshape(PATCHES_ZONAL, PATCHES_MERIDION, BATCHES).astype(jnp.int32)


def with_ends(values, own_key, smallest, largest):
    shape = values.shape
    place = [jax.random.randint(jax.random.fold_in(own_key, axis), (), 0, shape[axis]) for axis in range(len(shape))]
    values = values.at[tuple(place)].set(smallest)
    longest = shape.index(max(shape))
    place[longest] = (place[longest] + 1) % shape[longest]
    return values.at[tuple(place)].set(largest)


def shard_levels(rng, dims, cuts, smallest, top_value):
    level = 1.0
    for axis_at, shards_of in cuts:
        draws = jax.random.uniform(jax.random.fold_in(jax.random.fold_in(rng, 6), axis_at), (shards_of,), jnp.float32, smallest / len(cuts), top_value / len(cuts))
        level = level * jnp.repeat(jnp.exp(draws), dims[axis_at] // shards_of).reshape((-1,) + (1,) * (len(dims) - 1 - axis_at))
    return level


def scatter_about(stream_key, extent, width, limit, pieces=(), held_as=jnp.bfloat16):
    drawn = width * jax.random.normal(stream_key, extent, jnp.float32)
    if pieces:
        drawn = drawn * shard_levels(stream_key, extent, pieces, -0.22, 0.18)
    return jnp.clip(drawn, -limit, limit).astype(held_as)


def setup_inputs(seed: int = 0) -> dict:
    key_list = jax.random.split(jax.random.key(seed), 10)
    return {
        "background_sample": scatter_about(key_list[0], (MEMBERS, VERTICAL_LAYERS, PROGNOSTIC_VARS, NX, NY), 1.0, 6.0, ((3, 32), (4, 8)), jnp.float32),
        "courant_eastward": jnp.clip(jax.random.uniform(key_list[1], (VERTICAL_LAYERS, NX, NY), jnp.float32, -0.3, 0.3) * shard_levels(key_list[1], (VERTICAL_LAYERS, NX, NY), ((1, 32), (2, 8)), -0.4, 0.0), -0.3, 0.3),
        "courant_northward": jnp.clip(jax.random.uniform(key_list[2], (VERTICAL_LAYERS, NX, NY), jnp.float32, -0.3, 0.3) * shard_levels(key_list[2], (VERTICAL_LAYERS, NX, NY), ((1, 32), (2, 8)), -0.4, 0.0), -0.3, 0.3),
        "diffusivity": jnp.clip(jnp.exp(math.log(0.1) - 1.609438 * jax.random.uniform(key_list[3], (NX, NY), jnp.float32) ** shard_levels(key_list[3], (NX, NY), ((0, 32), (1, 8)), -0.2, 0.2)), 0.02, 0.1),
        "sample_site": with_ends(jax.random.randint(key_list[4], (PATCHES_ZONAL, PATCHES_MERIDION, BATCHES, QMAX), 0, VERTICAL_LAYERS * PROGNOSTIC_VARS * PATCH_WIDTH_ZON * PATCH_WIDTH_MER), jax.random.fold_in(key_list[4], 1), 0, (VERTICAL_LAYERS * PROGNOSTIC_VARS * PATCH_WIDTH_ZON * PATCH_WIDTH_MER) - 1).astype(jnp.int32),
        "live_count": draw_live_count(jax.random.fold_in(key_list[9], 71), 0),
        "observed": scatter_about(key_list[6], (PATCHES_ZONAL, PATCHES_MERIDION, BATCHES, QMAX), 1.5, 8.0, ((0, 32), (1, 8)), jnp.float32),
        "error_variance": jnp.clip(jnp.exp(math.log(40.0) - 2.3025851 * jax.random.uniform(key_list[7], (PATCHES_ZONAL, PATCHES_MERIDION, BATCHES, QMAX), jnp.float32) ** shard_levels(key_list[7], (PATCHES_ZONAL, PATCHES_MERIDION, BATCHES, QMAX), ((0, 32), (1, 8)), -0.2, 0.2)), 4.0, 40.0),
        "reach_mask": with_ends((jax.random.randint(key_list[8], (PATCHES_ZONAL, PATCHES_MERIDION, 2 * RAD + 1, 2 * RAD + 1), 0, 4) < 3).astype(jnp.int32), jax.random.fold_in(key_list[8], 1), 0, 1),
    }


def matmul_full(left, right):
    return jnp.dot(left, right, precision=lax.Precision.HIGHEST, preferred_element_type=jnp.float32)

def integrate_model_timestep(halo_padded, courant_eastward, courant_northward, diffusivity):
    centre = halo_padded[..., 1:-1, 1:-1]
    east_cell = halo_padded[..., 2:, 1:-1]
    west_cell = halo_padded[..., :-2, 1:-1]
    north_cell = halo_padded[..., 1:-1, 2:]
    south_cell = halo_padded[..., 1:-1, :-2]
    flux_x = jnp.maximum(courant_eastward, 0.0) * (centre - west_cell) + jnp.minimum(courant_eastward, 0.0) * (east_cell - centre)
    flux_y = jnp.maximum(courant_northward, 0.0) * (centre - south_cell) + jnp.minimum(courant_northward, 0.0) * (north_cell - centre)
    spread_term = diffusivity * (east_cell + west_cell + north_cell + south_cell - 4.0 * centre)
    return centre + spread_term - flux_x - flux_y

def mixing_matrix(gram_matrix, projection):
    realisation_vectors = gram_matrix.shape[0]
    identity = jnp.eye(realisation_vectors, dtype=jnp.float32)
    precision_matrix = identity + gram_matrix / (realisation_vectors - 1)
    frobenius = jnp.sqrt(jnp.sum(precision_matrix * precision_matrix))
    iterate = precision_matrix / frobenius
    inverse = identity
    for repeat in range(NS_STEPS):
        factor = 1.5 * identity - 0.5 * matmul_full(inverse, iterate)
        iterate = matmul_full(iterate, factor)
        inverse = matmul_full(factor, inverse)
    transform = inverse / jnp.sqrt(frobenius)
    weights = matmul_full(transform, matmul_full(transform, projection)) / (realisation_vectors - 1)
    return transform + weights[:, None]

def reference(background_sample, courant_eastward, courant_northward, diffusivity, sample_site, live_count, observed, error_variance, reach_mask):

    def integrate_single_realisation(member):
        halo_padded = jnp.pad(member, ((0, 0), (0, 0), (1, 1), (1, 1)))
        return integrate_model_timestep(halo_padded, courant_eastward[:, None], courant_northward[:, None], diffusivity)
    predicted_realisations = lax.map(integrate_single_realisation, background_sample)
    realisation_vectors = background_sample.shape[0]
    patch_model_vector = predicted_realisations.reshape(realisation_vectors, VERTICAL_LAYERS, PROGNOSTIC_VARS, PATCHES_ZONAL, PATCH_WIDTH_ZON, PATCHES_MERIDION, PATCH_WIDTH_MER).transpose(3, 5, 0, 1, 2, 4, 6)
    patch_model_vector = patch_model_vector.reshape(PATCHES_ZONAL, PATCHES_MERIDION, realisation_vectors, VERTICAL_LAYERS * PROGNOSTIC_VARS * PATCH_WIDTH_ZON * PATCH_WIDTH_MER)
    width_mask = 2 * RAD + 1
    centre_one = ((jnp.arange(width_mask)[:, None] == RAD) & (jnp.arange(width_mask)[None, :] == RAD)).astype(jnp.float32)
    reach = jnp.maximum(reach_mask.astype(jnp.float32), centre_one[None, None])
    slot_index = jnp.arange(QMAX)
    for batch_index in range(BATCHES):
        site_table = sample_site[:, :, batch_index, :]
        sampled = jnp.take_along_axis(patch_model_vector, site_table[:, :, None, :], axis=3)
        prior_mean = lax.optimization_barrier(jnp.mean(sampled, axis=2))
        live_slot = (slot_index[None, None, :] < live_count[:, :, batch_index][:, :, None]).astype(jnp.float32)
        error_scale = 1.0 / jnp.sqrt(error_variance[:, :, batch_index, :])
        scaled_rows = (live_slot * error_scale)[:, :, None, :] * (sampled - prior_mean[:, :, None, :])
        innovation = live_slot * (observed[:, :, batch_index, :] - prior_mean) * error_scale
        gram_matrix = jnp.einsum('xymq,xynq->xymn', scaled_rows, scaled_rows, precision=lax.Precision.HIGHEST, preferred_element_type=jnp.float32)
        projection = jnp.einsum('xymq,xyq->xym', scaled_rows, innovation, precision=lax.Precision.HIGHEST, preferred_element_type=jnp.float32)
        gram_padded = jnp.pad(gram_matrix, ((RAD, RAD), (RAD, RAD), (0, 0), (0, 0)))
        proj_padded = jnp.pad(projection, ((RAD, RAD), (RAD, RAD), (0, 0)))
        gram_total = jnp.zeros_like(gram_matrix)
        proj_total = jnp.zeros_like(projection)
        for offset_x in range(width_mask):
            for offset_y in range(width_mask):
                factor_reach = reach[:, :, offset_x, offset_y]
                gram_total = gram_total + factor_reach[:, :, None, None] * gram_padded[offset_x:offset_x + PATCHES_ZONAL, offset_y:offset_y + PATCHES_MERIDION]
                proj_total = proj_total + factor_reach[:, :, None] * proj_padded[offset_x:offset_x + PATCHES_ZONAL, offset_y:offset_y + PATCHES_MERIDION]
        mixing = jax.vmap(jax.vmap(mixing_matrix))(gram_total, proj_total)
        mean_row = lax.optimization_barrier(jnp.mean(patch_model_vector, axis=2))
        deviation = patch_model_vector - mean_row[:, :, None, :]
        patch_model_vector = mean_row[:, :, None, :] + jnp.einsum('xykm,xykc->xymc', mixing, deviation, precision=lax.Precision.HIGHEST, preferred_element_type=jnp.float32)
    result = patch_model_vector.reshape(PATCHES_ZONAL, PATCHES_MERIDION, realisation_vectors, VERTICAL_LAYERS, PROGNOSTIC_VARS, PATCH_WIDTH_ZON, PATCH_WIDTH_MER).transpose(2, 3, 4, 0, 5, 1, 6)
    return result.reshape(realisation_vectors, VERTICAL_LAYERS, PROGNOSTIC_VARS, NX, NY)
```

```python
import functools

import jax
import jax.numpy as jnp
from jax import lax
from jax.experimental import pallas as pl
from jax.experimental.pallas import tpu as pltpu
from jax.sharding import PartitionSpec as P

BATCHES = 4
RAD = 2
NS_STEPS = 6
WIDTH = 2 * RAD + 1
OFFSETS = [(dx, dy) for dx in range(-RAD, RAD + 1) for dy in range(-RAD, RAD + 1)]


def extended(cells, sides, width):
    for axis, dim in sides:
        count = lax.axis_size(axis)
        ends = count - 1
        head = lax.slice_in_dim(cells, 0, width, axis=dim)
        tail = lax.slice_in_dim(cells, cells.shape[dim] - width, cells.shape[dim], axis=dim)
        cells = jnp.concatenate(
            [
                lax.ppermute(tail, axis, [(i, (i + 1) % count) for i in range(ends)]),
                cells,
                lax.ppermute(head, axis, [((i + 1) % count, i) for i in range(ends)]),
            ],
            axis=dim,
        )
    return cells


def matmul_full(left, right):
    return jnp.dot(left, right, precision=lax.Precision.HIGHEST, preferred_element_type=jnp.float32)


def integrate_model_timestep(halo_padded, courant_eastward, courant_northward, diffusivity):
    centre = halo_padded[..., 1:-1, 1:-1]
    east_cell = halo_padded[..., 2:, 1:-1]
    west_cell = halo_padded[..., :-2, 1:-1]
    north_cell = halo_padded[..., 1:-1, 2:]
    south_cell = halo_padded[..., 1:-1, :-2]
    flux_x = jnp.maximum(courant_eastward, 0.0) * (centre - west_cell) + jnp.minimum(
        courant_eastward, 0.0
    ) * (east_cell - centre)
    flux_y = jnp.maximum(courant_northward, 0.0) * (centre - south_cell) + jnp.minimum(
        courant_northward, 0.0
    ) * (north_cell - centre)
    spread_term = diffusivity * (east_cell + west_cell + north_cell + south_cell - 4.0 * centre)
    return centre + spread_term - flux_x - flux_y


def mixing_matrix(gram_matrix, projection):
    realisation_vectors = gram_matrix.shape[0]
    identity = jnp.eye(realisation_vectors, dtype=jnp.float32)
    precision_matrix = identity + gram_matrix / (realisation_vectors - 1)
    frobenius = jnp.sqrt(jnp.sum(precision_matrix * precision_matrix))
    iterate = precision_matrix / frobenius
    inverse = identity
    for repeat in range(NS_STEPS):
        factor = 1.5 * identity - 0.5 * matmul_full(inverse, iterate)
        iterate = matmul_full(iterate, factor)
        inverse = matmul_full(factor, inverse)
    transform = inverse / jnp.sqrt(frobenius)
    weights = matmul_full(transform, matmul_full(transform, projection)) / (realisation_vectors - 1)
    return transform + weights[:, None]


def exchange_kernel(nx, ny, payload_ref, out_ref, slots, send_sem, recv_sem):
    me_x = lax.axis_index("gx")
    me_y = lax.axis_index("gy")

    def inside(x, y):
        return (x >= 0) & (x < nx) & (y >= 0) & (y < ny)

    barrier = pltpu.get_barrier_semaphore()
    partners = jnp.int32(0)
    for dx, dy in OFFSETS:
        if dx == 0 and dy == 0:
            continue
        ok = inside(me_x - dx, me_y - dy)
        partners = partners + ok.astype(jnp.int32)

        @pl.when(ok)
        def _():
            pl.semaphore_signal(
                barrier, inc=1, device_id=(me_x - dx, me_y - dy),
                device_id_type=pl.DeviceIdType.MESH,
            )

    pl.semaphore_wait(barrier, partners)

    copies = []
    for k, (dx, dy) in enumerate(OFFSETS):
        if dx == 0 and dy == 0:
            continue
        copy = pltpu.make_async_remote_copy(
            src_ref=payload_ref,
            dst_ref=slots.at[k],
            send_sem=send_sem.at[k],
            recv_sem=recv_sem.at[k],
            device_id=(me_x - dx, me_y - dy),
            device_id_type=pl.DeviceIdType.MESH,
        )
        ok = inside(me_x - dx, me_y - dy)

        @pl.when(ok)
        def _():
            copy.start()

        copies.append((k, dx, dy, copy, ok))

    out_ref[RAD * WIDTH + RAD] = payload_ref[...]
    for k, dx, dy, copy, ok in copies:
        @pl.when(ok)
        def _():
            copy.wait_send()

        arrives = inside(me_x + dx, me_y + dy)

        @pl.when(arrives)
        def _():
            copy.wait_recv()
            out_ref[k] = slots[k]

        @pl.when(jnp.logical_not(arrives))
        def _():
            out_ref[k] = jnp.zeros(out_ref.shape[1:], out_ref.dtype)


def gather_neighbourhood(payload, nx, ny):
    count = len(OFFSETS)
    return pl.pallas_call(
        functools.partial(exchange_kernel, nx, ny),
        out_shape=jax.ShapeDtypeStruct((count,) + payload.shape, payload.dtype),
        in_specs=[pl.BlockSpec(memory_space=pltpu.VMEM)],
        out_specs=pl.BlockSpec(memory_space=pltpu.VMEM),
        scratch_shapes=[
            pltpu.VMEM((count,) + payload.shape, payload.dtype),
            pltpu.SemaphoreType.DMA((count,)),
            pltpu.SemaphoreType.DMA((count,)),
        ],
        compiler_params=pltpu.CompilerParams(collective_id=0, has_side_effects=True),
    )(payload)


def on_device(
    background_sample,
    courant_eastward,
    courant_northward,
    diffusivity,
    sample_site,
    live_count,
    observed,
    error_variance,
    reach_mask,
):
    nx = lax.axis_size("gx")
    ny = lax.axis_size("gy")
    halo_padded = extended(background_sample, (("gx", 3), ("gy", 4)), 1)
    forecast = integrate_model_timestep(
        halo_padded, courant_eastward[:, None], courant_northward[:, None], diffusivity
    )
    members = forecast.shape[0]
    state = forecast.reshape(members, -1)
    site_table = sample_site[0, 0]
    counts = live_count[0, 0]
    observed_here = observed[0, 0]
    variance_here = error_variance[0, 0]
    batches, slot_count = site_table.shape
    slot_index = jnp.arange(slot_count)
    mask_index = jnp.arange(WIDTH)
    centre_one = ((mask_index[:, None] == RAD) & (mask_index[None, :] == RAD)).astype(jnp.float32)
    reach_weight = jnp.maximum(reach_mask[0, 0].astype(jnp.float32), centre_one).reshape(-1)
    all_sampled = jnp.take(state, site_table.reshape(-1), axis=1).reshape(members, batches, slot_count)
    identity = jnp.eye(members, dtype=jnp.float32)
    carried = identity
    half = members * members // 128
    for batch_index in range(batches):
        if batch_index == 0:
            sampled = all_sampled[:, 0]
        else:
            sampled = matmul_full(carried, all_sampled[:, batch_index])
        prior_mean = jnp.mean(sampled, axis=0)
        live_slot = (slot_index < counts[batch_index]).astype(jnp.float32)
        error_scale = 1.0 / jnp.sqrt(variance_here[batch_index])
        scaled_rows = (live_slot * error_scale)[None, :] * (sampled - prior_mean[None, :])
        innovation = live_slot * (observed_here[batch_index] - prior_mean) * error_scale
        gram_here = matmul_full(scaled_rows, scaled_rows.T)
        proj_here = matmul_full(scaled_rows, innovation[:, None])[:, 0]
        payload = jnp.concatenate(
            [
                gram_here.reshape(half, 128),
                jnp.pad(proj_here, (0, 128 - members))[None, :],
                jnp.zeros((7, 128), jnp.float32),
            ],
            axis=0,
        )
        stack = gather_neighbourhood(payload, nx, ny)
        gram_total = jnp.sum(reach_weight[:, None, None] * stack[:, :half], axis=0).reshape(members, members)
        proj_total = jnp.sum(reach_weight[:, None] * stack[:, half, :members], axis=0)
        mixing = mixing_matrix(gram_total, proj_total)
        step = 1.0 / members + mixing.T - jnp.mean(mixing, axis=0)[:, None]
        carried = step if batch_index == 0 else matmul_full(step, carried)
    analysis = matmul_full(carried, state)
    return analysis.reshape(forecast.shape)


def solution(mesh):
    in_specs = (
        P(None, None, None, "gx", "gy"),
        P(None, "gx", "gy"),
        P(None, "gx", "gy"),
        P("gx", "gy"),
        P("gx", "gy", None, None),
        P("gx", "gy", None),
        P("gx", "gy", None, None),
        P("gx", "gy", None, None),
        P("gx", "gy", None, None),
    )
    out_specs = P(None, None, None, "gx", "gy")
    return jax.shard_map(
        on_device, mesh=mesh, in_specs=in_specs, out_specs=out_specs, check_vma=False
    )
```

```python
import functools

import jax
import jax.numpy as jnp
from jax import lax
from jax.experimental import pallas as pl
from jax.experimental.pallas import tpu as pltpu
from jax.sharding import PartitionSpec as P

BATCHES = 4
RAD = 2
NS_STEPS = 6
WIDTH = 2 * RAD + 1
OFFSETS = [(dx, dy) for dx in range(-RAD, RAD + 1) for dy in range(-RAD, RAD + 1)]


def matmul_full(left, right):
    return jnp.dot(left, right, precision=lax.Precision.HIGHEST, preferred_element_type=jnp.float32)


def mixing_matrix(gram_matrix, projection):
    realisation_vectors = gram_matrix.shape[0]
    identity = jnp.eye(realisation_vectors, dtype=jnp.float32)
    precision_matrix = identity + gram_matrix / (realisation_vectors - 1)
    frobenius = jnp.sqrt(jnp.sum(precision_matrix * precision_matrix))
    iterate = precision_matrix / frobenius
    inverse = identity
    for repeat in range(NS_STEPS):
        factor = 1.5 * identity - 0.5 * matmul_full(inverse, iterate)
        iterate = matmul_full(iterate, factor)
        inverse = matmul_full(factor, inverse)
    transform = inverse / jnp.sqrt(frobenius)
    weights = matmul_full(transform, matmul_full(transform, projection)) / (realisation_vectors - 1)
    return transform + weights[:, None]


def stencil_kernel(x_ref, east_ref, west_ref, edge_ref, u_ref, v_ref, d_ref, o_ref, east_scr, west_scr):
    rows = x_ref.shape[3]
    lanes = x_ref.shape[4]
    east_scr[:, :, :, 0 : rows - 1, :] = x_ref[:, :, :, 1:rows, :]
    east_scr[:, :, :, rows - 1 : rows, :] = east_ref[...]
    west_scr[:, :, :, 1:rows, :] = x_ref[:, :, :, 0 : rows - 1, :]
    west_scr[:, :, :, 0:1, :] = west_ref[...]
    centre = x_ref[...]
    east_cell = east_scr[...]
    west_cell = west_scr[...]
    edge = edge_ref[...]
    lane = lax.broadcasted_iota(jnp.int32, centre.shape, 4)
    north_cell = jnp.where(lane == lanes - 1, edge, pltpu.roll(centre, lanes - 1, 4))
    south_cell = jnp.where(lane == 0, edge, pltpu.roll(centre, 1, 4))
    u = u_ref[...][None, :, None]
    v = v_ref[...][None, :, None]
    d = d_ref[...][None, None, None]
    flux_x = jnp.maximum(u, 0.0) * (centre - west_cell) + jnp.minimum(u, 0.0) * (east_cell - centre)
    flux_y = jnp.maximum(v, 0.0) * (centre - south_cell) + jnp.minimum(v, 0.0) * (north_cell - centre)
    spread_term = d * (east_cell + west_cell + north_cell + south_cell - 4.0 * centre)
    o_ref[...] = centre + spread_term - flux_x - flux_y


def forecast_step(cells, courant_eastward, courant_northward, diffusivity):
    nx = lax.axis_size("gx")
    ny = lax.axis_size("gy")
    rows, lanes = cells.shape[3], cells.shape[4]
    east_halo = lax.ppermute(cells[:, :, :, 0:1, :], "gx", [(i + 1, i) for i in range(nx - 1)])
    west_halo = lax.ppermute(cells[:, :, :, rows - 1 : rows, :], "gx", [(i, i + 1) for i in range(nx - 1)])
    north_halo = lax.ppermute(cells[..., 0], "gy", [(i + 1, i) for i in range(ny - 1)])
    south_halo = lax.ppermute(cells[..., lanes - 1], "gy", [(i, i + 1) for i in range(ny - 1)])
    lane = lax.broadcasted_iota(jnp.int32, cells.shape, 4)
    edge = jnp.where(
        lane == lanes - 1,
        north_halo[..., None],
        jnp.where(lane == 0, south_halo[..., None], 0.0),
    )
    block = 8
    members = cells.shape[0]
    big = pl.BlockSpec((block,) + cells.shape[1:], lambda i: (i, 0, 0, 0, 0))
    thin = pl.BlockSpec((block,) + cells.shape[1:3] + (1, lanes), lambda i: (i, 0, 0, 0, 0))
    whole3 = pl.BlockSpec(courant_eastward.shape, lambda i: (0, 0, 0))
    whole2 = pl.BlockSpec(diffusivity.shape, lambda i: (0, 0))
    return pl.pallas_call(
        stencil_kernel,
        out_shape=jax.ShapeDtypeStruct(cells.shape, cells.dtype),
        grid=(members // block,),
        in_specs=[big, thin, thin, big, whole3, whole3, whole2],
        out_specs=big,
        scratch_shapes=[
            pltpu.VMEM((block,) + cells.shape[1:], cells.dtype),
            pltpu.VMEM((block,) + cells.shape[1:], cells.dtype),
        ],
    )(cells, east_halo, west_halo, edge, courant_eastward, courant_northward, diffusivity)


def exchange_kernel(nx, ny, payload_ref, out_ref, slots, send_sem, recv_sem):
    me_x = lax.axis_index("gx")
    me_y = lax.axis_index("gy")

    def inside(x, y):
        return (x >= 0) & (x < nx) & (y >= 0) & (y < ny)

    barrier = pltpu.get_barrier_semaphore()
    partners = jnp.int32(0)
    for dx, dy in OFFSETS:
        if dx == 0 and dy == 0:
            continue
        ok = inside(me_x - dx, me_y - dy)
        partners = partners + ok.astype(jnp.int32)

        @pl.when(ok)
        def _():
            pl.semaphore_signal(
                barrier, inc=1, device_id=(me_x - dx, me_y - dy),
                device_id_type=pl.DeviceIdType.MESH,
            )

    pl.semaphore_wait(barrier, partners)

    copies = []
    for k, (dx, dy) in enumerate(OFFSETS):
        if dx == 0 and dy == 0:
            continue
        copy = pltpu.make_async_remote_copy(
            src_ref=payload_ref,
            dst_ref=slots.at[k],
            send_sem=send_sem.at[k],
            recv_sem=recv_sem.at[k],
            device_id=(me_x - dx, me_y - dy),
            device_id_type=pl.DeviceIdType.MESH,
        )
        ok = inside(me_x - dx, me_y - dy)

        @pl.when(ok)
        def _():
            copy.start()

        copies.append((k, dx, dy, copy, ok))

    out_ref[RAD * WIDTH + RAD] = payload_ref[...]
    for k, dx, dy, copy, ok in copies:
        @pl.when(ok)
        def _():
            copy.wait_send()

        arrives = inside(me_x + dx, me_y + dy)

        @pl.when(arrives)
        def _():
            copy.wait_recv()
            out_ref[k] = slots[k]

        @pl.when(jnp.logical_not(arrives))
        def _():
            out_ref[k] = jnp.zeros(out_ref.shape[1:], out_ref.dtype)


def gather_neighbourhood(payload, nx, ny):
    count = len(OFFSETS)
    return pl.pallas_call(
        functools.partial(exchange_kernel, nx, ny),
        out_shape=jax.ShapeDtypeStruct((count,) + payload.shape, payload.dtype),
        in_specs=[pl.BlockSpec(memory_space=pltpu.VMEM)],
        out_specs=pl.BlockSpec(memory_space=pltpu.VMEM),
        scratch_shapes=[
            pltpu.VMEM((count,) + payload.shape, payload.dtype),
            pltpu.SemaphoreType.DMA((count,)),
            pltpu.SemaphoreType.DMA((count,)),
        ],
        compiler_params=pltpu.CompilerParams(collective_id=0, has_side_effects=True),
    )(payload)


def on_device(
    background_sample,
    courant_eastward,
    courant_northward,
    diffusivity,
    sample_site,
    live_count,
    observed,
    error_variance,
    reach_mask,
):
    nx = lax.axis_size("gx")
    ny = lax.axis_size("gy")
    forecast = forecast_step(background_sample, courant_eastward, courant_northward, diffusivity)
    members = forecast.shape[0]
    state = forecast.reshape(members, -1)
    site_table = sample_site[0, 0]
    counts = live_count[0, 0]
    observed_here = observed[0, 0]
    variance_here = error_variance[0, 0]
    batches, slot_count = site_table.shape
    slot_index = jnp.arange(slot_count)
    mask_index = jnp.arange(WIDTH)
    centre_one = ((mask_index[:, None] == RAD) & (mask_index[None, :] == RAD)).astype(jnp.float32)
    reach_weight = jnp.maximum(reach_mask[0, 0].astype(jnp.float32), centre_one).reshape(-1)
    all_sampled = jnp.take(state, site_table.reshape(-1), axis=1).reshape(members, batches, slot_count)
    identity = jnp.eye(members, dtype=jnp.float32)
    carried = identity
    half = members * members // 128
    for batch_index in range(batches):
        if batch_index == 0:
            sampled = all_sampled[:, 0]
        else:
            sampled = matmul_full(carried, all_sampled[:, batch_index])
        prior_mean = jnp.mean(sampled, axis=0)
        live_slot = (slot_index < counts[batch_index]).astype(jnp.float32)
        error_scale = 1.0 / jnp.sqrt(variance_here[batch_index])
        scaled_rows = (live_slot * error_scale)[None, :] * (sampled - prior_mean[None, :])
        innovation = live_slot * (observed_here[batch_index] - prior_mean) * error_scale
        gram_here = matmul_full(scaled_rows, scaled_rows.T)
        proj_here = matmul_full(scaled_rows, innovation[:, None])[:, 0]
        payload = jnp.concatenate(
            [
                gram_here.reshape(half, 128),
                jnp.pad(proj_here, (0, 128 - members))[None, :],
                jnp.zeros((7, 128), jnp.float32),
            ],
            axis=0,
        )
        stack = gather_neighbourhood(payload, nx, ny)
        gram_total = jnp.sum(reach_weight[:, None, None] * stack[:, :half], axis=0).reshape(members, members)
        proj_total = jnp.sum(reach_weight[:, None] * stack[:, half, :members], axis=0)
        mixing = mixing_matrix(gram_total, proj_total)
        step = 1.0 / members + mixing.T - jnp.mean(mixing, axis=0)[:, None]
        carried = step if batch_index == 0 else matmul_full(step, carried)
    analysis = matmul_full(carried, state)
    return analysis.reshape(forecast.shape)


def solution(mesh):
    in_specs = (
        P(None, None, None, "gx", "gy"),
        P(None, "gx", "gy"),
        P(None, "gx", "gy"),
        P("gx", "gy"),
        P("gx", "gy", None, None),
        P("gx", "gy", None),
        P("gx", "gy", None, None),
        P("gx", "gy", None, None),
        P("gx", "gy", None, None),
    )
    out_specs = P(None, None, None, "gx", "gy")
    return jax.shard_map(
        on_device, mesh=mesh, in_specs=in_specs, out_specs=out_specs, check_vma=False
    )
```

```python
import functools

import jax
import jax.numpy as jnp
from jax import lax
from jax.experimental import pallas as pl
from jax.experimental.pallas import tpu as pltpu
from jax.sharding import PartitionSpec as P

BATCHES = 4
RAD = 2
NS_STEPS = 6
WIDTH = 2 * RAD + 1
OFFSETS = [(dx, dy) for dx in range(-RAD, RAD + 1) for dy in range(-RAD, RAD + 1)]


def matmul_full(left, right):
    return jnp.dot(left, right, precision=lax.Precision.HIGHEST, preferred_element_type=jnp.float32)


def mixing_matrix(gram_matrix, projection):
    realisation_vectors = gram_matrix.shape[0]
    identity = jnp.eye(realisation_vectors, dtype=jnp.float32)
    precision_matrix = identity + gram_matrix / (realisation_vectors - 1)
    frobenius = jnp.sqrt(jnp.sum(precision_matrix * precision_matrix))
    iterate = precision_matrix / frobenius
    inverse = identity
    for repeat in range(NS_STEPS):
        factor = 1.5 * identity - 0.5 * matmul_full(inverse, iterate)
        iterate = matmul_full(iterate, factor)
        inverse = matmul_full(factor, inverse)
    transform = inverse / jnp.sqrt(frobenius)
    weights = matmul_full(transform, matmul_full(transform, projection)) / (realisation_vectors - 1)
    return transform + weights[:, None]


def stencil_kernel(x_ref, east_ref, west_ref, edge_ref, u_ref, v_ref, d_ref, o_ref, east_scr, west_scr):
    rows = x_ref.shape[3]
    lanes = x_ref.shape[4]
    east_scr[:, :, :, 0 : rows - 1, :] = x_ref[:, :, :, 1:rows, :]
    east_scr[:, :, :, rows - 1 : rows, :] = east_ref[...]
    west_scr[:, :, :, 1:rows, :] = x_ref[:, :, :, 0 : rows - 1, :]
    west_scr[:, :, :, 0:1, :] = west_ref[...]
    centre = x_ref[...]
    east_cell = east_scr[...]
    west_cell = west_scr[...]
    edge = edge_ref[...]
    lane = lax.broadcasted_iota(jnp.int32, centre.shape, 4)
    north_cell = jnp.where(lane == lanes - 1, edge, pltpu.roll(centre, lanes - 1, 4))
    south_cell = jnp.where(lane == 0, edge, pltpu.roll(centre, 1, 4))
    u = u_ref[...][None, :, None]
    v = v_ref[...][None, :, None]
    d = d_ref[...][None, None, None]
    flux_x = jnp.maximum(u, 0.0) * (centre - west_cell) + jnp.minimum(u, 0.0) * (east_cell - centre)
    flux_y = jnp.maximum(v, 0.0) * (centre - south_cell) + jnp.minimum(v, 0.0) * (north_cell - centre)
    spread_term = d * (east_cell + west_cell + north_cell + south_cell - 4.0 * centre)
    o_ref[...] = centre + spread_term - flux_x - flux_y


def forecast_step(cells, courant_eastward, courant_northward, diffusivity):
    nx = lax.axis_size("gx")
    ny = lax.axis_size("gy")
    rows, lanes = cells.shape[3], cells.shape[4]
    east_halo = lax.ppermute(cells[:, :, :, 0:1, :], "gx", [(i + 1, i) for i in range(nx - 1)])
    west_halo = lax.ppermute(cells[:, :, :, rows - 1 : rows, :], "gx", [(i, i + 1) for i in range(nx - 1)])
    lane_index = jnp.arange(lanes)
    pick = jnp.stack([lane_index == 0, lane_index == lanes - 1]).astype(jnp.float32)
    place = jnp.stack([lane_index == lanes - 1, lane_index == 0]).astype(jnp.float32)
    sides = jnp.einsum(
        "abcil,sl->sabci",
        cells, pick, precision=lax.Precision.HIGHEST, preferred_element_type=jnp.float32,
    )
    north_halo = lax.ppermute(sides[0], "gy", [(i + 1, i) for i in range(ny - 1)])
    south_halo = lax.ppermute(sides[1], "gy", [(i, i + 1) for i in range(ny - 1)])
    edge = jnp.einsum(
        "sabci,sl->abcil", jnp.stack([north_halo, south_halo]), place,
        precision=lax.Precision.HIGHEST, preferred_element_type=jnp.float32,
    )
    block = 8
    members = cells.shape[0]
    big = pl.BlockSpec((block,) + cells.shape[1:], lambda i: (i, 0, 0, 0, 0))
    thin = pl.BlockSpec((block,) + cells.shape[1:3] + (1, lanes), lambda i: (i, 0, 0, 0, 0))
    whole3 = pl.BlockSpec(courant_eastward.shape, lambda i: (0, 0, 0))
    whole2 = pl.BlockSpec(diffusivity.shape, lambda i: (0, 0))
    return pl.pallas_call(
        stencil_kernel,
        out_shape=jax.ShapeDtypeStruct(cells.shape, cells.dtype),
        grid=(members // block,),
        in_specs=[big, thin, thin, big, whole3, whole3, whole2],
        out_specs=big,
        scratch_shapes=[
            pltpu.VMEM((block,) + cells.shape[1:], cells.dtype),
            pltpu.VMEM((block,) + cells.shape[1:], cells.dtype),
        ],
    )(cells, east_halo, west_halo, edge, courant_eastward, courant_northward, diffusivity)


def exchange_kernel(nx, ny, payload_ref, out_ref, slots, send_sem, recv_sem):
    me_x = lax.axis_index("gx")
    me_y = lax.axis_index("gy")

    def inside(x, y):
        return (x >= 0) & (x < nx) & (y >= 0) & (y < ny)

    barrier = pltpu.get_barrier_semaphore()
    partners = jnp.int32(0)
    for dx, dy in OFFSETS:
        if dx == 0 and dy == 0:
            continue
        ok = inside(me_x - dx, me_y - dy)
        partners = partners + ok.astype(jnp.int32)

        @pl.when(ok)
        def _():
            pl.semaphore_signal(
                barrier, inc=1, device_id=(me_x - dx, me_y - dy),
                device_id_type=pl.DeviceIdType.MESH,
            )

    pl.semaphore_wait(barrier, partners)

    copies = []
    for k, (dx, dy) in enumerate(OFFSETS):
        if dx == 0 and dy == 0:
            continue
        copy = pltpu.make_async_remote_copy(
            src_ref=payload_ref,
            dst_ref=slots.at[k],
            send_sem=send_sem.at[k],
            recv_sem=recv_sem.at[k],
            device_id=(me_x - dx, me_y - dy),
            device_id_type=pl.DeviceIdType.MESH,
        )
        ok = inside(me_x - dx, me_y - dy)

        @pl.when(ok)
        def _():
            copy.start()

        copies.append((k, dx, dy, copy, ok))

    out_ref[RAD * WIDTH + RAD] = payload_ref[...]
    for k, dx, dy, copy, ok in copies:
        @pl.when(ok)
        def _():
            copy.wait_send()

        arrives = inside(me_x + dx, me_y + dy)

        @pl.when(arrives)
        def _():
            copy.wait_recv()
            out_ref[k] = slots[k]

        @pl.when(jnp.logical_not(arrives))
        def _():
            out_ref[k] = jnp.zeros(out_ref.shape[1:], out_ref.dtype)


def gather_neighbourhood(payload, nx, ny):
    count = len(OFFSETS)
    return pl.pallas_call(
        functools.partial(exchange_kernel, nx, ny),
        out_shape=jax.ShapeDtypeStruct((count,) + payload.shape, payload.dtype),
        in_specs=[pl.BlockSpec(memory_space=pltpu.VMEM)],
        out_specs=pl.BlockSpec(memory_space=pltpu.VMEM),
        scratch_shapes=[
            pltpu.VMEM((count,) + payload.shape, payload.dtype),
            pltpu.SemaphoreType.DMA((count,)),
            pltpu.SemaphoreType.DMA((count,)),
        ],
        compiler_params=pltpu.CompilerParams(collective_id=0, has_side_effects=True),
    )(payload)


def on_device(
    background_sample,
    courant_eastward,
    courant_northward,
    diffusivity,
    sample_site,
    live_count,
    observed,
    error_variance,
    reach_mask,
):
    nx = lax.axis_size("gx")
    ny = lax.axis_size("gy")
    forecast = forecast_step(background_sample, courant_eastward, courant_northward, diffusivity)
    members = forecast.shape[0]
    state = forecast.reshape(members, -1)
    site_table = sample_site[0, 0]
    counts = live_count[0, 0]
    observed_here = observed[0, 0]
    variance_here = error_variance[0, 0]
    batches, slot_count = site_table.shape
    slot_index = jnp.arange(slot_count)
    mask_index = jnp.arange(WIDTH)
    centre_one = ((mask_index[:, None] == RAD) & (mask_index[None, :] == RAD)).astype(jnp.float32)
    reach_weight = jnp.maximum(reach_mask[0, 0].astype(jnp.float32), centre_one).reshape(-1)
    all_sampled = jnp.take(state, site_table.reshape(-1), axis=1).reshape(members, batches, slot_count)
    identity = jnp.eye(members, dtype=jnp.float32)
    carried = identity
    half = members * members // 128
    for batch_index in range(batches):
        if batch_index == 0:
            sampled = all_sampled[:, 0]
        else:
            sampled = matmul_full(carried, all_sampled[:, batch_index])
        prior_mean = jnp.mean(sampled, axis=0)
        live_slot = (slot_index < counts[batch_index]).astype(jnp.float32)
        error_scale = 1.0 / jnp.sqrt(variance_here[batch_index])
        scaled_rows = (live_slot * error_scale)[None, :] * (sampled - prior_mean[None, :])
        innovation = live_slot * (observed_here[batch_index] - prior_mean) * error_scale
        gram_here = matmul_full(scaled_rows, scaled_rows.T)
        proj_here = matmul_full(scaled_rows, innovation[:, None])[:, 0]
        payload = jnp.concatenate(
            [
                gram_here.reshape(half, 128),
                jnp.pad(proj_here, (0, 128 - members))[None, :],
                jnp.zeros((7, 128), jnp.float32),
            ],
            axis=0,
        )
        stack = gather_neighbourhood(payload, nx, ny)
        gram_total = jnp.sum(reach_weight[:, None, None] * stack[:, :half], axis=0).reshape(members, members)
        proj_total = jnp.sum(reach_weight[:, None] * stack[:, half, :members], axis=0)
        mixing = mixing_matrix(gram_total, proj_total)
        step = 1.0 / members + mixing.T - jnp.mean(mixing, axis=0)[:, None]
        carried = step if batch_index == 0 else matmul_full(step, carried)
    analysis = matmul_full(carried, state)
    return analysis.reshape(forecast.shape)


def solution(mesh):
    in_specs = (
        P(None, None, None, "gx", "gy"),
        P(None, "gx", "gy"),
        P(None, "gx", "gy"),
        P("gx", "gy"),
        P("gx", "gy", None, None),
        P("gx", "gy", None),
        P("gx", "gy", None, None),
        P("gx", "gy", None, None),
        P("gx", "gy", None, None),
    )
    out_specs = P(None, None, None, "gx", "gy")
    return jax.shard_map(
        on_device, mesh=mesh, in_specs=in_specs, out_specs=out_specs, check_vma=False
    )
```

```python
import functools

import jax
import jax.numpy as jnp
from jax import lax
from jax.experimental import pallas as pl
from jax.experimental.pallas import tpu as pltpu
from jax.sharding import PartitionSpec as P

BATCHES = 4
RAD = 2
NS_STEPS = 6
WIDTH = 2 * RAD + 1
OFFSETS = [(dx, dy) for dx in range(-RAD, RAD + 1) for dy in range(-RAD, RAD + 1)]


def matmul_full(left, right):
    return jnp.dot(left, right, precision=lax.Precision.HIGHEST, preferred_element_type=jnp.float32)


def mixing_matrix(gram_matrix, projection):
    realisation_vectors = gram_matrix.shape[0]
    identity = jnp.eye(realisation_vectors, dtype=jnp.float32)
    precision_matrix = identity + gram_matrix / (realisation_vectors - 1)
    frobenius = jnp.sqrt(jnp.sum(precision_matrix * precision_matrix))
    iterate = precision_matrix / frobenius
    inverse = identity
    for repeat in range(NS_STEPS):
        factor = 1.5 * identity - 0.5 * matmul_full(inverse, iterate)
        iterate = matmul_full(iterate, factor)
        inverse = matmul_full(factor, inverse)
    transform = inverse / jnp.sqrt(frobenius)
    weights = matmul_full(transform, matmul_full(transform, projection)) / (realisation_vectors - 1)
    return transform + weights[:, None]


def stencil_kernel(x_ref, east_ref, west_ref, edge_ref, u_ref, v_ref, d_ref, o_ref, east_scr, west_scr):
    rows = x_ref.shape[3]
    lanes = x_ref.shape[4]
    east_scr[:, :, :, 0 : rows - 1, :] = x_ref[:, :, :, 1:rows, :]
    east_scr[:, :, :, rows - 1 : rows, :] = east_ref[...]
    west_scr[:, :, :, 1:rows, :] = x_ref[:, :, :, 0 : rows - 1, :]
    west_scr[:, :, :, 0:1, :] = west_ref[...]
    centre = x_ref[...]
    east_cell = east_scr[...]
    west_cell = west_scr[...]
    edge = edge_ref[...]
    lane = lax.broadcasted_iota(jnp.int32, centre.shape, 4)
    north_cell = jnp.where(lane == lanes - 1, edge, pltpu.roll(centre, lanes - 1, 4))
    south_cell = jnp.where(lane == 0, edge, pltpu.roll(centre, 1, 4))
    u = u_ref[...][None, :, None]
    v = v_ref[...][None, :, None]
    d = d_ref[...][None, None, None]
    flux_x = jnp.maximum(u, 0.0) * (centre - west_cell) + jnp.minimum(u, 0.0) * (east_cell - centre)
    flux_y = jnp.maximum(v, 0.0) * (centre - south_cell) + jnp.minimum(v, 0.0) * (north_cell - centre)
    spread_term = d * (east_cell + west_cell + north_cell + south_cell - 4.0 * centre)
    o_ref[...] = centre + spread_term - flux_x - flux_y


def forecast_step(cells, courant_eastward, courant_northward, diffusivity):
    nx = lax.axis_size("gx")
    ny = lax.axis_size("gy")
    rows, lanes = cells.shape[3], cells.shape[4]
    east_halo = lax.ppermute(cells[:, :, :, 0:1, :], "gx", [(i + 1, i) for i in range(nx - 1)])
    west_halo = lax.ppermute(cells[:, :, :, rows - 1 : rows, :], "gx", [(i, i + 1) for i in range(nx - 1)])
    lane_index = jnp.arange(lanes)
    pick = jnp.stack([lane_index == 0, lane_index == lanes - 1]).astype(jnp.float32)
    place = jnp.stack([lane_index == lanes - 1, lane_index == 0]).astype(jnp.float32)
    sides = jnp.einsum(
        "abcil,sl->sabci",
        cells, pick, precision=lax.Precision.HIGHEST, preferred_element_type=jnp.float32,
    )
    north_halo = lax.ppermute(sides[0], "gy", [(i + 1, i) for i in range(ny - 1)])
    south_halo = lax.ppermute(sides[1], "gy", [(i, i + 1) for i in range(ny - 1)])
    edge = jnp.einsum(
        "sabci,sl->abcil", jnp.stack([north_halo, south_halo]), place,
        precision=lax.Precision.HIGHEST, preferred_element_type=jnp.float32,
    )
    block = 8
    members = cells.shape[0]
    big = pl.BlockSpec((block,) + cells.shape[1:], lambda i: (i, 0, 0, 0, 0))
    thin = pl.BlockSpec((block,) + cells.shape[1:3] + (1, lanes), lambda i: (i, 0, 0, 0, 0))
    whole3 = pl.BlockSpec(courant_eastward.shape, lambda i: (0, 0, 0))
    whole2 = pl.BlockSpec(diffusivity.shape, lambda i: (0, 0))
    return pl.pallas_call(
        stencil_kernel,
        out_shape=jax.ShapeDtypeStruct(cells.shape, cells.dtype),
        grid=(members // block,),
        in_specs=[big, thin, thin, big, whole3, whole3, whole2],
        out_specs=big,
        scratch_shapes=[
            pltpu.VMEM((block,) + cells.shape[1:], cells.dtype),
            pltpu.VMEM((block,) + cells.shape[1:], cells.dtype),
        ],
    )(cells, east_halo, west_halo, edge, courant_eastward, courant_northward, diffusivity)


def mm(left, right):
    return jnp.dot(left, right, precision=lax.Precision.HIGHEST, preferred_element_type=jnp.float32)


def mm_nt(left, right):
    return lax.dot_general(
        left, right, (((1,), (1,)), ((), ())),
        precision=lax.Precision.HIGHEST, preferred_element_type=jnp.float32,
    )


def analysis_kernel(
    nx, ny, y_ref, scale_ref, obs_ref, w_ref, out_ref,
    slots, payload, rows_t, total, carried, send_sem, recv_sem,
):
    me_x = lax.axis_index("gx")
    me_y = lax.axis_index("gy")
    members = y_ref.shape[1]
    slot_count = y_ref.shape[2]
    wide = payload.shape[2]
    batches = y_ref.shape[0]
    centre_k = RAD * WIDTH + RAD

    def inside(x, y):
        return (x >= 0) & (x < nx) & (y >= 0) & (y < ny)

    barrier = pltpu.get_barrier_semaphore()
    partners = jnp.int32(0)
    for dx, dy in OFFSETS:
        if dx == 0 and dy == 0:
            continue
        ok = inside(me_x - dx, me_y - dy)
        partners = partners + ok.astype(jnp.int32)

        @pl.when(ok)
        def _():
            pl.semaphore_signal(
                barrier, inc=1, device_id=(me_x - dx, me_y - dy),
                device_id_type=pl.DeviceIdType.MESH,
            )

    pl.semaphore_wait(barrier, partners)

    row = lax.broadcasted_iota(jnp.int32, (members, members), 0)
    col = lax.broadcasted_iota(jnp.int32, (members, members), 1)
    identity = (row == col).astype(jnp.float32)
    carried[...] = identity
    rows_t[...] = jnp.zeros(rows_t.shape, jnp.float32)

    def batch_step(b, _):
        par = b % 2
        sampled = mm(carried[...], y_ref[b])
        prior_mean = jnp.mean(sampled, axis=0, keepdims=True)
        scale = scale_ref[b]
        scaled_rows = scale * (sampled - prior_mean)
        innovation = scale * (obs_ref[b] - prior_mean)
        rows_t[0:members, :] = scaled_rows
        rows_t[members : members + 1, :] = innovation
        payload[par] = mm_nt(scaled_rows, rows_t[...])

        copies = []
        for k, (dx, dy) in enumerate(OFFSETS):
            if dx == 0 and dy == 0:
                continue
            copy = pltpu.make_async_remote_copy(
                src_ref=payload.at[par],
                dst_ref=slots.at[par, k],
                send_sem=send_sem.at[par, k],
                recv_sem=recv_sem.at[par, k],
                device_id=(me_x - dx, me_y - dy),
                device_id_type=pl.DeviceIdType.MESH,
            )
            ok = inside(me_x - dx, me_y - dy)

            @pl.when(ok)
            def _():
                copy.start()

            copies.append((k, dx, dy, copy, ok))

        total[...] = jnp.zeros(total.shape, jnp.float32)
        for k, (dx, dy) in enumerate(OFFSETS):
            if dx == 0 and dy == 0:
                total[...] += w_ref[k] * payload[par]
        for k, dx, dy, copy, ok in copies:
            @pl.when(ok)
            def _():
                copy.wait_send()

            arrives = inside(me_x + dx, me_y + dy)

            @pl.when(arrives)
            def _():
                copy.wait_recv()
                total[...] += w_ref[k] * slots[par, k]

        summed = total[...]
        gram_total = summed[:, 0:members]
        proj_block = summed[:, members : 2 * members]
        precision_matrix = identity + gram_total / (members - 1)
        squares = precision_matrix * precision_matrix
        frobenius = jnp.sqrt(jnp.sum(jnp.sum(squares, axis=1, keepdims=True), axis=0, keepdims=True))
        iterate = precision_matrix / frobenius

        def ns_step(_, pair):
            iterate, inverse = pair
            factor = 1.5 * identity - 0.5 * mm(inverse, iterate)
            return mm(iterate, factor), mm(factor, inverse)

        pair = (iterate, identity)
        for _i in range(NS_STEPS):
            pair = ns_step(_i, pair)
        iterate, inverse = pair
        transform = inverse / jnp.sqrt(frobenius)
        weights = mm(transform, mm(transform, proj_block)) / (members - 1)
        mixing = transform + weights[:, 0:1]
        mixing_t = mm_nt(identity, mixing)
        step = 1.0 / members + mixing_t - jnp.mean(mixing_t, axis=1, keepdims=True)
        carried[...] = mm(step, carried[...])
        return 0

    lax.fori_loop(0, batches, batch_step, 0)
    out_ref[...] = carried[...]


def run_analysis(y, scale, obs, weights, nx, ny):
    batches, members, slot_count = y.shape
    count = len(OFFSETS)
    wide = 2 * members
    return pl.pallas_call(
        functools.partial(analysis_kernel, nx, ny),
        out_shape=jax.ShapeDtypeStruct((members, members), jnp.float32),
        in_specs=[
            pl.BlockSpec(memory_space=pltpu.VMEM),
            pl.BlockSpec(memory_space=pltpu.VMEM),
            pl.BlockSpec(memory_space=pltpu.VMEM),
            pl.BlockSpec(memory_space=pltpu.SMEM),
        ],
        out_specs=pl.BlockSpec(memory_space=pltpu.VMEM),
        scratch_shapes=[
            pltpu.VMEM((2, count, members, wide), jnp.float32),
            pltpu.VMEM((2, members, wide), jnp.float32),
            pltpu.VMEM((wide, slot_count), jnp.float32),
            pltpu.VMEM((members, wide), jnp.float32),
            pltpu.VMEM((members, members), jnp.float32),
            pltpu.SemaphoreType.DMA((2, count)),
            pltpu.SemaphoreType.DMA((2, count)),
        ],
        compiler_params=pltpu.CompilerParams(collective_id=0, has_side_effects=True),
    )(y, scale, obs, weights)


def on_device(
    background_sample,
    courant_eastward,
    courant_northward,
    diffusivity,
    sample_site,
    live_count,
    observed,
    error_variance,
    reach_mask,
):
    nx = lax.axis_size("gx")
    ny = lax.axis_size("gy")
    forecast = forecast_step(background_sample, courant_eastward, courant_northward, diffusivity)
    members = forecast.shape[0]
    state = forecast.reshape(members, -1)
    site_table = sample_site[0, 0]
    counts = live_count[0, 0]
    observed_here = observed[0, 0]
    variance_here = error_variance[0, 0]
    batches, slot_count = site_table.shape
    slot_index = jnp.arange(slot_count)
    mask_index = jnp.arange(WIDTH)
    centre_one = ((mask_index[:, None] == RAD) & (mask_index[None, :] == RAD)).astype(jnp.float32)
    reach_weight = jnp.maximum(reach_mask[0, 0].astype(jnp.float32), centre_one).reshape(-1)
    all_sampled = jnp.take(state, site_table.reshape(-1), axis=1).reshape(members, batches, slot_count)
    y = jnp.transpose(all_sampled, (1, 0, 2))
    live_slot = (slot_index[None, :] < counts[:, None]).astype(jnp.float32)
    scale = (live_slot * (1.0 / jnp.sqrt(variance_here)))[:, None, :]
    carried = run_analysis(y, scale, observed_here[:, None, :], reach_weight, nx, ny)
    analysis = matmul_full(carried, state)
    return analysis.reshape(forecast.shape)


def solution(mesh):
    in_specs = (
        P(None, None, None, "gx", "gy"),
        P(None, "gx", "gy"),
        P(None, "gx", "gy"),
        P("gx", "gy"),
        P("gx", "gy", None, None),
        P("gx", "gy", None),
        P("gx", "gy", None, None),
        P("gx", "gy", None, None),
        P("gx", "gy", None, None),
    )
    out_specs = P(None, None, None, "gx", "gy")
    return jax.shard_map(
        on_device, mesh=mesh, in_specs=in_specs, out_specs=out_specs, check_vma=False
    )
```

```python
import functools

import jax
import jax.numpy as jnp
from jax import lax
from jax.experimental import pallas as pl
from jax.experimental.pallas import tpu as pltpu
from jax.sharding import PartitionSpec as P

BATCHES = 4
RAD = 2
NS_STEPS = 6
WIDTH = 2 * RAD + 1
OFFSETS = [(dx, dy) for dx in range(-RAD, RAD + 1) for dy in range(-RAD, RAD + 1)]


def matmul_full(left, right):
    return jnp.dot(left, right, precision=lax.Precision.HIGHEST, preferred_element_type=jnp.float32)


def mixing_matrix(gram_matrix, projection):
    realisation_vectors = gram_matrix.shape[0]
    identity = jnp.eye(realisation_vectors, dtype=jnp.float32)
    precision_matrix = identity + gram_matrix / (realisation_vectors - 1)
    frobenius = jnp.sqrt(jnp.sum(precision_matrix * precision_matrix))
    iterate = precision_matrix / frobenius
    inverse = identity
    for repeat in range(NS_STEPS):
        factor = 1.5 * identity - 0.5 * matmul_full(inverse, iterate)
        iterate = matmul_full(iterate, factor)
        inverse = matmul_full(factor, inverse)
    transform = inverse / jnp.sqrt(frobenius)
    weights = matmul_full(transform, matmul_full(transform, projection)) / (realisation_vectors - 1)
    return transform + weights[:, None]


def stencil_kernel(x_ref, east_ref, west_ref, edge_ref, u_ref, v_ref, d_ref, col_ref, row_ref, o_ref, s_ref, east_scr, west_scr):
    rows = x_ref.shape[3]
    lanes = x_ref.shape[4]
    east_scr[:, :, :, 0 : rows - 1, :] = x_ref[:, :, :, 1:rows, :]
    east_scr[:, :, :, rows - 1 : rows, :] = east_ref[...]
    west_scr[:, :, :, 1:rows, :] = x_ref[:, :, :, 0 : rows - 1, :]
    west_scr[:, :, :, 0:1, :] = west_ref[...]
    centre = x_ref[...]
    east_cell = east_scr[...]
    west_cell = west_scr[...]
    edge = edge_ref[...]
    lane = lax.broadcasted_iota(jnp.int32, centre.shape, 4)
    north_cell = jnp.where(lane == lanes - 1, edge, pltpu.roll(centre, lanes - 1, 4))
    south_cell = jnp.where(lane == 0, edge, pltpu.roll(centre, 1, 4))
    u = u_ref[...][None, :, None]
    v = v_ref[...][None, :, None]
    d = d_ref[...][None, None, None]
    flux_x = jnp.maximum(u, 0.0) * (centre - west_cell) + jnp.minimum(u, 0.0) * (east_cell - centre)
    flux_y = jnp.maximum(v, 0.0) * (centre - south_cell) + jnp.minimum(v, 0.0) * (north_cell - centre)
    spread_term = d * (east_cell + west_cell + north_cell + south_cell - 4.0 * centre)
    result = centre + spread_term - flux_x - flux_y
    o_ref[...] = result
    block, rows_all = result.shape[0], result.shape[1] * result.shape[2] * rows
    flat = result.reshape(block * rows_all, lanes)
    high = flat.astype(jnp.bfloat16)
    rest = flat - high.astype(jnp.float32)
    mid = rest.astype(jnp.bfloat16)
    low = (rest - mid.astype(jnp.float32)).astype(jnp.bfloat16)
    pick = col_ref[...]
    picked = jnp.dot(high, pick, preferred_element_type=jnp.float32)
    picked = picked + jnp.dot(mid, pick, preferred_element_type=jnp.float32)
    picked = picked + jnp.dot(low, pick, preferred_element_type=jnp.float32)
    picked = picked.reshape(block, rows_all, picked.shape[-1]) * row_ref[...][None]
    s_ref[...] = jnp.sum(picked, axis=1)


def forecast_step(cells, courant_eastward, courant_northward, diffusivity, sites):
    nx = lax.axis_size("gx")
    ny = lax.axis_size("gy")
    rows, lanes = cells.shape[3], cells.shape[4]
    east_halo = lax.ppermute(cells[:, :, :, 0:1, :], "gx", [(i + 1, i) for i in range(nx - 1)])
    west_halo = lax.ppermute(cells[:, :, :, rows - 1 : rows, :], "gx", [(i, i + 1) for i in range(nx - 1)])
    lane_index = jnp.arange(lanes)
    pick = jnp.stack([lane_index == 0, lane_index == lanes - 1]).astype(jnp.float32)
    place = jnp.stack([lane_index == lanes - 1, lane_index == 0]).astype(jnp.float32)
    sides = jnp.einsum(
        "abcil,sl->sabci",
        cells, pick, precision=lax.Precision.HIGHEST, preferred_element_type=jnp.float32,
    )
    north_halo = lax.ppermute(sides[0], "gy", [(i + 1, i) for i in range(ny - 1)])
    south_halo = lax.ppermute(sides[1], "gy", [(i, i + 1) for i in range(ny - 1)])
    edge = jnp.einsum(
        "sabci,sl->abcil", jnp.stack([north_halo, south_halo]), place,
        precision=lax.Precision.HIGHEST, preferred_element_type=jnp.float32,
    )
    block = 8
    members = cells.shape[0]
    big = pl.BlockSpec((block,) + cells.shape[1:], lambda i: (i, 0, 0, 0, 0))
    thin = pl.BlockSpec((block,) + cells.shape[1:3] + (1, lanes), lambda i: (i, 0, 0, 0, 0))
    whole3 = pl.BlockSpec(courant_eastward.shape, lambda i: (0, 0, 0))
    whole2 = pl.BlockSpec(diffusivity.shape, lambda i: (0, 0))
    site_count = sites.shape[0]
    rows_all = cells.shape[1] * cells.shape[2] * rows
    col_pick = (sites[None, :] % lanes == jnp.arange(lanes)[:, None]).astype(jnp.bfloat16)
    row_pick = (sites[None, :] // lanes == jnp.arange(rows_all)[:, None]).astype(jnp.float32)
    picks = pl.BlockSpec((lanes, site_count), lambda i: (0, 0))
    return pl.pallas_call(
        stencil_kernel,
        out_shape=(
            jax.ShapeDtypeStruct(cells.shape, cells.dtype),
            jax.ShapeDtypeStruct((members, site_count), cells.dtype),
        ),
        grid=(members // block,),
        in_specs=[big, thin, thin, big, whole3, whole3, whole2, picks,
                  pl.BlockSpec((rows_all, site_count), lambda i: (0, 0))],
        out_specs=(big, pl.BlockSpec((block, site_count), lambda i: (i, 0))),
        scratch_shapes=[
            pltpu.VMEM((block,) + cells.shape[1:], cells.dtype),
            pltpu.VMEM((block,) + cells.shape[1:], cells.dtype),
        ],
    )(cells, east_halo, west_halo, edge, courant_eastward, courant_northward, diffusivity, col_pick, row_pick)


def mm(left, right):
    return jnp.dot(left, right, precision=lax.Precision.HIGHEST, preferred_element_type=jnp.float32)


def mm_nt(left, right):
    return lax.dot_general(
        left, right, (((1,), (1,)), ((), ())),
        precision=lax.Precision.HIGHEST, preferred_element_type=jnp.float32,
    )


def analysis_kernel(
    nx, ny, y_ref, scale_ref, obs_ref, w_ref, out_ref,
    slots, payload, rows_t, total, carried, send_sem, recv_sem,
):
    me_x = lax.axis_index("gx")
    me_y = lax.axis_index("gy")
    members = y_ref.shape[1]
    slot_count = y_ref.shape[2]
    wide = payload.shape[2]
    batches = y_ref.shape[0]
    centre_k = RAD * WIDTH + RAD

    def inside(x, y):
        return (x >= 0) & (x < nx) & (y >= 0) & (y < ny)

    barrier = pltpu.get_barrier_semaphore()
    partners = jnp.int32(0)
    for dx, dy in OFFSETS:
        if dx == 0 and dy == 0:
            continue
        ok = inside(me_x - dx, me_y - dy)
        partners = partners + ok.astype(jnp.int32)

        @pl.when(ok)
        def _():
            pl.semaphore_signal(
                barrier, inc=1, device_id=(me_x - dx, me_y - dy),
                device_id_type=pl.DeviceIdType.MESH,
            )

    pl.semaphore_wait(barrier, partners)

    row = lax.broadcasted_iota(jnp.int32, (members, members), 0)
    col = lax.broadcasted_iota(jnp.int32, (members, members), 1)
    identity = (row == col).astype(jnp.float32)
    carried[...] = identity
    rows_t[...] = jnp.zeros(rows_t.shape, jnp.float32)

    def batch_step(b, _):
        par = b % 2
        sampled = mm(carried[...], y_ref[b])
        prior_mean = jnp.mean(sampled, axis=0, keepdims=True)
        scale = scale_ref[b]
        scaled_rows = scale * (sampled - prior_mean)
        innovation = scale * (obs_ref[b] - prior_mean)
        rows_t[0:members, :] = scaled_rows
        rows_t[members : members + 1, :] = innovation
        payload[par] = mm_nt(scaled_rows, rows_t[...])

        copies = []
        for k, (dx, dy) in enumerate(OFFSETS):
            if dx == 0 and dy == 0:
                continue
            copy = pltpu.make_async_remote_copy(
                src_ref=payload.at[par],
                dst_ref=slots.at[par, k],
                send_sem=send_sem.at[par, k],
                recv_sem=recv_sem.at[par, k],
                device_id=(me_x - dx, me_y - dy),
                device_id_type=pl.DeviceIdType.MESH,
            )
            ok = inside(me_x - dx, me_y - dy)

            @pl.when(ok)
            def _():
                copy.start()

            copies.append((k, dx, dy, copy, ok))

        total[...] = jnp.zeros(total.shape, jnp.float32)
        for k, (dx, dy) in enumerate(OFFSETS):
            if dx == 0 and dy == 0:
                total[...] += w_ref[k] * payload[par]
        for k, dx, dy, copy, ok in copies:
            @pl.when(ok)
            def _():
                copy.wait_send()

            arrives = inside(me_x + dx, me_y + dy)

            @pl.when(arrives)
            def _():
                copy.wait_recv()
                total[...] += w_ref[k] * slots[par, k]

        summed = total[...]
        gram_total = summed[:, 0:members]
        proj_block = summed[:, members : 2 * members]
        precision_matrix = identity + gram_total / (members - 1)
        squares = precision_matrix * precision_matrix
        frobenius = jnp.sqrt(jnp.sum(jnp.sum(squares, axis=1, keepdims=True), axis=0, keepdims=True))
        iterate = precision_matrix / frobenius

        def ns_step(_, pair):
            iterate, inverse = pair
            factor = 1.5 * identity - 0.5 * mm(inverse, iterate)
            return mm(iterate, factor), mm(factor, inverse)

        pair = (iterate, identity)
        for _i in range(NS_STEPS):
            pair = ns_step(_i, pair)
        iterate, inverse = pair
        transform = inverse / jnp.sqrt(frobenius)
        weights = mm(transform, mm(transform, proj_block)) / (members - 1)
        mixing = transform + weights[:, 0:1]
        mixing_t = mm_nt(identity, mixing)
        step = 1.0 / members + mixing_t - jnp.mean(mixing_t, axis=1, keepdims=True)
        carried[...] = mm(step, carried[...])
        return 0

    lax.fori_loop(0, batches, batch_step, 0)
    out_ref[...] = carried[...]


def run_analysis(y, scale, obs, weights, nx, ny):
    batches, members, slot_count = y.shape
    count = len(OFFSETS)
    wide = 2 * members
    return pl.pallas_call(
        functools.partial(analysis_kernel, nx, ny),
        out_shape=jax.ShapeDtypeStruct((members, members), jnp.float32),
        in_specs=[
            pl.BlockSpec(memory_space=pltpu.VMEM),
            pl.BlockSpec(memory_space=pltpu.VMEM),
            pl.BlockSpec(memory_space=pltpu.VMEM),
            pl.BlockSpec(memory_space=pltpu.SMEM),
        ],
        out_specs=pl.BlockSpec(memory_space=pltpu.VMEM),
        scratch_shapes=[
            pltpu.VMEM((2, count, members, wide), jnp.float32),
            pltpu.VMEM((2, members, wide), jnp.float32),
            pltpu.VMEM((wide, slot_count), jnp.float32),
            pltpu.VMEM((members, wide), jnp.float32),
            pltpu.VMEM((members, members), jnp.float32),
            pltpu.SemaphoreType.DMA((2, count)),
            pltpu.SemaphoreType.DMA((2, count)),
        ],
        compiler_params=pltpu.CompilerParams(collective_id=0, has_side_effects=True),
    )(y, scale, obs, weights)


def transform_kernel(k_ref, x_ref, o_ref):
    members, rows, lanes = x_ref.shape[0], x_ref.shape[3], x_ref.shape[4]
    sub = 8
    parts = [x_ref[:, 0, 0, h * sub : (h + 1) * sub, :].reshape(members * sub, lanes) for h in range(rows // sub)]
    mixed = jnp.dot(k_ref[...], jnp.concatenate(parts, axis=1),
                    precision=lax.Precision.HIGHEST, preferred_element_type=jnp.float32)
    for h in range(rows // sub):
        o_ref[:, 0, 0, h * sub : (h + 1) * sub, :] = mixed[:, h * lanes : (h + 1) * lanes].reshape(members, sub, lanes)


def apply_transform(carried, cells):
    members, levels, fields, rows, lanes = cells.shape
    sub = 8
    kron = (carried[:, None, :, None] * jnp.eye(sub, dtype=jnp.float32)[None, :, None, :]).reshape(members * sub, members * sub)
    block = pl.BlockSpec((members, 1, 1, rows, lanes), lambda a, b: (0, a, b, 0, 0))
    return pl.pallas_call(
        transform_kernel,
        out_shape=jax.ShapeDtypeStruct(cells.shape, cells.dtype),
        grid=(levels, fields),
        in_specs=[pl.BlockSpec((members * sub, members * sub), lambda a, b: (0, 0)), block],
        out_specs=block,
    )(kron, cells)


def on_device(
    background_sample,
    courant_eastward,
    courant_northward,
    diffusivity,
    sample_site,
    live_count,
    observed,
    error_variance,
    reach_mask,
):
    nx = lax.axis_size("gx")
    ny = lax.axis_size("gy")
    site_table = sample_site[0, 0]
    forecast, gathered = forecast_step(
        background_sample, courant_eastward, courant_northward, diffusivity, site_table.reshape(-1)
    )
    members = forecast.shape[0]
    counts = live_count[0, 0]
    observed_here = observed[0, 0]
    variance_here = error_variance[0, 0]
    batches, slot_count = site_table.shape
    slot_index = jnp.arange(slot_count)
    mask_index = jnp.arange(WIDTH)
    centre_one = ((mask_index[:, None] == RAD) & (mask_index[None, :] == RAD)).astype(jnp.float32)
    reach_weight = jnp.maximum(reach_mask[0, 0].astype(jnp.float32), centre_one).reshape(-1)
    all_sampled = gathered.reshape(members, batches, slot_count)
    y = jnp.transpose(all_sampled, (1, 0, 2))
    live_slot = (slot_index[None, :] < counts[:, None]).astype(jnp.float32)
    scale = (live_slot * (1.0 / jnp.sqrt(variance_here)))[:, None, :]
    carried = run_analysis(y, scale, observed_here[:, None, :], reach_weight, nx, ny)
    return apply_transform(carried, forecast)


def solution(mesh):
    in_specs = (
        P(None, None, None, "gx", "gy"),
        P(None, "gx", "gy"),
        P(None, "gx", "gy"),
        P("gx", "gy"),
        P("gx", "gy", None, None),
        P("gx", "gy", None),
        P("gx", "gy", None, None),
        P("gx", "gy", None, None),
        P("gx", "gy", None, None),
    )
    out_specs = P(None, None, None, "gx", "gy")
    return jax.shard_map(
        on_device, mesh=mesh, in_specs=in_specs, out_specs=out_specs, check_vma=False
    )
```

```python
import functools

import jax
import jax.numpy as jnp
from jax import lax
from jax.experimental import pallas as pl
from jax.experimental.pallas import tpu as pltpu
from jax.sharding import PartitionSpec as P

BATCHES = 4
RAD = 2
NS_STEPS = 6
WIDTH = 2 * RAD + 1
OFFSETS = [(dx, dy) for dx in range(-RAD, RAD + 1) for dy in range(-RAD, RAD + 1)]


def matmul_full(left, right):
    return jnp.dot(left, right, precision=lax.Precision.HIGHEST, preferred_element_type=jnp.float32)


def mixing_matrix(gram_matrix, projection):
    realisation_vectors = gram_matrix.shape[0]
    identity = jnp.eye(realisation_vectors, dtype=jnp.float32)
    precision_matrix = identity + gram_matrix / (realisation_vectors - 1)
    frobenius = jnp.sqrt(jnp.sum(precision_matrix * precision_matrix))
    iterate = precision_matrix / frobenius
    inverse = identity
    for repeat in range(NS_STEPS):
        factor = 1.5 * identity - 0.5 * matmul_full(inverse, iterate)
        iterate = matmul_full(iterate, factor)
        inverse = matmul_full(factor, inverse)
    transform = inverse / jnp.sqrt(frobenius)
    weights = matmul_full(transform, matmul_full(transform, projection)) / (realisation_vectors - 1)
    return transform + weights[:, None]


def stencil_kernel(x_ref, east_ref, west_ref, edge_ref, u_ref, v_ref, d_ref, col_ref, row_ref, o_ref, s_ref, east_scr, west_scr):
    rows = x_ref.shape[3]
    lanes = x_ref.shape[4]
    east_scr[:, :, :, 0 : rows - 1, :] = x_ref[:, :, :, 1:rows, :]
    east_scr[:, :, :, rows - 1 : rows, :] = east_ref[...]
    west_scr[:, :, :, 1:rows, :] = x_ref[:, :, :, 0 : rows - 1, :]
    west_scr[:, :, :, 0:1, :] = west_ref[...]
    centre = x_ref[...]
    east_cell = east_scr[...]
    west_cell = west_scr[...]
    edge = edge_ref[...]
    lane = lax.broadcasted_iota(jnp.int32, centre.shape, 4)
    north_cell = jnp.where(lane == lanes - 1, edge, pltpu.roll(centre, lanes - 1, 4))
    south_cell = jnp.where(lane == 0, edge, pltpu.roll(centre, 1, 4))
    u = u_ref[...][None, :, None]
    v = v_ref[...][None, :, None]
    d = d_ref[...][None, None, None]
    flux_x = jnp.maximum(u, 0.0) * (centre - west_cell) + jnp.minimum(u, 0.0) * (east_cell - centre)
    flux_y = jnp.maximum(v, 0.0) * (centre - south_cell) + jnp.minimum(v, 0.0) * (north_cell - centre)
    spread_term = d * (east_cell + west_cell + north_cell + south_cell - 4.0 * centre)
    result = centre + spread_term - flux_x - flux_y
    o_ref[...] = result
    block, rows_all = result.shape[0], result.shape[1] * result.shape[2] * rows
    flat = result.reshape(block * rows_all, lanes)
    high = flat.astype(jnp.bfloat16)
    rest = flat - high.astype(jnp.float32)
    mid = rest.astype(jnp.bfloat16)
    low = (rest - mid.astype(jnp.float32)).astype(jnp.bfloat16)
    pick = col_ref[...]
    picked = jnp.dot(high, pick, preferred_element_type=jnp.float32)
    picked = picked + jnp.dot(mid, pick, preferred_element_type=jnp.float32)
    picked = picked + jnp.dot(low, pick, preferred_element_type=jnp.float32)
    picked = picked.reshape(block, rows_all, picked.shape[-1]) * row_ref[...][None]
    s_ref[...] = jnp.sum(picked, axis=1)


def forecast_step(cells, courant_eastward, courant_northward, diffusivity, sites):
    nx = lax.axis_size("gx")
    ny = lax.axis_size("gy")
    rows, lanes = cells.shape[3], cells.shape[4]
    east_halo = lax.ppermute(cells[:, :, :, 0:1, :], "gx", [(i + 1, i) for i in range(nx - 1)])
    west_halo = lax.ppermute(cells[:, :, :, rows - 1 : rows, :], "gx", [(i, i + 1) for i in range(nx - 1)])
    lane_index = jnp.arange(lanes)
    pick = jnp.stack([lane_index == 0, lane_index == lanes - 1]).astype(jnp.float32)
    place = jnp.stack([lane_index == lanes - 1, lane_index == 0]).astype(jnp.float32)
    sides = jnp.einsum(
        "abcil,sl->sabci",
        cells, pick, precision=lax.Precision.HIGHEST, preferred_element_type=jnp.float32,
    )
    north_halo = lax.ppermute(sides[0], "gy", [(i + 1, i) for i in range(ny - 1)])
    south_halo = lax.ppermute(sides[1], "gy", [(i, i + 1) for i in range(ny - 1)])
    edge = jnp.einsum(
        "sabci,sl->abcil", jnp.stack([north_halo, south_halo]), place,
        precision=lax.Precision.HIGHEST, preferred_element_type=jnp.float32,
    )
    block = 8
    members = cells.shape[0]
    big = pl.BlockSpec((block,) + cells.shape[1:], lambda i: (i, 0, 0, 0, 0))
    thin = pl.BlockSpec((block,) + cells.shape[1:3] + (1, lanes), lambda i: (i, 0, 0, 0, 0))
    whole3 = pl.BlockSpec(courant_eastward.shape, lambda i: (0, 0, 0))
    whole2 = pl.BlockSpec(diffusivity.shape, lambda i: (0, 0))
    site_count = sites.shape[0]
    rows_all = cells.shape[1] * cells.shape[2] * rows
    col_pick = (sites[None, :] % lanes == jnp.arange(lanes)[:, None]).astype(jnp.bfloat16)
    row_pick = (sites[None, :] // lanes == jnp.arange(rows_all)[:, None]).astype(jnp.float32)
    picks = pl.BlockSpec((lanes, site_count), lambda i: (0, 0))
    return pl.pallas_call(
        stencil_kernel,
        out_shape=(
            jax.ShapeDtypeStruct(cells.shape, cells.dtype),
            jax.ShapeDtypeStruct((members, site_count), cells.dtype),
        ),
        grid=(members // block,),
        in_specs=[big, thin, thin, big, whole3, whole3, whole2, picks,
                  pl.BlockSpec((rows_all, site_count), lambda i: (0, 0))],
        out_specs=(big, pl.BlockSpec((block, site_count), lambda i: (i, 0))),
        scratch_shapes=[
            pltpu.VMEM((block,) + cells.shape[1:], cells.dtype),
            pltpu.VMEM((block,) + cells.shape[1:], cells.dtype),
        ],
    )(cells, east_halo, west_halo, edge, courant_eastward, courant_northward, diffusivity, col_pick, row_pick)


def mm(left, right):
    return jnp.dot(left, right, precision=lax.Precision.HIGHEST, preferred_element_type=jnp.float32)


def mm_nt(left, right):
    return lax.dot_general(
        left, right, (((1,), (1,)), ((), ())),
        precision=lax.Precision.HIGHEST, preferred_element_type=jnp.float32,
    )


def analysis_kernel(
    nx, ny, y_ref, scale_ref, obs_ref, w_ref, out_ref,
    slots, payload, rows_t, total, carried, send_sem, recv_sem,
):
    me_x = lax.axis_index("gx")
    me_y = lax.axis_index("gy")
    members = y_ref.shape[1]
    slot_count = y_ref.shape[2]
    wide = payload.shape[2]
    batches = y_ref.shape[0]
    centre_k = RAD * WIDTH + RAD

    def inside(x, y):
        return (x >= 0) & (x < nx) & (y >= 0) & (y < ny)

    barrier = pltpu.get_barrier_semaphore()
    partners = jnp.int32(0)
    for dx, dy in OFFSETS:
        if dx == 0 and dy == 0:
            continue
        ok = inside(me_x - dx, me_y - dy)
        partners = partners + ok.astype(jnp.int32)

        @pl.when(ok)
        def _():
            pl.semaphore_signal(
                barrier, inc=1, device_id=(me_x - dx, me_y - dy),
                device_id_type=pl.DeviceIdType.MESH,
            )

    pl.semaphore_wait(barrier, partners)

    row = lax.broadcasted_iota(jnp.int32, (members, members), 0)
    col = lax.broadcasted_iota(jnp.int32, (members, members), 1)
    identity = (row == col).astype(jnp.float32)
    carried[...] = identity
    rows_t[...] = jnp.zeros(rows_t.shape, jnp.float32)

    def batch_step(b, _):
        par = b % 2
        sampled = mm(carried[...], y_ref[b])
        prior_mean = jnp.mean(sampled, axis=0, keepdims=True)
        scale = scale_ref[b]
        scaled_rows = scale * (sampled - prior_mean)
        innovation = scale * (obs_ref[b] - prior_mean)
        rows_t[0:members, :] = scaled_rows
        rows_t[members : members + 1, :] = innovation
        payload[par] = mm_nt(scaled_rows, rows_t[...])

        copies = []
        for k, (dx, dy) in enumerate(OFFSETS):
            if dx == 0 and dy == 0:
                continue
            copy = pltpu.make_async_remote_copy(
                src_ref=payload.at[par],
                dst_ref=slots.at[par, k],
                send_sem=send_sem.at[par, k],
                recv_sem=recv_sem.at[par, k],
                device_id=(me_x - dx, me_y - dy),
                device_id_type=pl.DeviceIdType.MESH,
            )
            ok = inside(me_x - dx, me_y - dy)

            @pl.when(ok)
            def _():
                copy.start()

            copies.append((k, dx, dy, copy, ok))

        total[...] = jnp.zeros(total.shape, jnp.float32)
        for k, (dx, dy) in enumerate(OFFSETS):
            if dx == 0 and dy == 0:
                total[...] += w_ref[k] * payload[par]
        for k, dx, dy, copy, ok in copies:
            @pl.when(ok)
            def _():
                copy.wait_send()

            arrives = inside(me_x + dx, me_y + dy)

            @pl.when(arrives)
            def _():
                copy.wait_recv()
                total[...] += w_ref[k] * slots[par, k]

        summed = total[...]
        gram_total = summed[:, 0:members]
        proj_block = summed[:, members : 2 * members]
        precision_matrix = identity + gram_total / (members - 1)
        squares = precision_matrix * precision_matrix
        frobenius = jnp.sqrt(jnp.sum(jnp.sum(squares, axis=1, keepdims=True), axis=0, keepdims=True))
        iterate = precision_matrix / frobenius

        def ns_step(_, pair):
            iterate, inverse = pair
            factor = 1.5 * identity - 0.5 * mm(inverse, iterate)
            return mm(iterate, factor), mm(factor, inverse)

        pair = (iterate, identity)
        for _i in range(NS_STEPS):
            pair = ns_step(_i, pair)
        iterate, inverse = pair
        transform = inverse / jnp.sqrt(frobenius)
        weights = mm(transform, mm(transform, proj_block)) / (members - 1)
        mixing = transform + weights[:, 0:1]
        mixing_t = mm_nt(identity, mixing)
        step = 1.0 / members + mixing_t - jnp.mean(mixing_t, axis=1, keepdims=True)
        carried[...] = mm(step, carried[...])
        return 0

    lax.fori_loop(0, batches, batch_step, 0)
    out_ref[...] = carried[...]


def run_analysis(y, scale, obs, weights, nx, ny):
    batches, members, slot_count = y.shape
    count = len(OFFSETS)
    wide = 2 * members
    return pl.pallas_call(
        functools.partial(analysis_kernel, nx, ny),
        out_shape=jax.ShapeDtypeStruct((members, members), jnp.float32),
        in_specs=[
            pl.BlockSpec(memory_space=pltpu.VMEM),
            pl.BlockSpec(memory_space=pltpu.VMEM),
            pl.BlockSpec(memory_space=pltpu.VMEM),
            pl.BlockSpec(memory_space=pltpu.SMEM),
        ],
        out_specs=pl.BlockSpec(memory_space=pltpu.VMEM),
        scratch_shapes=[
            pltpu.VMEM((2, count, members, wide), jnp.float32),
            pltpu.VMEM((2, members, wide), jnp.float32),
            pltpu.VMEM((wide, slot_count), jnp.float32),
            pltpu.VMEM((members, wide), jnp.float32),
            pltpu.VMEM((members, members), jnp.float32),
            pltpu.SemaphoreType.DMA((2, count)),
            pltpu.SemaphoreType.DMA((2, count)),
        ],
        compiler_params=pltpu.CompilerParams(collective_id=0, has_side_effects=True),
    )(y, scale, obs, weights)


def transform_kernel(p_ref, x_ref, o_ref, k_scr):
    members, rows, lanes = x_ref.shape[0], x_ref.shape[3], x_ref.shape[4]
    sub = 8
    size = members * sub

    @pl.when((pl.program_id(0) == 0) & (pl.program_id(1) == 0))
    def _():
        spread = (
            lax.broadcasted_iota(jnp.int32, (size, members), 0) // sub
            == lax.broadcasted_iota(jnp.int32, (size, members), 1)
        ).astype(jnp.float32)
        full = mm_nt(mm(spread, p_ref[...]), spread)
        same = (
            lax.broadcasted_iota(jnp.int32, (size, size), 0) % sub
            == lax.broadcasted_iota(jnp.int32, (size, size), 1) % sub
        )
        k_scr[...] = jnp.where(same, full, 0.0)

    parts = [x_ref[:, 0, 0, h * sub : (h + 1) * sub, :].reshape(size, lanes) for h in range(rows // sub)]
    mixed = jnp.dot(k_scr[...], jnp.concatenate(parts, axis=1),
                    precision=lax.Precision.HIGHEST, preferred_element_type=jnp.float32)
    for h in range(rows // sub):
        o_ref[:, 0, 0, h * sub : (h + 1) * sub, :] = mixed[:, h * lanes : (h + 1) * lanes].reshape(members, sub, lanes)


def apply_transform(carried, cells):
    members, levels, fields, rows, lanes = cells.shape
    sub = 8
    block = pl.BlockSpec((members, 1, 1, rows, lanes), lambda a, b: (0, a, b, 0, 0))
    return pl.pallas_call(
        transform_kernel,
        out_shape=jax.ShapeDtypeStruct(cells.shape, cells.dtype),
        grid=(levels, fields),
        in_specs=[pl.BlockSpec((members, members), lambda a, b: (0, 0)), block],
        out_specs=block,
        scratch_shapes=[pltpu.VMEM((members * sub, members * sub), jnp.float32)],
        compiler_params=pltpu.CompilerParams(dimension_semantics=("arbitrary", "arbitrary")),
    )(carried, cells)


def on_device(
    background_sample,
    courant_eastward,
    courant_northward,
    diffusivity,
    sample_site,
    live_count,
    observed,
    error_variance,
    reach_mask,
):
    nx = lax.axis_size("gx")
    ny = lax.axis_size("gy")
    site_table = sample_site[0, 0]
    forecast, gathered = forecast_step(
        background_sample, courant_eastward, courant_northward, diffusivity, site_table.reshape(-1)
    )
    members = forecast.shape[0]
    counts = live_count[0, 0]
    observed_here = observed[0, 0]
    variance_here = error_variance[0, 0]
    batches, slot_count = site_table.shape
    slot_index = jnp.arange(slot_count)
    mask_index = jnp.arange(WIDTH)
    centre_one = ((mask_index[:, None] == RAD) & (mask_index[None, :] == RAD)).astype(jnp.float32)
    reach_weight = jnp.maximum(reach_mask[0, 0].astype(jnp.float32), centre_one).reshape(-1)
    all_sampled = gathered.reshape(members, batches, slot_count)
    y = jnp.transpose(all_sampled, (1, 0, 2))
    live_slot = (slot_index[None, :] < counts[:, None]).astype(jnp.float32)
    scale = (live_slot * (1.0 / jnp.sqrt(variance_here)))[:, None, :]
    carried = run_analysis(y, scale, observed_here[:, None, :], reach_weight, nx, ny)
    return apply_transform(carried, forecast)


def solution(mesh):
    in_specs = (
        P(None, None, None, "gx", "gy"),
        P(None, "gx", "gy"),
        P(None, "gx", "gy"),
        P("gx", "gy"),
        P("gx", "gy", None, None),
        P("gx", "gy", None),
        P("gx", "gy", None, None),
        P("gx", "gy", None, None),
        P("gx", "gy", None, None),
    )
    out_specs = P(None, None, None, "gx", "gy")
    return jax.shard_map(
        on_device, mesh=mesh, in_specs=in_specs, out_specs=out_specs, check_vma=False
    )
```

```python
import functools

import jax
import jax.numpy as jnp
from jax import lax
from jax.experimental import pallas as pl
from jax.experimental.pallas import tpu as pltpu
from jax.sharding import PartitionSpec as P

BATCHES = 4
RAD = 2
NS_STEPS = 6
WIDTH = 2 * RAD + 1
OFFSETS = [(dx, dy) for dx in range(-RAD, RAD + 1) for dy in range(-RAD, RAD + 1)]


def matmul_full(left, right):
    return jnp.dot(left, right, precision=lax.Precision.HIGHEST, preferred_element_type=jnp.float32)


def mixing_matrix(gram_matrix, projection):
    realisation_vectors = gram_matrix.shape[0]
    identity = jnp.eye(realisation_vectors, dtype=jnp.float32)
    precision_matrix = identity + gram_matrix / (realisation_vectors - 1)
    frobenius = jnp.sqrt(jnp.sum(precision_matrix * precision_matrix))
    iterate = precision_matrix / frobenius
    inverse = identity
    for repeat in range(NS_STEPS):
        factor = 1.5 * identity - 0.5 * matmul_full(inverse, iterate)
        iterate = matmul_full(iterate, factor)
        inverse = matmul_full(factor, inverse)
    transform = inverse / jnp.sqrt(frobenius)
    weights = matmul_full(transform, matmul_full(transform, projection)) / (realisation_vectors - 1)
    return transform + weights[:, None]


def stencil_kernel(x_ref, east_ref, west_ref, edge_ref, u_ref, v_ref, d_ref, col_ref, row_ref, o_ref, s_ref, east_scr, west_scr):
    rows = x_ref.shape[3]
    lanes = x_ref.shape[4]
    east_scr[:, :, :, 0 : rows - 1, :] = x_ref[:, :, :, 1:rows, :]
    east_scr[:, :, :, rows - 1 : rows, :] = east_ref[...]
    west_scr[:, :, :, 1:rows, :] = x_ref[:, :, :, 0 : rows - 1, :]
    west_scr[:, :, :, 0:1, :] = west_ref[...]
    centre = x_ref[...]
    east_cell = east_scr[...]
    west_cell = west_scr[...]
    edge = edge_ref[...]
    lane = lax.broadcasted_iota(jnp.int32, centre.shape, 4)
    north_cell = jnp.where(lane == lanes - 1, edge, pltpu.roll(centre, lanes - 1, 4))
    south_cell = jnp.where(lane == 0, edge, pltpu.roll(centre, 1, 4))
    u = u_ref[...][None, :, None]
    v = v_ref[...][None, :, None]
    d = d_ref[...][None, None, None]
    flux_x = jnp.maximum(u, 0.0) * (centre - west_cell) + jnp.minimum(u, 0.0) * (east_cell - centre)
    flux_y = jnp.maximum(v, 0.0) * (centre - south_cell) + jnp.minimum(v, 0.0) * (north_cell - centre)
    spread_term = d * (east_cell + west_cell + north_cell + south_cell - 4.0 * centre)
    result = centre + spread_term - flux_x - flux_y
    o_ref[...] = result
    block, rows_all = result.shape[0], result.shape[1] * result.shape[2] * rows
    flat = result.reshape(block * rows_all, lanes)
    high = flat.astype(jnp.bfloat16)
    rest = flat - high.astype(jnp.float32)
    mid = rest.astype(jnp.bfloat16)
    low = (rest - mid.astype(jnp.float32)).astype(jnp.bfloat16)
    pick = col_ref[...]
    picked = jnp.dot(high, pick, preferred_element_type=jnp.float32)
    picked = picked + jnp.dot(mid, pick, preferred_element_type=jnp.float32)
    picked = picked + jnp.dot(low, pick, preferred_element_type=jnp.float32)
    picked = picked.reshape(block, rows_all, picked.shape[-1]) * row_ref[...][None]
    s_ref[...] = jnp.sum(picked, axis=1)


def forecast_step(cells, courant_eastward, courant_northward, diffusivity, sites):
    nx = lax.axis_size("gx")
    ny = lax.axis_size("gy")
    rows, lanes = cells.shape[3], cells.shape[4]
    east_halo = lax.ppermute(cells[:, :, :, 0:1, :], "gx", [(i + 1, i) for i in range(nx - 1)])
    west_halo = lax.ppermute(cells[:, :, :, rows - 1 : rows, :], "gx", [(i, i + 1) for i in range(nx - 1)])
    lane_index = jnp.arange(lanes)
    pick = jnp.stack([lane_index == 0, lane_index == lanes - 1]).astype(jnp.float32)
    place = jnp.stack([lane_index == lanes - 1, lane_index == 0]).astype(jnp.float32)
    sides = jnp.einsum(
        "abcil,sl->sabci",
        cells, pick, precision=lax.Precision.HIGHEST, preferred_element_type=jnp.float32,
    )
    north_halo = lax.ppermute(sides[0], "gy", [(i + 1, i) for i in range(ny - 1)])
    south_halo = lax.ppermute(sides[1], "gy", [(i, i + 1) for i in range(ny - 1)])
    edge = jnp.einsum(
        "sabci,sl->abcil", jnp.stack([north_halo, south_halo]), place,
        precision=lax.Precision.HIGHEST, preferred_element_type=jnp.float32,
    )
    block = 8
    members = cells.shape[0]
    big = pl.BlockSpec((block,) + cells.shape[1:], lambda i: (i, 0, 0, 0, 0))
    thin = pl.BlockSpec((block,) + cells.shape[1:3] + (1, lanes), lambda i: (i, 0, 0, 0, 0))
    whole3 = pl.BlockSpec(courant_eastward.shape, lambda i: (0, 0, 0))
    whole2 = pl.BlockSpec(diffusivity.shape, lambda i: (0, 0))
    site_count = sites.shape[0]
    rows_all = cells.shape[1] * cells.shape[2] * rows
    col_pick = (sites[None, :] % lanes == jnp.arange(lanes)[:, None]).astype(jnp.bfloat16)
    row_pick = (sites[None, :] // lanes == jnp.arange(rows_all)[:, None]).astype(jnp.float32)
    picks = pl.BlockSpec((lanes, site_count), lambda i: (0, 0))
    return pl.pallas_call(
        stencil_kernel,
        out_shape=(
            jax.ShapeDtypeStruct(cells.shape, cells.dtype),
            jax.ShapeDtypeStruct((members, site_count), cells.dtype),
        ),
        grid=(members // block,),
        in_specs=[big, thin, thin, big, whole3, whole3, whole2, picks,
                  pl.BlockSpec((rows_all, site_count), lambda i: (0, 0))],
        out_specs=(big, pl.BlockSpec((block, site_count), lambda i: (i, 0))),
        scratch_shapes=[
            pltpu.VMEM((block,) + cells.shape[1:], cells.dtype),
            pltpu.VMEM((block,) + cells.shape[1:], cells.dtype),
        ],
    )(cells, east_halo, west_halo, edge, courant_eastward, courant_northward, diffusivity, col_pick, row_pick)


def mm(left, right):
    return jnp.dot(left, right, precision=lax.Precision.HIGHEST, preferred_element_type=jnp.float32)


def mm_nt(left, right):
    return lax.dot_general(
        left, right, (((1,), (1,)), ((), ())),
        precision=lax.Precision.HIGHEST, preferred_element_type=jnp.float32,
    )


def analysis_kernel(
    nx, ny, y_ref, scale_ref, obs_ref, w_ref, out_ref,
    slots, payload, rows_t, total, carried, send_sem, recv_sem,
):
    me_x = lax.axis_index("gx")
    me_y = lax.axis_index("gy")
    members = y_ref.shape[1]
    slot_count = y_ref.shape[2]
    wide = payload.shape[2]
    batches = y_ref.shape[0]
    centre_k = RAD * WIDTH + RAD

    def inside(x, y):
        return (x >= 0) & (x < nx) & (y >= 0) & (y < ny)

    barrier = pltpu.get_barrier_semaphore()
    partners = jnp.int32(0)
    for dx, dy in OFFSETS:
        if dx == 0 and dy == 0:
            continue
        ok = inside(me_x - dx, me_y - dy)
        partners = partners + ok.astype(jnp.int32)

        @pl.when(ok)
        def _():
            pl.semaphore_signal(
                barrier, inc=1, device_id=(me_x - dx, me_y - dy),
                device_id_type=pl.DeviceIdType.MESH,
            )

    pl.semaphore_wait(barrier, partners)

    row = lax.broadcasted_iota(jnp.int32, (members, members), 0)
    col = lax.broadcasted_iota(jnp.int32, (members, members), 1)
    identity = (row == col).astype(jnp.float32)
    carried[...] = identity
    rows_t[...] = jnp.zeros(rows_t.shape, jnp.float32)

    def batch_step(b, _):
        par = b % 2
        sampled = mm(carried[...], y_ref[b])
        prior_mean = jnp.mean(sampled, axis=0, keepdims=True)
        scale = scale_ref[b]
        scaled_rows = scale * (sampled - prior_mean)
        innovation = scale * (obs_ref[b] - prior_mean)
        rows_t[0:members, :] = scaled_rows
        rows_t[members : members + 1, :] = innovation
        payload[par] = mm_nt(scaled_rows, rows_t[...])

        copies = []
        for k, (dx, dy) in enumerate(OFFSETS):
            if dx == 0 and dy == 0:
                continue
            copy = pltpu.make_async_remote_copy(
                src_ref=payload.at[par],
                dst_ref=slots.at[par, k],
                send_sem=send_sem.at[par, k],
                recv_sem=recv_sem.at[par, k],
                device_id=(me_x - dx, me_y - dy),
                device_id_type=pl.DeviceIdType.MESH,
            )
            ok = inside(me_x - dx, me_y - dy)

            @pl.when(ok)
            def _():
                copy.start()

            copies.append((k, dx, dy, copy, ok))

        total[...] = jnp.zeros(total.shape, jnp.float32)
        for k, (dx, dy) in enumerate(OFFSETS):
            if dx == 0 and dy == 0:
                total[...] += w_ref[k] * payload[par]
        for k, dx, dy, copy, ok in copies:
            @pl.when(ok)
            def _():
                copy.wait_send()

            arrives = inside(me_x + dx, me_y + dy)

            @pl.when(arrives)
            def _():
                copy.wait_recv()
                total[...] += w_ref[k] * slots[par, k]

        summed = total[...]
        gram_total = summed[:, 0:members]
        proj_block = summed[:, members : 2 * members]
        precision_matrix = identity + gram_total / (members - 1)
        squares = precision_matrix * precision_matrix
        frobenius = jnp.sqrt(jnp.sum(jnp.sum(squares, axis=1, keepdims=True), axis=0, keepdims=True))
        iterate = precision_matrix / frobenius

        def ns_step(_, pair):
            iterate, inverse = pair
            factor = 1.5 * identity - 0.5 * mm(inverse, iterate)
            return mm(iterate, factor), mm(factor, inverse)

        pair = (iterate, identity)
        for _i in range(NS_STEPS):
            pair = ns_step(_i, pair)
        iterate, inverse = pair
        transform = inverse / jnp.sqrt(frobenius)
        weights = mm(transform, mm(transform, proj_block)) / (members - 1)
        mixing = transform + weights[:, 0:1]
        mixing_t = mm_nt(identity, mixing)
        step = 1.0 / members + mixing_t - jnp.mean(mixing_t, axis=1, keepdims=True)
        carried[...] = mm(step, carried[...])
        return 0

    lax.fori_loop(0, batches, batch_step, 0)
    out_ref[...] = carried[...]


def run_analysis(y, scale, obs, weights, nx, ny):
    batches, members, slot_count = y.shape
    count = len(OFFSETS)
    wide = 2 * members
    return pl.pallas_call(
        functools.partial(analysis_kernel, nx, ny),
        out_shape=jax.ShapeDtypeStruct((members, members), jnp.float32),
        in_specs=[
            pl.BlockSpec(memory_space=pltpu.VMEM),
            pl.BlockSpec(memory_space=pltpu.VMEM),
            pl.BlockSpec(memory_space=pltpu.VMEM),
            pl.BlockSpec(memory_space=pltpu.SMEM),
        ],
        out_specs=pl.BlockSpec(memory_space=pltpu.VMEM),
        scratch_shapes=[
            pltpu.VMEM((2, count, members, wide), jnp.float32),
            pltpu.VMEM((2, members, wide), jnp.float32),
            pltpu.VMEM((wide, slot_count), jnp.float32),
            pltpu.VMEM((members, wide), jnp.float32),
            pltpu.VMEM((members, members), jnp.float32),
            pltpu.SemaphoreType.DMA((2, count)),
            pltpu.SemaphoreType.DMA((2, count)),
        ],
        compiler_params=pltpu.CompilerParams(collective_id=0, has_side_effects=True),
    )(y, scale, obs, weights)


def transform_kernel(p_ref, x_ref, o_ref, k_scr):
    members, rows, lanes = x_ref.shape[0], x_ref.shape[3], x_ref.shape[4]
    sub = 8
    size = members * sub

    @pl.when((pl.program_id(0) == 0) & (pl.program_id(1) == 0))
    def _():
        spread = (
            lax.broadcasted_iota(jnp.int32, (size, members), 0) // sub
            == lax.broadcasted_iota(jnp.int32, (size, members), 1)
        ).astype(jnp.float32)
        full = mm_nt(mm(spread, p_ref[...]), spread)
        same = (
            lax.broadcasted_iota(jnp.int32, (size, size), 0) % sub
            == lax.broadcasted_iota(jnp.int32, (size, size), 1) % sub
        )
        k_scr[...] = jnp.where(same, full, 0.0)

    parts = [x_ref[:, 0, 0, h * sub : (h + 1) * sub, :].reshape(size, lanes) for h in range(rows // sub)]
    mixed = jnp.dot(k_scr[...], jnp.concatenate(parts, axis=1),
                    precision=lax.Precision.HIGH, preferred_element_type=jnp.float32)
    for h in range(rows // sub):
        o_ref[:, 0, 0, h * sub : (h + 1) * sub, :] = mixed[:, h * lanes : (h + 1) * lanes].reshape(members, sub, lanes)


def apply_transform(carried, cells):
    members, levels, fields, rows, lanes = cells.shape
    sub = 8
    block = pl.BlockSpec((members, 1, 1, rows, lanes), lambda a, b: (0, a, b, 0, 0))
    return pl.pallas_call(
        transform_kernel,
        out_shape=jax.ShapeDtypeStruct(cells.shape, cells.dtype),
        grid=(levels, fields),
        in_specs=[pl.BlockSpec((members, members), lambda a, b: (0, 0)), block],
        out_specs=block,
        scratch_shapes=[pltpu.VMEM((members * sub, members * sub), jnp.float32)],
        compiler_params=pltpu.CompilerParams(dimension_semantics=("arbitrary", "arbitrary")),
    )(carried, cells)


def on_device(
    background_sample,
    courant_eastward,
    courant_northward,
    diffusivity,
    sample_site,
    live_count,
    observed,
    error_variance,
    reach_mask,
):
    nx = lax.axis_size("gx")
    ny = lax.axis_size("gy")
    site_table = sample_site[0, 0]
    forecast, gathered = forecast_step(
        background_sample, courant_eastward, courant_northward, diffusivity, site_table.reshape(-1)
    )
    members = forecast.shape[0]
    counts = live_count[0, 0]
    observed_here = observed[0, 0]
    variance_here = error_variance[0, 0]
    batches, slot_count = site_table.shape
    slot_index = jnp.arange(slot_count)
    mask_index = jnp.arange(WIDTH)
    centre_one = ((mask_index[:, None] == RAD) & (mask_index[None, :] == RAD)).astype(jnp.float32)
    reach_weight = jnp.maximum(reach_mask[0, 0].astype(jnp.float32), centre_one).reshape(-1)
    all_sampled = gathered.reshape(members, batches, slot_count)
    y = jnp.transpose(all_sampled, (1, 0, 2))
    live_slot = (slot_index[None, :] < counts[:, None]).astype(jnp.float32)
    scale = (live_slot * (1.0 / jnp.sqrt(variance_here)))[:, None, :]
    carried = run_analysis(y, scale, observed_here[:, None, :], reach_weight, nx, ny)
    return apply_transform(carried, forecast)


def solution(mesh):
    in_specs = (
        P(None, None, None, "gx", "gy"),
        P(None, "gx", "gy"),
        P(None, "gx", "gy"),
        P("gx", "gy"),
        P("gx", "gy", None, None),
        P("gx", "gy", None),
        P("gx", "gy", None, None),
        P("gx", "gy", None, None),
        P("gx", "gy", None, None),
    )
    out_specs = P(None, None, None, "gx", "gy")
    return jax.shard_map(
        on_device, mesh=mesh, in_specs=in_specs, out_specs=out_specs, check_vma=False
    )
```

```python
import functools

import jax
import jax.numpy as jnp
from jax import lax
from jax.experimental import pallas as pl
from jax.experimental.pallas import tpu as pltpu
from jax.sharding import PartitionSpec as P

BATCHES = 4
RAD = 2
NS_STEPS = 6
WIDTH = 2 * RAD + 1
OFFSETS = [(dx, dy) for dx in range(-RAD, RAD + 1) for dy in range(-RAD, RAD + 1)]


def matmul_full(left, right):
    return jnp.dot(left, right, precision=lax.Precision.HIGHEST, preferred_element_type=jnp.float32)


def mixing_matrix(gram_matrix, projection):
    realisation_vectors = gram_matrix.shape[0]
    identity = jnp.eye(realisation_vectors, dtype=jnp.float32)
    precision_matrix = identity + gram_matrix / (realisation_vectors - 1)
    frobenius = jnp.sqrt(jnp.sum(precision_matrix * precision_matrix))
    iterate = precision_matrix / frobenius
    inverse = identity
    for repeat in range(NS_STEPS):
        factor = 1.5 * identity - 0.5 * matmul_full(inverse, iterate)
        iterate = matmul_full(iterate, factor)
        inverse = matmul_full(factor, inverse)
    transform = inverse / jnp.sqrt(frobenius)
    weights = matmul_full(transform, matmul_full(transform, projection)) / (realisation_vectors - 1)
    return transform + weights[:, None]


def stencil_kernel(x_ref, east_ref, west_ref, edge_ref, u_ref, v_ref, d_ref, col_ref, row_ref, o_ref, s_ref, east_scr, west_scr):
    rows = x_ref.shape[3]
    lanes = x_ref.shape[4]
    east_scr[:, :, :, 0 : rows - 1, :] = x_ref[:, :, :, 1:rows, :]
    east_scr[:, :, :, rows - 1 : rows, :] = east_ref[...]
    west_scr[:, :, :, 1:rows, :] = x_ref[:, :, :, 0 : rows - 1, :]
    west_scr[:, :, :, 0:1, :] = west_ref[...]
    centre = x_ref[...]
    east_cell = east_scr[...]
    west_cell = west_scr[...]
    edge = edge_ref[...]
    lane = lax.broadcasted_iota(jnp.int32, centre.shape, 4)
    north_cell = jnp.where(lane == lanes - 1, edge, pltpu.roll(centre, lanes - 1, 4))
    south_cell = jnp.where(lane == 0, edge, pltpu.roll(centre, 1, 4))
    u = u_ref[...][None, :, None]
    v = v_ref[...][None, :, None]
    d = d_ref[...][None, None, None]
    flux_x = jnp.maximum(u, 0.0) * (centre - west_cell) + jnp.minimum(u, 0.0) * (east_cell - centre)
    flux_y = jnp.maximum(v, 0.0) * (centre - south_cell) + jnp.minimum(v, 0.0) * (north_cell - centre)
    spread_term = d * (east_cell + west_cell + north_cell + south_cell - 4.0 * centre)
    result = centre + spread_term - flux_x - flux_y
    o_ref[...] = result
    block, rows_all = result.shape[0], result.shape[1] * result.shape[2] * rows
    flat = result.reshape(block * rows_all, lanes)
    high = flat.astype(jnp.bfloat16)
    rest = flat - high.astype(jnp.float32)
    mid = rest.astype(jnp.bfloat16)
    low = (rest - mid.astype(jnp.float32)).astype(jnp.bfloat16)
    pick = col_ref[...]
    picked = jnp.dot(high, pick, preferred_element_type=jnp.float32)
    picked = picked + jnp.dot(mid, pick, preferred_element_type=jnp.float32)
    picked = picked + jnp.dot(low, pick, preferred_element_type=jnp.float32)
    picked = picked.reshape(block, rows_all, picked.shape[-1]) * row_ref[...][None]
    s_ref[...] = jnp.sum(picked, axis=1)


def forecast_step(cells, courant_eastward, courant_northward, diffusivity, sites):
    nx = lax.axis_size("gx")
    ny = lax.axis_size("gy")
    rows, lanes = cells.shape[3], cells.shape[4]
    east_halo = lax.ppermute(cells[:, :, :, 0:1, :], "gx", [(i + 1, i) for i in range(nx - 1)])
    west_halo = lax.ppermute(cells[:, :, :, rows - 1 : rows, :], "gx", [(i, i + 1) for i in range(nx - 1)])
    lane_index = jnp.arange(lanes)
    pick = jnp.stack([lane_index == 0, lane_index == lanes - 1]).astype(jnp.float32)
    place = jnp.stack([lane_index == lanes - 1, lane_index == 0]).astype(jnp.float32)
    sides = jnp.einsum(
        "abcil,sl->sabci",
        cells, pick, precision=lax.Precision.HIGHEST, preferred_element_type=jnp.float32,
    )
    north_halo = lax.ppermute(sides[0], "gy", [(i + 1, i) for i in range(ny - 1)])
    south_halo = lax.ppermute(sides[1], "gy", [(i, i + 1) for i in range(ny - 1)])
    edge = jnp.einsum(
        "sabci,sl->abcil", jnp.stack([north_halo, south_halo]), place,
        precision=lax.Precision.HIGHEST, preferred_element_type=jnp.float32,
    )
    block = 8
    members = cells.shape[0]
    big = pl.BlockSpec((block,) + cells.shape[1:], lambda i: (i, 0, 0, 0, 0))
    thin = pl.BlockSpec((block,) + cells.shape[1:3] + (1, lanes), lambda i: (i, 0, 0, 0, 0))
    whole3 = pl.BlockSpec(courant_eastward.shape, lambda i: (0, 0, 0))
    whole2 = pl.BlockSpec(diffusivity.shape, lambda i: (0, 0))
    site_count = sites.shape[0]
    rows_all = cells.shape[1] * cells.shape[2] * rows
    col_pick = (sites[None, :] % lanes == jnp.arange(lanes)[:, None]).astype(jnp.bfloat16)
    row_pick = (sites[None, :] // lanes == jnp.arange(rows_all)[:, None]).astype(jnp.float32)
    picks = pl.BlockSpec((lanes, site_count), lambda i: (0, 0))
    return pl.pallas_call(
        stencil_kernel,
        out_shape=(
            jax.ShapeDtypeStruct(cells.shape, cells.dtype),
            jax.ShapeDtypeStruct((members, site_count), cells.dtype),
        ),
        grid=(members // block,),
        in_specs=[big, thin, thin, big, whole3, whole3, whole2, picks,
                  pl.BlockSpec((rows_all, site_count), lambda i: (0, 0))],
        out_specs=(big, pl.BlockSpec((block, site_count), lambda i: (i, 0))),
        scratch_shapes=[
            pltpu.VMEM((block,) + cells.shape[1:], cells.dtype),
            pltpu.VMEM((block,) + cells.shape[1:], cells.dtype),
        ],
    )(cells, east_halo, west_halo, edge, courant_eastward, courant_northward, diffusivity, col_pick, row_pick)


def mm(left, right):
    return jnp.dot(left, right, precision=lax.Precision.HIGHEST, preferred_element_type=jnp.float32)


def mm_nt(left, right):
    return lax.dot_general(
        left, right, (((1,), (1,)), ((), ())),
        precision=lax.Precision.HIGHEST, preferred_element_type=jnp.float32,
    )


def analysis_kernel(
    nx, ny, y_ref, scale_ref, obs_ref, w_ref, out_ref,
    slots, payload, rows_t, rows_u, total, carried, send_sem, recv_sem,
):
    me_x = lax.axis_index("gx")
    me_y = lax.axis_index("gy")
    members = y_ref.shape[1]
    slot_count = y_ref.shape[2]
    wide = payload.shape[2]
    batches = y_ref.shape[0]
    centre_k = RAD * WIDTH + RAD

    def inside(x, y):
        return (x >= 0) & (x < nx) & (y >= 0) & (y < ny)

    barrier = pltpu.get_barrier_semaphore()
    partners = jnp.int32(0)
    for dx, dy in OFFSETS:
        if dx == 0 and dy == 0:
            continue
        ok = inside(me_x - dx, me_y - dy)
        partners = partners + ok.astype(jnp.int32)

        @pl.when(ok)
        def _():
            pl.semaphore_signal(
                barrier, inc=1, device_id=(me_x - dx, me_y - dy),
                device_id_type=pl.DeviceIdType.MESH,
            )

    pl.semaphore_wait(barrier, partners)

    half = members // 2
    row = lax.broadcasted_iota(jnp.int32, (members, members), 0)
    col = lax.broadcasted_iota(jnp.int32, (members, members), 1)
    identity = (row == col).astype(jnp.float32)
    pair_row = lax.broadcasted_iota(jnp.int32, (half, members), 0)
    pair_col = lax.broadcasted_iota(jnp.int32, (half, members), 1)
    take_even = (pair_col == 2 * pair_row).astype(jnp.float32)
    take_odd = (pair_col == 2 * pair_row + 1).astype(jnp.float32)
    spread_row = lax.broadcasted_iota(jnp.int32, (members, half), 0)
    spread_col = lax.broadcasted_iota(jnp.int32, (members, half), 1)
    put_even = (spread_row == 2 * spread_col).astype(jnp.float32)
    put_odd = (spread_row == 2 * spread_col + 1).astype(jnp.float32)
    first_row = lax.broadcasted_iota(jnp.int32, (8, slot_count), 0) == 0
    carried[...] = identity
    rows_t[...] = jnp.zeros(rows_t.shape, jnp.float32)
    rows_u[...] = jnp.zeros(rows_u.shape, jnp.float32)

    def batch_step(b, _):
        par = b % 2
        sampled = mm(carried[...], y_ref[b])
        prior_mean = jnp.mean(sampled, axis=0, keepdims=True)
        scale = scale_ref[b]
        scaled_rows = scale * (sampled - prior_mean)
        innovation = scale * (obs_ref[b] - prior_mean)
        rows_t[0:members, :] = scaled_rows
        rows_u[members : 2 * members, :] = scaled_rows
        lead = mm_nt(mm(take_even, scaled_rows), rows_t[...]) + mm_nt(mm(take_odd, scaled_rows), rows_u[...])
        tail = mm_nt(jnp.where(first_row, innovation, 0.0), rows_t[...])
        payload[par, 0:half, :] = lead
        payload[par, half : half + 8, :] = tail

        copies = []
        for k, (dx, dy) in enumerate(OFFSETS):
            if dx == 0 and dy == 0:
                continue
            copy = pltpu.make_async_remote_copy(
                src_ref=payload.at[par],
                dst_ref=slots.at[par, k],
                send_sem=send_sem.at[par, k],
                recv_sem=recv_sem.at[par, k],
                device_id=(me_x - dx, me_y - dy),
                device_id_type=pl.DeviceIdType.MESH,
            )
            ok = inside(me_x - dx, me_y - dy)

            @pl.when(ok)
            def _():
                copy.start()

            copies.append((k, dx, dy, copy, ok))

        total[...] = jnp.zeros(total.shape, jnp.float32)
        for k, (dx, dy) in enumerate(OFFSETS):
            if dx == 0 and dy == 0:
                total[...] += w_ref[k] * payload[par]
        for k, dx, dy, copy, ok in copies:
            @pl.when(ok)
            def _():
                copy.wait_send()

            arrives = inside(me_x + dx, me_y + dy)

            @pl.when(arrives)
            def _():
                copy.wait_recv()
                total[...] += w_ref[k] * slots[par, k]

        summed = total[...]
        packed = summed[0:half, :]
        gram_total = mm(put_even, packed[:, 0:members]) + mm(put_odd, packed[:, members : 2 * members])
        proj_rows = summed[half : half + 8, 0:members]
        precision_matrix = identity + gram_total / (members - 1)
        squares = precision_matrix * precision_matrix
        frobenius = jnp.sqrt(jnp.sum(jnp.sum(squares, axis=1, keepdims=True), axis=0, keepdims=True))
        iterate = precision_matrix / frobenius

        def ns_step(_, pair):
            iterate, inverse = pair
            factor = 1.5 * identity - 0.5 * mm(inverse, iterate)
            return mm(iterate, factor), mm(factor, inverse)

        pair = (iterate, identity)
        for _i in range(NS_STEPS):
            pair = ns_step(_i, pair)
        iterate, inverse = pair
        transform = inverse / jnp.sqrt(frobenius)
        weights = mm_nt(mm_nt(proj_rows, transform), transform) / (members - 1)
        mixing_t = mm_nt(identity, transform) + weights[0:1, :]
        step = 1.0 / members + mixing_t - jnp.mean(mixing_t, axis=1, keepdims=True)
        carried[...] = mm(step, carried[...])
        return 0

    lax.fori_loop(0, batches, batch_step, 0)
    out_ref[...] = carried[...]


def run_analysis(y, scale, obs, weights, nx, ny):
    batches, members, slot_count = y.shape
    count = len(OFFSETS)
    wide = 2 * members
    packed_rows = members // 2 + 8
    return pl.pallas_call(
        functools.partial(analysis_kernel, nx, ny),
        out_shape=jax.ShapeDtypeStruct((members, members), jnp.float32),
        in_specs=[
            pl.BlockSpec(memory_space=pltpu.VMEM),
            pl.BlockSpec(memory_space=pltpu.VMEM),
            pl.BlockSpec(memory_space=pltpu.VMEM),
            pl.BlockSpec(memory_space=pltpu.SMEM),
        ],
        out_specs=pl.BlockSpec(memory_space=pltpu.VMEM),
        scratch_shapes=[
            pltpu.VMEM((2, count, packed_rows, wide), jnp.float32),
            pltpu.VMEM((2, packed_rows, wide), jnp.float32),
            pltpu.VMEM((wide, slot_count), jnp.float32),
            pltpu.VMEM((wide, slot_count), jnp.float32),
            pltpu.VMEM((packed_rows, wide), jnp.float32),
            pltpu.VMEM((members, members), jnp.float32),
            pltpu.SemaphoreType.DMA((2, count)),
            pltpu.SemaphoreType.DMA((2, count)),
        ],
        compiler_params=pltpu.CompilerParams(collective_id=0, has_side_effects=True),
    )(y, scale, obs, weights)


def transform_kernel(p_ref, x_ref, o_ref, k_scr):
    members, rows, lanes = x_ref.shape[0], x_ref.shape[3], x_ref.shape[4]
    sub = 8
    size = members * sub

    @pl.when((pl.program_id(0) == 0) & (pl.program_id(1) == 0))
    def _():
        spread = (
            lax.broadcasted_iota(jnp.int32, (size, members), 0) // sub
            == lax.broadcasted_iota(jnp.int32, (size, members), 1)
        ).astype(jnp.float32)
        full = mm_nt(mm(spread, p_ref[...]), spread)
        same = (
            lax.broadcasted_iota(jnp.int32, (size, size), 0) % sub
            == lax.broadcasted_iota(jnp.int32, (size, size), 1) % sub
        )
        k_scr[...] = jnp.where(same, full, 0.0)

    parts = [x_ref[:, 0, 0, h * sub : (h + 1) * sub, :].reshape(size, lanes) for h in range(rows // sub)]
    mixed = jnp.dot(k_scr[...], jnp.concatenate(parts, axis=1),
                    precision=lax.Precision.HIGH, preferred_element_type=jnp.float32)
    for h in range(rows // sub):
        o_ref[:, 0, 0, h * sub : (h + 1) * sub, :] = mixed[:, h * lanes : (h + 1) * lanes].reshape(members, sub, lanes)


def apply_transform(carried, cells):
    members, levels, fields, rows, lanes = cells.shape
    sub = 8
    block = pl.BlockSpec((members, 1, 1, rows, lanes), lambda a, b: (0, a, b, 0, 0))
    return pl.pallas_call(
        transform_kernel,
        out_shape=jax.ShapeDtypeStruct(cells.shape, cells.dtype),
        grid=(levels, fields),
        in_specs=[pl.BlockSpec((members, members), lambda a, b: (0, 0)), block],
        out_specs=block,
        scratch_shapes=[pltpu.VMEM((members * sub, members * sub), jnp.float32)],
        compiler_params=pltpu.CompilerParams(dimension_semantics=("arbitrary", "arbitrary")),
    )(carried, cells)


def on_device(
    background_sample,
    courant_eastward,
    courant_northward,
    diffusivity,
    sample_site,
    live_count,
    observed,
    error_variance,
    reach_mask,
):
    nx = lax.axis_size("gx")
    ny = lax.axis_size("gy")
    site_table = sample_site[0, 0]
    forecast, gathered = forecast_step(
        background_sample, courant_eastward, courant_northward, diffusivity, site_table.reshape(-1)
    )
    members = forecast.shape[0]
    counts = live_count[0, 0]
    observed_here = observed[0, 0]
    variance_here = error_variance[0, 0]
    batches, slot_count = site_table.shape
    slot_index = jnp.arange(slot_count)
    mask_index = jnp.arange(WIDTH)
    centre_one = ((mask_index[:, None] == RAD) & (mask_index[None, :] == RAD)).astype(jnp.float32)
    reach_weight = jnp.maximum(reach_mask[0, 0].astype(jnp.float32), centre_one).reshape(-1)
    all_sampled = gathered.reshape(members, batches, slot_count)
    y = jnp.transpose(all_sampled, (1, 0, 2))
    live_slot = (slot_index[None, :] < counts[:, None]).astype(jnp.float32)
    scale = (live_slot * (1.0 / jnp.sqrt(variance_here)))[:, None, :]
    carried = run_analysis(y, scale, observed_here[:, None, :], reach_weight, nx, ny)
    return apply_transform(carried, forecast)


def solution(mesh):
    in_specs = (
        P(None, None, None, "gx", "gy"),
        P(None, "gx", "gy"),
        P(None, "gx", "gy"),
        P("gx", "gy"),
        P("gx", "gy", None, None),
        P("gx", "gy", None),
        P("gx", "gy", None, None),
        P("gx", "gy", None, None),
        P("gx", "gy", None, None),
    )
    out_specs = P(None, None, None, "gx", "gy")
    return jax.shard_map(
        on_device, mesh=mesh, in_specs=in_specs, out_specs=out_specs, check_vma=False
    )
```

```python
import functools

import jax
import jax.numpy as jnp
from jax import lax
from jax.experimental import pallas as pl
from jax.experimental.pallas import tpu as pltpu
from jax.sharding import PartitionSpec as P

BATCHES = 4
RAD = 2
NS_STEPS = 6
WIDTH = 2 * RAD + 1
OFFSETS = [(dx, dy) for dx in range(-RAD, RAD + 1) for dy in range(-RAD, RAD + 1)]


def matmul_full(left, right):
    return jnp.dot(left, right, precision=lax.Precision.HIGHEST, preferred_element_type=jnp.float32)


def mixing_matrix(gram_matrix, projection):
    realisation_vectors = gram_matrix.shape[0]
    identity = jnp.eye(realisation_vectors, dtype=jnp.float32)
    precision_matrix = identity + gram_matrix / (realisation_vectors - 1)
    frobenius = jnp.sqrt(jnp.sum(precision_matrix * precision_matrix))
    iterate = precision_matrix / frobenius
    inverse = identity
    for repeat in range(NS_STEPS):
        factor = 1.5 * identity - 0.5 * matmul_full(inverse, iterate)
        iterate = matmul_full(iterate, factor)
        inverse = matmul_full(factor, inverse)
    transform = inverse / jnp.sqrt(frobenius)
    weights = matmul_full(transform, matmul_full(transform, projection)) / (realisation_vectors - 1)
    return transform + weights[:, None]


def stencil_kernel(x_ref, east_ref, west_ref, halo_ref, u_ref, v_ref, d_ref, col_ref, row_ref, o_ref, s_ref, east_scr, west_scr):
    rows = x_ref.shape[3]
    lanes = x_ref.shape[4]
    east_scr[:, :, :, 0 : rows - 1, :] = x_ref[:, :, :, 1:rows, :]
    east_scr[:, :, :, rows - 1 : rows, :] = east_ref[...]
    west_scr[:, :, :, 1:rows, :] = x_ref[:, :, :, 0 : rows - 1, :]
    west_scr[:, :, :, 0:1, :] = west_ref[...]
    centre = x_ref[...]
    east_cell = east_scr[...]
    west_cell = west_scr[...]
    sides = halo_ref[...]
    padded = jnp.concatenate([sides, jnp.zeros((lanes - sides.shape[0], sides.shape[1]), jnp.float32)], axis=0)
    columns = jnp.transpose(padded)
    north_edge = jnp.broadcast_to(columns[:, 0:1], columns.shape).reshape(centre.shape)
    south_edge = jnp.broadcast_to(columns[:, 1:2], columns.shape).reshape(centre.shape)
    lane = lax.broadcasted_iota(jnp.int32, centre.shape, 4)
    north_cell = jnp.where(lane == lanes - 1, north_edge, pltpu.roll(centre, lanes - 1, 4))
    south_cell = jnp.where(lane == 0, south_edge, pltpu.roll(centre, 1, 4))
    u = u_ref[...][None, :, None]
    v = v_ref[...][None, :, None]
    d = d_ref[...][None, None, None]
    flux_x = jnp.maximum(u, 0.0) * (centre - west_cell) + jnp.minimum(u, 0.0) * (east_cell - centre)
    flux_y = jnp.maximum(v, 0.0) * (centre - south_cell) + jnp.minimum(v, 0.0) * (north_cell - centre)
    spread_term = d * (east_cell + west_cell + north_cell + south_cell - 4.0 * centre)
    result = centre + spread_term - flux_x - flux_y
    o_ref[...] = result
    block, rows_all = result.shape[0], result.shape[1] * result.shape[2] * rows
    flat = result.reshape(block * rows_all, lanes)
    high = flat.astype(jnp.bfloat16)
    rest = flat - high.astype(jnp.float32)
    mid = rest.astype(jnp.bfloat16)
    low = (rest - mid.astype(jnp.float32)).astype(jnp.bfloat16)
    pick = col_ref[...]
    picked = jnp.dot(high, pick, preferred_element_type=jnp.float32)
    picked = picked + jnp.dot(mid, pick, preferred_element_type=jnp.float32)
    picked = picked + jnp.dot(low, pick, preferred_element_type=jnp.float32)
    picked = picked.reshape(block, rows_all, picked.shape[-1]) * row_ref[...][None]
    s_ref[...] = jnp.sum(picked, axis=1)


def pick_kernel(p_ref, x_ref, o_ref):
    o_ref[...] = mm_nt(p_ref[...], x_ref[...])


def forecast_step(cells, courant_eastward, courant_northward, diffusivity, sites):
    nx = lax.axis_size("gx")
    ny = lax.axis_size("gy")
    rows, lanes = cells.shape[3], cells.shape[4]
    east_halo = lax.ppermute(cells[:, :, :, 0:1, :], "gx", [(i + 1, i) for i in range(nx - 1)])
    west_halo = lax.ppermute(cells[:, :, :, rows - 1 : rows, :], "gx", [(i, i + 1) for i in range(nx - 1)])
    flat_rows = cells.size // lanes
    lane_index = jnp.arange(lanes)
    pick = jnp.zeros((8, lanes), jnp.float32)
    pick = pick.at[0].set((lane_index == 0).astype(jnp.float32))
    pick = pick.at[1].set((lane_index == lanes - 1).astype(jnp.float32))
    part = flat_rows // 8
    sides = pl.pallas_call(
        pick_kernel,
        out_shape=jax.ShapeDtypeStruct((8, flat_rows), jnp.float32),
        grid=(8,),
        in_specs=[pl.BlockSpec((8, lanes), lambda i: (0, 0)), pl.BlockSpec((part, lanes), lambda i: (i, 0))],
        out_specs=pl.BlockSpec((8, part), lambda i: (0, i)),
    )(pick, cells.reshape(flat_rows, lanes))
    north_halo = lax.ppermute(sides[0:1], "gy", [(i + 1, i) for i in range(ny - 1)])
    south_halo = lax.ppermute(sides[1:2], "gy", [(i, i + 1) for i in range(ny - 1)])
    edge = jnp.concatenate([north_halo, south_halo, jnp.zeros((6, flat_rows), jnp.float32)], axis=0)
    block = 8
    members = cells.shape[0]
    big = pl.BlockSpec((block,) + cells.shape[1:], lambda i: (i, 0, 0, 0, 0))
    thin = pl.BlockSpec((block,) + cells.shape[1:3] + (1, lanes), lambda i: (i, 0, 0, 0, 0))
    whole3 = pl.BlockSpec(courant_eastward.shape, lambda i: (0, 0, 0))
    whole2 = pl.BlockSpec(diffusivity.shape, lambda i: (0, 0))
    site_count = sites.shape[0]
    rows_all = cells.shape[1] * cells.shape[2] * rows
    col_pick = (sites[None, :] % lanes == jnp.arange(lanes)[:, None]).astype(jnp.bfloat16)
    row_pick = (sites[None, :] // lanes == jnp.arange(rows_all)[:, None]).astype(jnp.float32)
    picks = pl.BlockSpec((lanes, site_count), lambda i: (0, 0))
    return pl.pallas_call(
        stencil_kernel,
        out_shape=(
            jax.ShapeDtypeStruct(cells.shape, cells.dtype),
            jax.ShapeDtypeStruct((members, site_count), cells.dtype),
        ),
        grid=(members // block,),
        in_specs=[big, thin, thin, pl.BlockSpec((8, flat_rows // (members // block)), lambda i: (0, i)), whole3, whole3, whole2, picks,
                  pl.BlockSpec((rows_all, site_count), lambda i: (0, 0))],
        out_specs=(big, pl.BlockSpec((block, site_count), lambda i: (i, 0))),
        scratch_shapes=[
            pltpu.VMEM((block,) + cells.shape[1:], cells.dtype),
            pltpu.VMEM((block,) + cells.shape[1:], cells.dtype),
        ],
    )(cells, east_halo, west_halo, edge, courant_eastward, courant_northward, diffusivity, col_pick, row_pick)


def mm(left, right):
    return jnp.dot(left, right, precision=lax.Precision.HIGHEST, preferred_element_type=jnp.float32)


def mm_nt(left, right):
    return lax.dot_general(
        left, right, (((1,), (1,)), ((), ())),
        precision=lax.Precision.HIGHEST, preferred_element_type=jnp.float32,
    )


def analysis_kernel(
    nx, ny, y_ref, scale_ref, obs_ref, w_ref, out_ref,
    slots, payload, rows_t, rows_u, total, carried, send_sem, recv_sem,
):
    me_x = lax.axis_index("gx")
    me_y = lax.axis_index("gy")
    members = y_ref.shape[1]
    slot_count = y_ref.shape[2]
    wide = payload.shape[2]
    batches = y_ref.shape[0]
    centre_k = RAD * WIDTH + RAD

    def inside(x, y):
        return (x >= 0) & (x < nx) & (y >= 0) & (y < ny)

    barrier = pltpu.get_barrier_semaphore()
    partners = jnp.int32(0)
    for dx, dy in OFFSETS:
        if dx == 0 and dy == 0:
            continue
        ok = inside(me_x - dx, me_y - dy)
        partners = partners + ok.astype(jnp.int32)

        @pl.when(ok)
        def _():
            pl.semaphore_signal(
                barrier, inc=1, device_id=(me_x - dx, me_y - dy),
                device_id_type=pl.DeviceIdType.MESH,
            )

    pl.semaphore_wait(barrier, partners)

    half = members // 2
    row = lax.broadcasted_iota(jnp.int32, (members, members), 0)
    col = lax.broadcasted_iota(jnp.int32, (members, members), 1)
    identity = (row == col).astype(jnp.float32)
    pair_row = lax.broadcasted_iota(jnp.int32, (half, members), 0)
    pair_col = lax.broadcasted_iota(jnp.int32, (half, members), 1)
    take_even = (pair_col == 2 * pair_row).astype(jnp.float32)
    take_odd = (pair_col == 2 * pair_row + 1).astype(jnp.float32)
    spread_row = lax.broadcasted_iota(jnp.int32, (members, half), 0)
    spread_col = lax.broadcasted_iota(jnp.int32, (members, half), 1)
    put_even = (spread_row == 2 * spread_col).astype(jnp.float32)
    put_odd = (spread_row == 2 * spread_col + 1).astype(jnp.float32)
    first_row = lax.broadcasted_iota(jnp.int32, (8, slot_count), 0) == 0
    carried[...] = identity
    rows_t[...] = jnp.zeros(rows_t.shape, jnp.float32)
    rows_u[...] = jnp.zeros(rows_u.shape, jnp.float32)

    def batch_step(b, _):
        par = b % 2
        sampled = mm(carried[...], y_ref[b])
        prior_mean = jnp.mean(sampled, axis=0, keepdims=True)
        scale = scale_ref[b]
        scaled_rows = scale * (sampled - prior_mean)
        innovation = scale * (obs_ref[b] - prior_mean)
        rows_t[0:members, :] = scaled_rows
        rows_u[members : 2 * members, :] = scaled_rows
        lead = mm_nt(mm(take_even, scaled_rows), rows_t[...]) + mm_nt(mm(take_odd, scaled_rows), rows_u[...])
        tail = mm_nt(jnp.where(first_row, innovation, 0.0), rows_t[...])
        payload[par, 0:half, :] = lead
        payload[par, half : half + 8, :] = tail

        copies = []
        for k, (dx, dy) in enumerate(OFFSETS):
            if dx == 0 and dy == 0:
                continue
            copy = pltpu.make_async_remote_copy(
                src_ref=payload.at[par],
                dst_ref=slots.at[par, k],
                send_sem=send_sem.at[par, k],
                recv_sem=recv_sem.at[par, k],
                device_id=(me_x - dx, me_y - dy),
                device_id_type=pl.DeviceIdType.MESH,
            )
            ok = inside(me_x - dx, me_y - dy)

            @pl.when(ok)
            def _():
                copy.start()

            copies.append((k, dx, dy, copy, ok))

        total[...] = jnp.zeros(total.shape, jnp.float32)
        for k, (dx, dy) in enumerate(OFFSETS):
            if dx == 0 and dy == 0:
                total[...] += w_ref[k] * payload[par]
        for k, dx, dy, copy, ok in copies:
            @pl.when(ok)
            def _():
                copy.wait_send()

            arrives = inside(me_x + dx, me_y + dy)

            @pl.when(arrives)
            def _():
                copy.wait_recv()
                total[...] += w_ref[k] * slots[par, k]

        summed = total[...]
        packed = summed[0:half, :]
        gram_total = mm(put_even, packed[:, 0:members]) + mm(put_odd, packed[:, members : 2 * members])
        proj_rows = summed[half : half + 8, 0:members]
        precision_matrix = identity + gram_total / (members - 1)
        squares = precision_matrix * precision_matrix
        frobenius = jnp.sqrt(jnp.sum(jnp.sum(squares, axis=1, keepdims=True), axis=0, keepdims=True))
        iterate = precision_matrix / frobenius

        def ns_step(_, pair):
            iterate, inverse = pair
            factor = 1.5 * identity - 0.5 * mm(inverse, iterate)
            return mm(iterate, factor), mm(factor, inverse)

        pair = (iterate, identity)
        for _i in range(NS_STEPS):
            pair = ns_step(_i, pair)
        iterate, inverse = pair
        transform = inverse / jnp.sqrt(frobenius)
        weights = mm_nt(mm_nt(proj_rows, transform), transform) / (members - 1)
        mixing_t = mm_nt(identity, transform) + weights[0:1, :]
        step = 1.0 / members + mixing_t - jnp.mean(mixing_t, axis=1, keepdims=True)
        carried[...] = mm(step, carried[...])
        return 0

    lax.fori_loop(0, batches, batch_step, 0)
    out_ref[...] = carried[...]


def run_analysis(y, scale, obs, weights, nx, ny):
    batches, members, slot_count = y.shape
    count = len(OFFSETS)
    wide = 2 * members
    packed_rows = members // 2 + 8
    return pl.pallas_call(
        functools.partial(analysis_kernel, nx, ny),
        out_shape=jax.ShapeDtypeStruct((members, members), jnp.float32),
        in_specs=[
            pl.BlockSpec(memory_space=pltpu.VMEM),
            pl.BlockSpec(memory_space=pltpu.VMEM),
            pl.BlockSpec(memory_space=pltpu.VMEM),
            pl.BlockSpec(memory_space=pltpu.SMEM),
        ],
        out_specs=pl.BlockSpec(memory_space=pltpu.VMEM),
        scratch_shapes=[
            pltpu.VMEM((2, count, packed_rows, wide), jnp.float32),
            pltpu.VMEM((2, packed_rows, wide), jnp.float32),
            pltpu.VMEM((wide, slot_count), jnp.float32),
            pltpu.VMEM((wide, slot_count), jnp.float32),
            pltpu.VMEM((packed_rows, wide), jnp.float32),
            pltpu.VMEM((members, members), jnp.float32),
            pltpu.SemaphoreType.DMA((2, count)),
            pltpu.SemaphoreType.DMA((2, count)),
        ],
        compiler_params=pltpu.CompilerParams(collective_id=0, has_side_effects=True),
    )(y, scale, obs, weights)


def transform_kernel(p_ref, x_ref, o_ref, k_scr):
    members, rows, lanes = x_ref.shape[0], x_ref.shape[3], x_ref.shape[4]
    sub = 8
    size = members * sub

    @pl.when((pl.program_id(0) == 0) & (pl.program_id(1) == 0))
    def _():
        spread = (
            lax.broadcasted_iota(jnp.int32, (size, members), 0) // sub
            == lax.broadcasted_iota(jnp.int32, (size, members), 1)
        ).astype(jnp.float32)
        full = mm_nt(mm(spread, p_ref[...]), spread)
        same = (
            lax.broadcasted_iota(jnp.int32, (size, size), 0) % sub
            == lax.broadcasted_iota(jnp.int32, (size, size), 1) % sub
        )
        k_scr[...] = jnp.where(same, full, 0.0)

    parts = [x_ref[:, 0, 0, h * sub : (h + 1) * sub, :].reshape(size, lanes) for h in range(rows // sub)]
    mixed = jnp.dot(k_scr[...], jnp.concatenate(parts, axis=1),
                    precision=lax.Precision.HIGH, preferred_element_type=jnp.float32)
    for h in range(rows // sub):
        o_ref[:, 0, 0, h * sub : (h + 1) * sub, :] = mixed[:, h * lanes : (h + 1) * lanes].reshape(members, sub, lanes)


def apply_transform(carried, cells):
    members, levels, fields, rows, lanes = cells.shape
    sub = 8
    block = pl.BlockSpec((members, 1, 1, rows, lanes), lambda a, b: (0, a, b, 0, 0))
    return pl.pallas_call(
        transform_kernel,
        out_shape=jax.ShapeDtypeStruct(cells.shape, cells.dtype),
        grid=(levels, fields),
        in_specs=[pl.BlockSpec((members, members), lambda a, b: (0, 0)), block],
        out_specs=block,
        scratch_shapes=[pltpu.VMEM((members * sub, members * sub), jnp.float32)],
        compiler_params=pltpu.CompilerParams(dimension_semantics=("arbitrary", "arbitrary")),
    )(carried, cells)


def on_device(
    background_sample,
    courant_eastward,
    courant_northward,
    diffusivity,
    sample_site,
    live_count,
    observed,
    error_variance,
    reach_mask,
):
    nx = lax.axis_size("gx")
    ny = lax.axis_size("gy")
    site_table = sample_site[0, 0]
    forecast, gathered = forecast_step(
        background_sample, courant_eastward, courant_northward, diffusivity, site_table.reshape(-1)
    )
    members = forecast.shape[0]
    counts = live_count[0, 0]
    observed_here = observed[0, 0]
    variance_here = error_variance[0, 0]
    batches, slot_count = site_table.shape
    slot_index = jnp.arange(slot_count)
    mask_index = jnp.arange(WIDTH)
    centre_one = ((mask_index[:, None] == RAD) & (mask_index[None, :] == RAD)).astype(jnp.float32)
    reach_weight = jnp.maximum(reach_mask[0, 0].astype(jnp.float32), centre_one).reshape(-1)
    all_sampled = gathered.reshape(members, batches, slot_count)
    y = jnp.transpose(all_sampled, (1, 0, 2))
    live_slot = (slot_index[None, :] < counts[:, None]).astype(jnp.float32)
    scale = (live_slot * (1.0 / jnp.sqrt(variance_here)))[:, None, :]
    carried = run_analysis(y, scale, observed_here[:, None, :], reach_weight, nx, ny)
    return apply_transform(carried, forecast)


def solution(mesh):
    in_specs = (
        P(None, None, None, "gx", "gy"),
        P(None, "gx", "gy"),
        P(None, "gx", "gy"),
        P("gx", "gy"),
        P("gx", "gy", None, None),
        P("gx", "gy", None),
        P("gx", "gy", None, None),
        P("gx", "gy", None, None),
        P("gx", "gy", None, None),
    )
    out_specs = P(None, None, None, "gx", "gy")
    return jax.shard_map(
        on_device, mesh=mesh, in_specs=in_specs, out_specs=out_specs, check_vma=False
    )
```

```python
import functools

import jax
import jax.numpy as jnp
from jax import lax
from jax.experimental import pallas as pl
from jax.experimental.pallas import tpu as pltpu
from jax.sharding import PartitionSpec as P

BATCHES = 4
RAD = 2
NS_STEPS = 6
WIDTH = 2 * RAD + 1
OFFSETS = [(dx, dy) for dx in range(-RAD, RAD + 1) for dy in range(-RAD, RAD + 1)]


def matmul_full(left, right):
    return jnp.dot(left, right, precision=lax.Precision.HIGHEST, preferred_element_type=jnp.float32)


def mixing_matrix(gram_matrix, projection):
    realisation_vectors = gram_matrix.shape[0]
    identity = jnp.eye(realisation_vectors, dtype=jnp.float32)
    precision_matrix = identity + gram_matrix / (realisation_vectors - 1)
    frobenius = jnp.sqrt(jnp.sum(precision_matrix * precision_matrix))
    iterate = precision_matrix / frobenius
    inverse = identity
    for repeat in range(NS_STEPS):
        factor = 1.5 * identity - 0.5 * matmul_full(inverse, iterate)
        iterate = matmul_full(iterate, factor)
        inverse = matmul_full(factor, inverse)
    transform = inverse / jnp.sqrt(frobenius)
    weights = matmul_full(transform, matmul_full(transform, projection)) / (realisation_vectors - 1)
    return transform + weights[:, None]


def stencil_kernel(x_ref, east_ref, west_ref, edge_ref, u_ref, v_ref, d_ref, col_ref, row_ref, o_ref, s_ref, east_scr, west_scr):
    rows = x_ref.shape[3]
    lanes = x_ref.shape[4]
    east_scr[:, :, :, 0 : rows - 1, :] = x_ref[:, :, :, 1:rows, :]
    east_scr[:, :, :, rows - 1 : rows, :] = east_ref[...]
    west_scr[:, :, :, 1:rows, :] = x_ref[:, :, :, 0 : rows - 1, :]
    west_scr[:, :, :, 0:1, :] = west_ref[...]
    centre = x_ref[...]
    east_cell = east_scr[...]
    west_cell = west_scr[...]
    edge = edge_ref[...]
    lane = lax.broadcasted_iota(jnp.int32, centre.shape, 4)
    north_cell = jnp.where(lane == lanes - 1, edge, pltpu.roll(centre, lanes - 1, 4))
    south_cell = jnp.where(lane == 0, edge, pltpu.roll(centre, 1, 4))
    u = u_ref[...][None, :, None]
    v = v_ref[...][None, :, None]
    d = d_ref[...][None, None, None]
    flux_x = jnp.maximum(u, 0.0) * (centre - west_cell) + jnp.minimum(u, 0.0) * (east_cell - centre)
    flux_y = jnp.maximum(v, 0.0) * (centre - south_cell) + jnp.minimum(v, 0.0) * (north_cell - centre)
    spread_term = d * (east_cell + west_cell + north_cell + south_cell - 4.0 * centre)
    result = centre + spread_term - flux_x - flux_y
    o_ref[...] = result
    block, rows_all = result.shape[0], result.shape[1] * result.shape[2] * rows
    flat = result.reshape(block * rows_all, lanes)
    high = flat.astype(jnp.bfloat16)
    rest = flat - high.astype(jnp.float32)
    mid = rest.astype(jnp.bfloat16)
    low = (rest - mid.astype(jnp.float32)).astype(jnp.bfloat16)
    pick = col_ref[...]
    picked = jnp.dot(high, pick, preferred_element_type=jnp.float32)
    picked = picked + jnp.dot(mid, pick, preferred_element_type=jnp.float32)
    picked = picked + jnp.dot(low, pick, preferred_element_type=jnp.float32)
    picked = picked.reshape(block, rows_all, picked.shape[-1]) * row_ref[...][None]
    s_ref[...] = jnp.sum(picked, axis=1)


def forecast_step(cells, courant_eastward, courant_northward, diffusivity, sites):
    nx = lax.axis_size("gx")
    ny = lax.axis_size("gy")
    rows, lanes = cells.shape[3], cells.shape[4]
    east_halo = lax.ppermute(cells[:, :, :, 0:1, :], "gx", [(i + 1, i) for i in range(nx - 1)])
    west_halo = lax.ppermute(cells[:, :, :, rows - 1 : rows, :], "gx", [(i, i + 1) for i in range(nx - 1)])
    lane_index = jnp.arange(lanes)
    pick = jnp.stack([lane_index == 0, lane_index == lanes - 1]).astype(jnp.float32)
    place = jnp.stack([lane_index == lanes - 1, lane_index == 0]).astype(jnp.float32)
    sides = jnp.einsum(
        "abcil,sl->sabci",
        cells, pick, precision=lax.Precision.HIGHEST, preferred_element_type=jnp.float32,
    )
    north_halo = lax.ppermute(sides[0], "gy", [(i + 1, i) for i in range(ny - 1)])
    south_halo = lax.ppermute(sides[1], "gy", [(i, i + 1) for i in range(ny - 1)])
    edge = jnp.einsum(
        "sabci,sl->abcil", jnp.stack([north_halo, south_halo]), place,
        precision=lax.Precision.HIGHEST, preferred_element_type=jnp.float32,
    )
    block = 8
    members = cells.shape[0]
    big = pl.BlockSpec((block,) + cells.shape[1:], lambda i: (i, 0, 0, 0, 0))
    thin = pl.BlockSpec((block,) + cells.shape[1:3] + (1, lanes), lambda i: (i, 0, 0, 0, 0))
    whole3 = pl.BlockSpec(courant_eastward.shape, lambda i: (0, 0, 0))
    whole2 = pl.BlockSpec(diffusivity.shape, lambda i: (0, 0))
    site_count = sites.shape[0]
    rows_all = cells.shape[1] * cells.shape[2] * rows
    col_pick = (sites[None, :] % lanes == jnp.arange(lanes)[:, None]).astype(jnp.bfloat16)
    row_pick = (sites[None, :] // lanes == jnp.arange(rows_all)[:, None]).astype(jnp.float32)
    picks = pl.BlockSpec((lanes, site_count), lambda i: (0, 0))
    return pl.pallas_call(
        stencil_kernel,
        out_shape=(
            jax.ShapeDtypeStruct(cells.shape, cells.dtype),
            jax.ShapeDtypeStruct((members, site_count), cells.dtype),
        ),
        grid=(members // block,),
        in_specs=[big, thin, thin, big, whole3, whole3, whole2, picks,
                  pl.BlockSpec((rows_all, site_count), lambda i: (0, 0))],
        out_specs=(big, pl.BlockSpec((block, site_count), lambda i: (i, 0))),
        scratch_shapes=[
            pltpu.VMEM((block,) + cells.shape[1:], cells.dtype),
            pltpu.VMEM((block,) + cells.shape[1:], cells.dtype),
        ],
    )(cells, east_halo, west_halo, edge, courant_eastward, courant_northward, diffusivity, col_pick, row_pick)


def mm(left, right):
    return jnp.dot(left, right, precision=lax.Precision.HIGHEST, preferred_element_type=jnp.float32)


def mm_nt(left, right):
    return lax.dot_general(
        left, right, (((1,), (1,)), ((), ())),
        precision=lax.Precision.HIGHEST, preferred_element_type=jnp.float32,
    )


def analysis_kernel(
    nx, ny, y_ref, scale_ref, obs_ref, w_ref, out_ref,
    slots, payload, rows_t, rows_u, total, carried, send_sem, recv_sem,
):
    me_x = lax.axis_index("gx")
    me_y = lax.axis_index("gy")
    members = y_ref.shape[1]
    slot_count = y_ref.shape[2]
    wide = payload.shape[2]
    batches = y_ref.shape[0]
    centre_k = RAD * WIDTH + RAD

    def inside(x, y):
        return (x >= 0) & (x < nx) & (y >= 0) & (y < ny)

    barrier = pltpu.get_barrier_semaphore()
    partners = jnp.int32(0)
    for dx, dy in OFFSETS:
        if dx == 0 and dy == 0:
            continue
        ok = inside(me_x - dx, me_y - dy)
        partners = partners + ok.astype(jnp.int32)

        @pl.when(ok)
        def _():
            pl.semaphore_signal(
                barrier, inc=1, device_id=(me_x - dx, me_y - dy),
                device_id_type=pl.DeviceIdType.MESH,
            )

    pl.semaphore_wait(barrier, partners)

    half = members // 2
    row = lax.broadcasted_iota(jnp.int32, (members, members), 0)
    col = lax.broadcasted_iota(jnp.int32, (members, members), 1)
    identity = (row == col).astype(jnp.float32)
    pair_row = lax.broadcasted_iota(jnp.int32, (half, members), 0)
    pair_col = lax.broadcasted_iota(jnp.int32, (half, members), 1)
    take_even = (pair_col == 2 * pair_row).astype(jnp.float32)
    take_odd = (pair_col == 2 * pair_row + 1).astype(jnp.float32)
    spread_row = lax.broadcasted_iota(jnp.int32, (members, half), 0)
    spread_col = lax.broadcasted_iota(jnp.int32, (members, half), 1)
    put_even = (spread_row == 2 * spread_col).astype(jnp.float32)
    put_odd = (spread_row == 2 * spread_col + 1).astype(jnp.float32)
    first_row = lax.broadcasted_iota(jnp.int32, (8, slot_count), 0) == 0
    carried[...] = identity
    rows_t[...] = jnp.zeros(rows_t.shape, jnp.float32)
    rows_u[...] = jnp.zeros(rows_u.shape, jnp.float32)

    def batch_step(b, _):
        par = b % 2
        sampled = mm(carried[...], y_ref[b])
        prior_mean = jnp.mean(sampled, axis=0, keepdims=True)
        scale = scale_ref[b]
        scaled_rows = scale * (sampled - prior_mean)
        innovation = scale * (obs_ref[b] - prior_mean)
        rows_t[0:members, :] = scaled_rows
        rows_u[members : 2 * members, :] = scaled_rows
        lead = mm_nt(mm(take_even, scaled_rows), rows_t[...]) + mm_nt(mm(take_odd, scaled_rows), rows_u[...])
        tail = mm_nt(jnp.where(first_row, innovation, 0.0), rows_t[...])
        payload[par, 0:half, :] = lead
        payload[par, half : half + 8, :] = tail

        copies = []
        for k, (dx, dy) in enumerate(OFFSETS):
            if dx == 0 and dy == 0:
                continue
            copy = pltpu.make_async_remote_copy(
                src_ref=payload.at[par],
                dst_ref=slots.at[par, k],
                send_sem=send_sem.at[par, k],
                recv_sem=recv_sem.at[par, k],
                device_id=(me_x - dx, me_y - dy),
                device_id_type=pl.DeviceIdType.MESH,
            )
            ok = inside(me_x - dx, me_y - dy)

            @pl.when(ok)
            def _():
                copy.start()

            copies.append((k, dx, dy, copy, ok))

        total[...] = jnp.zeros(total.shape, jnp.float32)
        for k, (dx, dy) in enumerate(OFFSETS):
            if dx == 0 and dy == 0:
                total[...] += w_ref[k] * payload[par]
        for k, dx, dy, copy, ok in copies:
            @pl.when(ok)
            def _():
                copy.wait_send()

            arrives = inside(me_x + dx, me_y + dy)

            @pl.when(arrives)
            def _():
                copy.wait_recv()
                total[...] += w_ref[k] * slots[par, k]

        summed = total[...]
        packed = summed[0:half, :]
        gram_total = mm(put_even, packed[:, 0:members]) + mm(put_odd, packed[:, members : 2 * members])
        proj_rows = summed[half : half + 8, 0:members]
        precision_matrix = identity + gram_total / (members - 1)
        squares = precision_matrix * precision_matrix
        frobenius = jnp.sqrt(jnp.sum(jnp.sum(squares, axis=1, keepdims=True), axis=0, keepdims=True))
        iterate = precision_matrix / frobenius

        def ns_step(_, pair):
            iterate, inverse = pair
            factor = 1.5 * identity - 0.5 * mm(inverse, iterate)
            both = mm(jnp.concatenate([iterate, inverse], axis=0), factor)
            return both[0:members], both[members : 2 * members]

        pair = (iterate, identity)
        for _i in range(NS_STEPS):
            pair = ns_step(_i, pair)
        iterate, inverse = pair
        transform = inverse / jnp.sqrt(frobenius)
        weights = mm_nt(mm_nt(proj_rows, transform), transform) / (members - 1)
        mixing_t = mm_nt(identity, transform) + weights[0:1, :]
        step = 1.0 / members + mixing_t - jnp.mean(mixing_t, axis=1, keepdims=True)
        carried[...] = mm(step, carried[...])
        return 0

    lax.fori_loop(0, batches, batch_step, 0)
    out_ref[...] = carried[...]


def run_analysis(y, scale, obs, weights, nx, ny):
    batches, members, slot_count = y.shape
    count = len(OFFSETS)
    wide = 2 * members
    packed_rows = members // 2 + 8
    return pl.pallas_call(
        functools.partial(analysis_kernel, nx, ny),
        out_shape=jax.ShapeDtypeStruct((members, members), jnp.float32),
        in_specs=[
            pl.BlockSpec(memory_space=pltpu.VMEM),
            pl.BlockSpec(memory_space=pltpu.VMEM),
            pl.BlockSpec(memory_space=pltpu.VMEM),
            pl.BlockSpec(memory_space=pltpu.SMEM),
        ],
        out_specs=pl.BlockSpec(memory_space=pltpu.VMEM),
        scratch_shapes=[
            pltpu.VMEM((2, count, packed_rows, wide), jnp.float32),
            pltpu.VMEM((2, packed_rows, wide), jnp.float32),
            pltpu.VMEM((wide, slot_count), jnp.float32),
            pltpu.VMEM((wide, slot_count), jnp.float32),
            pltpu.VMEM((packed_rows, wide), jnp.float32),
            pltpu.VMEM((members, members), jnp.float32),
            pltpu.SemaphoreType.DMA((2, count)),
            pltpu.SemaphoreType.DMA((2, count)),
        ],
        compiler_params=pltpu.CompilerParams(collective_id=0, has_side_effects=True),
    )(y, scale, obs, weights)


def transform_kernel(p_ref, x_ref, o_ref, k_scr):
    members, rows, lanes = x_ref.shape[0], x_ref.shape[3], x_ref.shape[4]
    sub = 8
    size = members * sub

    @pl.when((pl.program_id(0) == 0) & (pl.program_id(1) == 0))
    def _():
        spread = (
            lax.broadcasted_iota(jnp.int32, (size, members), 0) // sub
            == lax.broadcasted_iota(jnp.int32, (size, members), 1)
        ).astype(jnp.float32)
        full = mm_nt(mm(spread, p_ref[...]), spread)
        same = (
            lax.broadcasted_iota(jnp.int32, (size, size), 0) % sub
            == lax.broadcasted_iota(jnp.int32, (size, size), 1) % sub
        )
        k_scr[...] = jnp.where(same, full, 0.0)

    parts = [x_ref[:, 0, 0, h * sub : (h + 1) * sub, :].reshape(size, lanes) for h in range(rows // sub)]
    mixed = jnp.dot(k_scr[...], jnp.concatenate(parts, axis=1),
                    precision=lax.Precision.HIGH, preferred_element_type=jnp.float32)
    for h in range(rows // sub):
        o_ref[:, 0, 0, h * sub : (h + 1) * sub, :] = mixed[:, h * lanes : (h + 1) * lanes].reshape(members, sub, lanes)


def apply_transform(carried, cells):
    members, levels, fields, rows, lanes = cells.shape
    sub = 8
    block = pl.BlockSpec((members, 1, 1, rows, lanes), lambda a, b: (0, a, b, 0, 0))
    return pl.pallas_call(
        transform_kernel,
        out_shape=jax.ShapeDtypeStruct(cells.shape, cells.dtype),
        grid=(levels, fields),
        in_specs=[pl.BlockSpec((members, members), lambda a, b: (0, 0)), block],
        out_specs=block,
        scratch_shapes=[pltpu.VMEM((members * sub, members * sub), jnp.float32)],
        compiler_params=pltpu.CompilerParams(dimension_semantics=("arbitrary", "arbitrary")),
    )(carried, cells)


def on_device(
    background_sample,
    courant_eastward,
    courant_northward,
    diffusivity,
    sample_site,
    live_count,
    observed,
    error_variance,
    reach_mask,
):
    nx = lax.axis_size("gx")
    ny = lax.axis_size("gy")
    site_table = sample_site[0, 0]
    forecast, gathered = forecast_step(
        background_sample, courant_eastward, courant_northward, diffusivity, site_table.reshape(-1)
    )
    members = forecast.shape[0]
    counts = live_count[0, 0]
    observed_here = observed[0, 0]
    variance_here = error_variance[0, 0]
    batches, slot_count = site_table.shape
    slot_index = jnp.arange(slot_count)
    mask_index = jnp.arange(WIDTH)
    centre_one = ((mask_index[:, None] == RAD) & (mask_index[None, :] == RAD)).astype(jnp.float32)
    reach_weight = jnp.maximum(reach_mask[0, 0].astype(jnp.float32), centre_one).reshape(-1)
    all_sampled = gathered.reshape(members, batches, slot_count)
    y = jnp.transpose(all_sampled, (1, 0, 2))
    live_slot = (slot_index[None, :] < counts[:, None]).astype(jnp.float32)
    scale = (live_slot * (1.0 / jnp.sqrt(variance_here)))[:, None, :]
    carried = run_analysis(y, scale, observed_here[:, None, :], reach_weight, nx, ny)
    return apply_transform(carried, forecast)


def solution(mesh):
    in_specs = (
        P(None, None, None, "gx", "gy"),
        P(None, "gx", "gy"),
        P(None, "gx", "gy"),
        P("gx", "gy"),
        P("gx", "gy", None, None),
        P("gx", "gy", None),
        P("gx", "gy", None, None),
        P("gx", "gy", None, None),
        P("gx", "gy", None, None),
    )
    out_specs = P(None, None, None, "gx", "gy")
    return jax.shard_map(
        on_device, mesh=mesh, in_specs=in_specs, out_specs=out_specs, check_vma=False
    )
```

```python
import functools

import jax
import jax.numpy as jnp
from jax import lax
from jax.experimental import pallas as pl
from jax.experimental.pallas import tpu as pltpu
from jax.sharding import PartitionSpec as P

BATCHES = 4
RAD = 2
NS_STEPS = 6
WIDTH = 2 * RAD + 1
OFFSETS = [(dx, dy) for dx in range(-RAD, RAD + 1) for dy in range(-RAD, RAD + 1)]


def matmul_full(left, right):
    return jnp.dot(left, right, precision=lax.Precision.HIGHEST, preferred_element_type=jnp.float32)


def mixing_matrix(gram_matrix, projection):
    realisation_vectors = gram_matrix.shape[0]
    identity = jnp.eye(realisation_vectors, dtype=jnp.float32)
    precision_matrix = identity + gram_matrix / (realisation_vectors - 1)
    frobenius = jnp.sqrt(jnp.sum(precision_matrix * precision_matrix))
    iterate = precision_matrix / frobenius
    inverse = identity
    for repeat in range(NS_STEPS):
        factor = 1.5 * identity - 0.5 * matmul_full(inverse, iterate)
        iterate = matmul_full(iterate, factor)
        inverse = matmul_full(factor, inverse)
    transform = inverse / jnp.sqrt(frobenius)
    weights = matmul_full(transform, matmul_full(transform, projection)) / (realisation_vectors - 1)
    return transform + weights[:, None]


def stencil_kernel(x_ref, east_ref, west_ref, edge_ref, u_ref, v_ref, d_ref, col_ref, row_ref, o_ref, s_ref, east_scr, west_scr):
    rows = x_ref.shape[3]
    lanes = x_ref.shape[4]
    east_scr[:, :, :, 0 : rows - 1, :] = x_ref[:, :, :, 1:rows, :]
    east_scr[:, :, :, rows - 1 : rows, :] = east_ref[...]
    west_scr[:, :, :, 1:rows, :] = x_ref[:, :, :, 0 : rows - 1, :]
    west_scr[:, :, :, 0:1, :] = west_ref[...]
    centre = x_ref[...]
    east_cell = east_scr[...]
    west_cell = west_scr[...]
    edge = edge_ref[...]
    lane = lax.broadcasted_iota(jnp.int32, centre.shape, 4)
    north_cell = jnp.where(lane == lanes - 1, edge, pltpu.roll(centre, lanes - 1, 4))
    south_cell = jnp.where(lane == 0, edge, pltpu.roll(centre, 1, 4))
    u = u_ref[...][None, :, None]
    v = v_ref[...][None, :, None]
    d = d_ref[...][None, None, None]
    flux_x = jnp.maximum(u, 0.0) * (centre - west_cell) + jnp.minimum(u, 0.0) * (east_cell - centre)
    flux_y = jnp.maximum(v, 0.0) * (centre - south_cell) + jnp.minimum(v, 0.0) * (north_cell - centre)
    spread_term = d * (east_cell + west_cell + north_cell + south_cell - 4.0 * centre)
    result = centre + spread_term - flux_x - flux_y
    o_ref[...] = result
    block, rows_all = result.shape[0], result.shape[1] * result.shape[2] * rows
    flat = result.reshape(block * rows_all, lanes)
    high = flat.astype(jnp.bfloat16)
    rest = flat - high.astype(jnp.float32)
    mid = rest.astype(jnp.bfloat16)
    low = (rest - mid.astype(jnp.float32)).astype(jnp.bfloat16)
    pick = col_ref[...]
    picked = jnp.dot(high, pick, preferred_element_type=jnp.float32)
    picked = picked + jnp.dot(mid, pick, preferred_element_type=jnp.float32)
    picked = picked + jnp.dot(low, pick, preferred_element_type=jnp.float32)
    picked = picked.reshape(block, rows_all, picked.shape[-1]) * row_ref[...][None]
    s_ref[...] = jnp.sum(picked, axis=1)


def forecast_step(cells, courant_eastward, courant_northward, diffusivity, sites):
    nx = lax.axis_size("gx")
    ny = lax.axis_size("gy")
    rows, lanes = cells.shape[3], cells.shape[4]
    east_halo = lax.ppermute(cells[:, :, :, 0:1, :], "gx", [(i + 1, i) for i in range(nx - 1)])
    west_halo = lax.ppermute(cells[:, :, :, rows - 1 : rows, :], "gx", [(i, i + 1) for i in range(nx - 1)])
    lane_index = jnp.arange(lanes)
    pick = jnp.stack([lane_index == 0, lane_index == lanes - 1]).astype(jnp.float32)
    place = jnp.stack([lane_index == lanes - 1, lane_index == 0]).astype(jnp.float32)
    sides = jnp.einsum(
        "abcil,sl->sabci",
        cells, pick, precision=lax.Precision.HIGHEST, preferred_element_type=jnp.float32,
    )
    north_halo = lax.ppermute(sides[0], "gy", [(i + 1, i) for i in range(ny - 1)])
    south_halo = lax.ppermute(sides[1], "gy", [(i, i + 1) for i in range(ny - 1)])
    edge = jnp.einsum(
        "sabci,sl->abcil", jnp.stack([north_halo, south_halo]), place,
        precision=lax.Precision.HIGHEST, preferred_element_type=jnp.float32,
    )
    block = 8
    members = cells.shape[0]
    big = pl.BlockSpec((block,) + cells.shape[1:], lambda i: (i, 0, 0, 0, 0))
    thin = pl.BlockSpec((block,) + cells.shape[1:3] + (1, lanes), lambda i: (i, 0, 0, 0, 0))
    whole3 = pl.BlockSpec(courant_eastward.shape, lambda i: (0, 0, 0))
    whole2 = pl.BlockSpec(diffusivity.shape, lambda i: (0, 0))
    site_count = sites.shape[0]
    rows_all = cells.shape[1] * cells.shape[2] * rows
    col_pick = (sites[None, :] % lanes == jnp.arange(lanes)[:, None]).astype(jnp.bfloat16)
    row_pick = (sites[None, :] // lanes == jnp.arange(rows_all)[:, None]).astype(jnp.float32)
    picks = pl.BlockSpec((lanes, site_count), lambda i: (0, 0))
    return pl.pallas_call(
        stencil_kernel,
        out_shape=(
            jax.ShapeDtypeStruct(cells.shape, cells.dtype),
            jax.ShapeDtypeStruct((members, site_count), cells.dtype),
        ),
        grid=(members // block,),
        in_specs=[big, thin, thin, big, whole3, whole3, whole2, picks,
                  pl.BlockSpec((rows_all, site_count), lambda i: (0, 0))],
        out_specs=(big, pl.BlockSpec((block, site_count), lambda i: (i, 0))),
        scratch_shapes=[
            pltpu.VMEM((block,) + cells.shape[1:], cells.dtype),
            pltpu.VMEM((block,) + cells.shape[1:], cells.dtype),
        ],
    )(cells, east_halo, west_halo, edge, courant_eastward, courant_northward, diffusivity, col_pick, row_pick)


def mm(left, right):
    return jnp.dot(left, right, precision=lax.Precision.HIGHEST, preferred_element_type=jnp.float32)


def mm_nt(left, right):
    return lax.dot_general(
        left, right, (((1,), (1,)), ((), ())),
        precision=lax.Precision.HIGHEST, preferred_element_type=jnp.float32,
    )


def analysis_kernel(
    nx, ny, y_ref, scale_ref, obs_ref, w_ref, out_ref,
    slots, payload, rows_t, rows_u, total, carried, send_sem, recv_sem,
):
    me_x = lax.axis_index("gx")
    me_y = lax.axis_index("gy")
    members = y_ref.shape[1]
    slot_count = y_ref.shape[2]
    wide = payload.shape[2]
    batches = y_ref.shape[0]
    centre_k = RAD * WIDTH + RAD

    def inside(x, y):
        return (x >= 0) & (x < nx) & (y >= 0) & (y < ny)

    barrier = pltpu.get_barrier_semaphore()
    partners = jnp.int32(0)
    for dx, dy in OFFSETS:
        if dx == 0 and dy == 0:
            continue
        ok = inside(me_x - dx, me_y - dy)
        partners = partners + ok.astype(jnp.int32)

        @pl.when(ok)
        def _():
            pl.semaphore_signal(
                barrier, inc=1, device_id=(me_x - dx, me_y - dy),
                device_id_type=pl.DeviceIdType.MESH,
            )

    pl.semaphore_wait(barrier, partners)

    half = members // 2
    row = lax.broadcasted_iota(jnp.int32, (members, members), 0)
    col = lax.broadcasted_iota(jnp.int32, (members, members), 1)
    identity = (row == col).astype(jnp.float32)
    pair_row = lax.broadcasted_iota(jnp.int32, (half, members), 0)
    pair_col = lax.broadcasted_iota(jnp.int32, (half, members), 1)
    take_even = (pair_col == 2 * pair_row).astype(jnp.float32)
    take_odd = (pair_col == 2 * pair_row + 1).astype(jnp.float32)
    spread_row = lax.broadcasted_iota(jnp.int32, (members, half), 0)
    spread_col = lax.broadcasted_iota(jnp.int32, (members, half), 1)
    put_even = (spread_row == 2 * spread_col).astype(jnp.float32)
    put_odd = (spread_row == 2 * spread_col + 1).astype(jnp.float32)
    first_row = lax.broadcasted_iota(jnp.int32, (8, slot_count), 0) == 0
    carried[...] = identity
    rows_t[...] = jnp.zeros(rows_t.shape, jnp.float32)
    rows_u[...] = jnp.zeros(rows_u.shape, jnp.float32)

    def batch_step(b, _):
        par = b % 2
        sampled = mm(carried[...], y_ref[b])
        prior_mean = jnp.mean(sampled, axis=0, keepdims=True)
        scale = scale_ref[b]
        scaled_rows = scale * (sampled - prior_mean)
        innovation = scale * (obs_ref[b] - prior_mean)
        rows_t[0:members, :] = scaled_rows
        rows_u[members : 2 * members, :] = scaled_rows
        lead = mm_nt(mm(take_even, scaled_rows), rows_t[...]) + mm_nt(mm(take_odd, scaled_rows), rows_u[...])
        tail = mm_nt(jnp.where(first_row, innovation, 0.0), rows_t[...])
        payload[par, 0:half, :] = lead
        payload[par, half : half + 8, :] = tail

        copies = []
        for k, (dx, dy) in enumerate(OFFSETS):
            if dx == 0 and dy == 0:
                continue
            copy = pltpu.make_async_remote_copy(
                src_ref=payload.at[par],
                dst_ref=slots.at[par, k],
                send_sem=send_sem.at[par, k],
                recv_sem=recv_sem.at[par, k],
                device_id=(me_x - dx, me_y - dy),
                device_id_type=pl.DeviceIdType.MESH,
            )
            ok = inside(me_x - dx, me_y - dy)

            @pl.when(ok)
            def _():
                copy.start()

            copies.append((k, dx, dy, copy, ok))

        total[...] = jnp.zeros(total.shape, jnp.float32)
        for k, (dx, dy) in enumerate(OFFSETS):
            if dx == 0 and dy == 0:
                total[...] += w_ref[k] * payload[par]
        for k, dx, dy, copy, ok in copies:
            @pl.when(ok)
            def _():
                copy.wait_send()

            arrives = inside(me_x + dx, me_y + dy)

            @pl.when(arrives)
            def _():
                copy.wait_recv()
                total[...] += w_ref[k] * slots[par, k]

        summed = total[...]
        packed = summed[0:half, :]
        gram_total = mm(put_even, packed[:, 0:members]) + mm(put_odd, packed[:, members : 2 * members])
        proj_rows = summed[half : half + 8, 0:members]
        precision_matrix = identity + gram_total / (members - 1)
        squares = precision_matrix * precision_matrix
        frobenius = jnp.sqrt(jnp.sum(jnp.sum(squares, axis=1, keepdims=True), axis=0, keepdims=True))
        iterate = precision_matrix / frobenius

        def ns_step(_, pair):
            iterate, inverse = pair
            factor = 1.5 * identity - 0.5 * mm(inverse, iterate)
            both = mm(jnp.concatenate([iterate, inverse], axis=0), factor)
            return both[0:members], both[members : 2 * members]

        pair = (iterate, identity)
        for _i in range(NS_STEPS):
            pair = ns_step(_i, pair)
        iterate, inverse = pair
        transform = inverse / jnp.sqrt(frobenius)
        weights = mm_nt(mm_nt(proj_rows, transform), transform) / (members - 1)
        mixing_t = mm_nt(identity, transform) + weights[0:1, :]
        step = 1.0 / members + mixing_t - jnp.mean(mixing_t, axis=1, keepdims=True)
        carried[...] = mm(step, carried[...])
        return 0

    lax.fori_loop(0, batches, batch_step, 0)
    out_ref[...] = carried[...]


def run_analysis(y, scale, obs, weights, nx, ny):
    batches, members, slot_count = y.shape
    count = len(OFFSETS)
    wide = 2 * members
    packed_rows = members // 2 + 8
    return pl.pallas_call(
        functools.partial(analysis_kernel, nx, ny),
        out_shape=jax.ShapeDtypeStruct((members, members), jnp.float32),
        in_specs=[
            pl.BlockSpec(memory_space=pltpu.VMEM),
            pl.BlockSpec(memory_space=pltpu.VMEM),
            pl.BlockSpec(memory_space=pltpu.VMEM),
            pl.BlockSpec(memory_space=pltpu.SMEM),
        ],
        out_specs=pl.BlockSpec(memory_space=pltpu.VMEM),
        scratch_shapes=[
            pltpu.VMEM((2, count, packed_rows, wide), jnp.float32),
            pltpu.VMEM((2, packed_rows, wide), jnp.float32),
            pltpu.VMEM((wide, slot_count), jnp.float32),
            pltpu.VMEM((wide, slot_count), jnp.float32),
            pltpu.VMEM((packed_rows, wide), jnp.float32),
            pltpu.VMEM((members, members), jnp.float32),
            pltpu.SemaphoreType.DMA((2, count)),
            pltpu.SemaphoreType.DMA((2, count)),
        ],
        compiler_params=pltpu.CompilerParams(collective_id=0, has_side_effects=True),
    )(y, scale, obs, weights)


def transform_kernel(p_ref, x_ref, o_ref):
    rows = x_ref.shape[3]
    mix = p_ref[...]
    for i in range(rows):
        o_ref[:, 0, 0, i, :] = jnp.dot(mix, x_ref[:, 0, 0, i, :],
                                       precision=lax.Precision.HIGH, preferred_element_type=jnp.float32)


def apply_transform(carried, cells):
    members, levels, fields, rows, lanes = cells.shape
    block = pl.BlockSpec((members, 1, 1, rows, lanes), lambda a, b: (0, a, b, 0, 0))
    return pl.pallas_call(
        transform_kernel,
        out_shape=jax.ShapeDtypeStruct(cells.shape, cells.dtype),
        grid=(levels, fields),
        in_specs=[pl.BlockSpec((members, members), lambda a, b: (0, 0)), block],
        out_specs=block,
    )(carried, cells)


def on_device(
    background_sample,
    courant_eastward,
    courant_northward,
    diffusivity,
    sample_site,
    live_count,
    observed,
    error_variance,
    reach_mask,
):
    nx = lax.axis_size("gx")
    ny = lax.axis_size("gy")
    site_table = sample_site[0, 0]
    forecast, gathered = forecast_step(
        background_sample, courant_eastward, courant_northward, diffusivity, site_table.reshape(-1)
    )
    members = forecast.shape[0]
    counts = live_count[0, 0]
    observed_here = observed[0, 0]
    variance_here = error_variance[0, 0]
    batches, slot_count = site_table.shape
    slot_index = jnp.arange(slot_count)
    mask_index = jnp.arange(WIDTH)
    centre_one = ((mask_index[:, None] == RAD) & (mask_index[None, :] == RAD)).astype(jnp.float32)
    reach_weight = jnp.maximum(reach_mask[0, 0].astype(jnp.float32), centre_one).reshape(-1)
    all_sampled = gathered.reshape(members, batches, slot_count)
    y = jnp.transpose(all_sampled, (1, 0, 2))
    live_slot = (slot_index[None, :] < counts[:, None]).astype(jnp.float32)
    scale = (live_slot * (1.0 / jnp.sqrt(variance_here)))[:, None, :]
    carried = run_analysis(y, scale, observed_here[:, None, :], reach_weight, nx, ny)
    return apply_transform(carried, forecast)


def solution(mesh):
    in_specs = (
        P(None, None, None, "gx", "gy"),
        P(None, "gx", "gy"),
        P(None, "gx", "gy"),
        P("gx", "gy"),
        P("gx", "gy", None, None),
        P("gx", "gy", None),
        P("gx", "gy", None, None),
        P("gx", "gy", None, None),
        P("gx", "gy", None, None),
    )
    out_specs = P(None, None, None, "gx", "gy")
    return jax.shard_map(
        on_device, mesh=mesh, in_specs=in_specs, out_specs=out_specs, check_vma=False
    )
```

```python
import functools

import jax
import jax.numpy as jnp
from jax import lax
from jax.experimental import pallas as pl
from jax.experimental.pallas import tpu as pltpu
from jax.sharding import PartitionSpec as P

BATCHES = 4
RAD = 2
NS_STEPS = 6
WIDTH = 2 * RAD + 1
OFFSETS = [(dx, dy) for dx in range(-RAD, RAD + 1) for dy in range(-RAD, RAD + 1)]


def matmul_full(left, right):
    return jnp.dot(left, right, precision=lax.Precision.HIGHEST, preferred_element_type=jnp.float32)


def mixing_matrix(gram_matrix, projection):
    realisation_vectors = gram_matrix.shape[0]
    identity = jnp.eye(realisation_vectors, dtype=jnp.float32)
    precision_matrix = identity + gram_matrix / (realisation_vectors - 1)
    frobenius = jnp.sqrt(jnp.sum(precision_matrix * precision_matrix))
    iterate = precision_matrix / frobenius
    inverse = identity
    for repeat in range(NS_STEPS):
        factor = 1.5 * identity - 0.5 * matmul_full(inverse, iterate)
        iterate = matmul_full(iterate, factor)
        inverse = matmul_full(factor, inverse)
    transform = inverse / jnp.sqrt(frobenius)
    weights = matmul_full(transform, matmul_full(transform, projection)) / (realisation_vectors - 1)
    return transform + weights[:, None]


def stencil_kernel(x_ref, east_ref, west_ref, edge_ref, u_ref, v_ref, d_ref, col_ref, row_ref, o_ref, s_ref, east_scr, west_scr):
    rows = x_ref.shape[3]
    lanes = x_ref.shape[4]
    east_scr[:, :, :, 0 : rows - 1, :] = x_ref[:, :, :, 1:rows, :]
    east_scr[:, :, :, rows - 1 : rows, :] = east_ref[...]
    west_scr[:, :, :, 1:rows, :] = x_ref[:, :, :, 0 : rows - 1, :]
    west_scr[:, :, :, 0:1, :] = west_ref[...]
    centre = x_ref[...]
    east_cell = east_scr[...]
    west_cell = west_scr[...]
    sides = edge_ref[...]
    count = centre.size // lanes
    spread = (
        lax.broadcasted_iota(jnp.int32, (count, sides.shape[1]), 0) // rows
        == lax.broadcasted_iota(jnp.int32, (count, sides.shape[1]), 1)
    ).astype(jnp.float32)
    own = (
        lax.broadcasted_iota(jnp.int32, (count, lanes), 0) % rows
        == lax.broadcasted_iota(jnp.int32, (count, lanes), 1)
    )

    def expand(side):
        column = jnp.sum(jnp.where(own, mm(spread, side), 0.0), axis=1, keepdims=True)
        return jnp.broadcast_to(column, (count, lanes)).reshape(centre.shape)

    lane = lax.broadcasted_iota(jnp.int32, centre.shape, 4)
    north_cell = jnp.where(lane == lanes - 1, expand(sides[0]), pltpu.roll(centre, lanes - 1, 4))
    south_cell = jnp.where(lane == 0, expand(sides[1]), pltpu.roll(centre, 1, 4))
    u = u_ref[...][None, :, None]
    v = v_ref[...][None, :, None]
    d = d_ref[...][None, None, None]
    flux_x = jnp.maximum(u, 0.0) * (centre - west_cell) + jnp.minimum(u, 0.0) * (east_cell - centre)
    flux_y = jnp.maximum(v, 0.0) * (centre - south_cell) + jnp.minimum(v, 0.0) * (north_cell - centre)
    spread_term = d * (east_cell + west_cell + north_cell + south_cell - 4.0 * centre)
    result = centre + spread_term - flux_x - flux_y
    o_ref[...] = result
    block, rows_all = result.shape[0], result.shape[1] * result.shape[2] * rows
    flat = result.reshape(block * rows_all, lanes)
    high = flat.astype(jnp.bfloat16)
    rest = flat - high.astype(jnp.float32)
    mid = rest.astype(jnp.bfloat16)
    low = (rest - mid.astype(jnp.float32)).astype(jnp.bfloat16)
    pick = col_ref[...]
    picked = jnp.dot(high, pick, preferred_element_type=jnp.float32)
    picked = picked + jnp.dot(mid, pick, preferred_element_type=jnp.float32)
    picked = picked + jnp.dot(low, pick, preferred_element_type=jnp.float32)
    picked = picked.reshape(block, rows_all, picked.shape[-1]) * row_ref[...][None]
    s_ref[...] = jnp.sum(picked, axis=1)


def forecast_step(cells, courant_eastward, courant_northward, diffusivity, sites):
    nx = lax.axis_size("gx")
    ny = lax.axis_size("gy")
    rows, lanes = cells.shape[3], cells.shape[4]
    east_halo = lax.ppermute(cells[:, :, :, 0:1, :], "gx", [(i + 1, i) for i in range(nx - 1)])
    west_halo = lax.ppermute(cells[:, :, :, rows - 1 : rows, :], "gx", [(i, i + 1) for i in range(nx - 1)])
    lane_index = jnp.arange(lanes)
    pick = jnp.stack([lane_index == 0, lane_index == lanes - 1]).astype(jnp.float32)
    sides = jnp.einsum(
        "abcil,sl->sabci",
        cells, pick, precision=lax.Precision.HIGHEST, preferred_element_type=jnp.float32,
    )
    north_halo = lax.ppermute(sides[0], "gy", [(i + 1, i) for i in range(ny - 1)])
    south_halo = lax.ppermute(sides[1], "gy", [(i, i + 1) for i in range(ny - 1)])
    flat_halo = jnp.stack([north_halo, south_halo]).reshape(2, -1, rows)
    edge = jnp.pad(flat_halo, ((0, 0), (0, 0), (0, lanes - rows)))
    block = 8
    members = cells.shape[0]
    big = pl.BlockSpec((block,) + cells.shape[1:], lambda i: (i, 0, 0, 0, 0))
    thin = pl.BlockSpec((block,) + cells.shape[1:3] + (1, lanes), lambda i: (i, 0, 0, 0, 0))
    whole3 = pl.BlockSpec(courant_eastward.shape, lambda i: (0, 0, 0))
    whole2 = pl.BlockSpec(diffusivity.shape, lambda i: (0, 0))
    site_count = sites.shape[0]
    rows_all = cells.shape[1] * cells.shape[2] * rows
    col_pick = (sites[None, :] % lanes == jnp.arange(lanes)[:, None]).astype(jnp.bfloat16)
    row_pick = (sites[None, :] // lanes == jnp.arange(rows_all)[:, None]).astype(jnp.float32)
    picks = pl.BlockSpec((lanes, site_count), lambda i: (0, 0))
    return pl.pallas_call(
        stencil_kernel,
        out_shape=(
            jax.ShapeDtypeStruct(cells.shape, cells.dtype),
            jax.ShapeDtypeStruct((members, site_count), cells.dtype),
        ),
        grid=(members // block,),
        in_specs=[big, thin, thin, pl.BlockSpec((2, block * cells.shape[1] * cells.shape[2], lanes), lambda i: (0, i, 0)), whole3, whole3, whole2, picks,
                  pl.BlockSpec((rows_all, site_count), lambda i: (0, 0))],
        out_specs=(big, pl.BlockSpec((block, site_count), lambda i: (i, 0))),
        scratch_shapes=[
            pltpu.VMEM((block,) + cells.shape[1:], cells.dtype),
            pltpu.VMEM((block,) + cells.shape[1:], cells.dtype),
        ],
    )(cells, east_halo, west_halo, edge, courant_eastward, courant_northward, diffusivity, col_pick, row_pick)


def mm(left, right):
    return jnp.dot(left, right, precision=lax.Precision.HIGHEST, preferred_element_type=jnp.float32)


def mm_nt(left, right):
    return lax.dot_general(
        left, right, (((1,), (1,)), ((), ())),
        precision=lax.Precision.HIGHEST, preferred_element_type=jnp.float32,
    )


def analysis_kernel(
    nx, ny, y_ref, scale_ref, obs_ref, w_ref, out_ref,
    slots, payload, rows_t, rows_u, total, carried, send_sem, recv_sem,
):
    me_x = lax.axis_index("gx")
    me_y = lax.axis_index("gy")
    members = y_ref.shape[1]
    slot_count = y_ref.shape[2]
    wide = payload.shape[2]
    batches = y_ref.shape[0]
    centre_k = RAD * WIDTH + RAD

    def inside(x, y):
        return (x >= 0) & (x < nx) & (y >= 0) & (y < ny)

    barrier = pltpu.get_barrier_semaphore()
    partners = jnp.int32(0)
    for dx, dy in OFFSETS:
        if dx == 0 and dy == 0:
            continue
        ok = inside(me_x - dx, me_y - dy)
        partners = partners + ok.astype(jnp.int32)

        @pl.when(ok)
        def _():
            pl.semaphore_signal(
                barrier, inc=1, device_id=(me_x - dx, me_y - dy),
                device_id_type=pl.DeviceIdType.MESH,
            )

    pl.semaphore_wait(barrier, partners)

    half = members // 2
    row = lax.broadcasted_iota(jnp.int32, (members, members), 0)
    col = lax.broadcasted_iota(jnp.int32, (members, members), 1)
    identity = (row == col).astype(jnp.float32)
    pair_row = lax.broadcasted_iota(jnp.int32, (half, members), 0)
    pair_col = lax.broadcasted_iota(jnp.int32, (half, members), 1)
    take_even = (pair_col == 2 * pair_row).astype(jnp.float32)
    take_odd = (pair_col == 2 * pair_row + 1).astype(jnp.float32)
    spread_row = lax.broadcasted_iota(jnp.int32, (members, half), 0)
    spread_col = lax.broadcasted_iota(jnp.int32, (members, half), 1)
    put_even = (spread_row == 2 * spread_col).astype(jnp.float32)
    put_odd = (spread_row == 2 * spread_col + 1).astype(jnp.float32)
    first_row = lax.broadcasted_iota(jnp.int32, (8, slot_count), 0) == 0
    carried[...] = identity
    rows_t[...] = jnp.zeros(rows_t.shape, jnp.float32)
    rows_u[...] = jnp.zeros(rows_u.shape, jnp.float32)

    def batch_step(b, _):
        par = b % 2
        sampled = mm(carried[...], y_ref[b])
        prior_mean = jnp.mean(sampled, axis=0, keepdims=True)
        scale = scale_ref[b]
        scaled_rows = scale * (sampled - prior_mean)
        innovation = scale * (obs_ref[b] - prior_mean)
        rows_t[0:members, :] = scaled_rows
        rows_u[members : 2 * members, :] = scaled_rows
        lead = mm_nt(mm(take_even, scaled_rows), rows_t[...]) + mm_nt(mm(take_odd, scaled_rows), rows_u[...])
        tail = mm_nt(jnp.where(first_row, innovation, 0.0), rows_t[...])
        payload[par, 0:half, :] = lead
        payload[par, half : half + 8, :] = tail

        copies = []
        for k, (dx, dy) in enumerate(OFFSETS):
            if dx == 0 and dy == 0:
                continue
            copy = pltpu.make_async_remote_copy(
                src_ref=payload.at[par],
                dst_ref=slots.at[par, k],
                send_sem=send_sem.at[par, k],
                recv_sem=recv_sem.at[par, k],
                device_id=(me_x - dx, me_y - dy),
                device_id_type=pl.DeviceIdType.MESH,
            )
            ok = inside(me_x - dx, me_y - dy)

            @pl.when(ok)
            def _():
                copy.start()

            copies.append((k, dx, dy, copy, ok))

        total[...] = jnp.zeros(total.shape, jnp.float32)
        for k, (dx, dy) in enumerate(OFFSETS):
            if dx == 0 and dy == 0:
                total[...] += w_ref[k] * payload[par]
        for k, dx, dy, copy, ok in copies:
            @pl.when(ok)
            def _():
                copy.wait_send()

            arrives = inside(me_x + dx, me_y + dy)

            @pl.when(arrives)
            def _():
                copy.wait_recv()
                total[...] += w_ref[k] * slots[par, k]

        summed = total[...]
        packed = summed[0:half, :]
        gram_total = mm(put_even, packed[:, 0:members]) + mm(put_odd, packed[:, members : 2 * members])
        proj_rows = summed[half : half + 8, 0:members]
        precision_matrix = identity + gram_total / (members - 1)
        squares = precision_matrix * precision_matrix
        frobenius = jnp.sqrt(jnp.sum(jnp.sum(squares, axis=1, keepdims=True), axis=0, keepdims=True))
        iterate = precision_matrix / frobenius

        def ns_step(_, pair):
            iterate, inverse = pair
            factor = 1.5 * identity - 0.5 * mm(inverse, iterate)
            both = mm(jnp.concatenate([iterate, inverse], axis=0), factor)
            return both[0:members], both[members : 2 * members]

        pair = (iterate, identity)
        for _i in range(NS_STEPS):
            pair = ns_step(_i, pair)
        iterate, inverse = pair
        transform = inverse / jnp.sqrt(frobenius)
        weights = mm_nt(mm_nt(proj_rows, transform), transform) / (members - 1)
        mixing_t = mm_nt(identity, transform) + weights[0:1, :]
        step = 1.0 / members + mixing_t - jnp.mean(mixing_t, axis=1, keepdims=True)
        carried[...] = mm(step, carried[...])
        return 0

    lax.fori_loop(0, batches, batch_step, 0)
    out_ref[...] = carried[...]


def run_analysis(y, scale, obs, weights, nx, ny):
    batches, members, slot_count = y.shape
    count = len(OFFSETS)
    wide = 2 * members
    packed_rows = members // 2 + 8
    return pl.pallas_call(
        functools.partial(analysis_kernel, nx, ny),
        out_shape=jax.ShapeDtypeStruct((members, members), jnp.float32),
        in_specs=[
            pl.BlockSpec(memory_space=pltpu.VMEM),
            pl.BlockSpec(memory_space=pltpu.VMEM),
            pl.BlockSpec(memory_space=pltpu.VMEM),
            pl.BlockSpec(memory_space=pltpu.SMEM),
        ],
        out_specs=pl.BlockSpec(memory_space=pltpu.VMEM),
        scratch_shapes=[
            pltpu.VMEM((2, count, packed_rows, wide), jnp.float32),
            pltpu.VMEM((2, packed_rows, wide), jnp.float32),
            pltpu.VMEM((wide, slot_count), jnp.float32),
            pltpu.VMEM((wide, slot_count), jnp.float32),
            pltpu.VMEM((packed_rows, wide), jnp.float32),
            pltpu.VMEM((members, members), jnp.float32),
            pltpu.SemaphoreType.DMA((2, count)),
            pltpu.SemaphoreType.DMA((2, count)),
        ],
        compiler_params=pltpu.CompilerParams(collective_id=0, has_side_effects=True),
    )(y, scale, obs, weights)


def transform_kernel(p_ref, x_ref, o_ref):
    rows = x_ref.shape[3]
    mix = p_ref[...]
    for i in range(rows):
        o_ref[:, 0, 0, i, :] = jnp.dot(mix, x_ref[:, 0, 0, i, :],
                                       precision=lax.Precision.HIGH, preferred_element_type=jnp.float32)


def apply_transform(carried, cells):
    members, levels, fields, rows, lanes = cells.shape
    block = pl.BlockSpec((members, 1, 1, rows, lanes), lambda a, b: (0, a, b, 0, 0))
    return pl.pallas_call(
        transform_kernel,
        out_shape=jax.ShapeDtypeStruct(cells.shape, cells.dtype),
        grid=(levels, fields),
        in_specs=[pl.BlockSpec((members, members), lambda a, b: (0, 0)), block],
        out_specs=block,
    )(carried, cells)


def on_device(
    background_sample,
    courant_eastward,
    courant_northward,
    diffusivity,
    sample_site,
    live_count,
    observed,
    error_variance,
    reach_mask,
):
    nx = lax.axis_size("gx")
    ny = lax.axis_size("gy")
    site_table = sample_site[0, 0]
    forecast, gathered = forecast_step(
        background_sample, courant_eastward, courant_northward, diffusivity, site_table.reshape(-1)
    )
    members = forecast.shape[0]
    counts = live_count[0, 0]
    observed_here = observed[0, 0]
    variance_here = error_variance[0, 0]
    batches, slot_count = site_table.shape
    slot_index = jnp.arange(slot_count)
    mask_index = jnp.arange(WIDTH)
    centre_one = ((mask_index[:, None] == RAD) & (mask_index[None, :] == RAD)).astype(jnp.float32)
    reach_weight = jnp.maximum(reach_mask[0, 0].astype(jnp.float32), centre_one).reshape(-1)
    all_sampled = gathered.reshape(members, batches, slot_count)
    y = jnp.transpose(all_sampled, (1, 0, 2))
    live_slot = (slot_index[None, :] < counts[:, None]).astype(jnp.float32)
    scale = (live_slot * (1.0 / jnp.sqrt(variance_here)))[:, None, :]
    carried = run_analysis(y, scale, observed_here[:, None, :], reach_weight, nx, ny)
    return apply_transform(carried, forecast)


def solution(mesh):
    in_specs = (
        P(None, None, None, "gx", "gy"),
        P(None, "gx", "gy"),
        P(None, "gx", "gy"),
        P("gx", "gy"),
        P("gx", "gy", None, None),
        P("gx", "gy", None),
        P("gx", "gy", None, None),
        P("gx", "gy", None, None),
        P("gx", "gy", None, None),
    )
    out_specs = P(None, None, None, "gx", "gy")
    return jax.shard_map(
        on_device, mesh=mesh, in_specs=in_specs, out_specs=out_specs, check_vma=False
    )
```

```python
import functools

import jax
import jax.numpy as jnp
from jax import lax
from jax.experimental import pallas as pl
from jax.experimental.pallas import tpu as pltpu
from jax.sharding import PartitionSpec as P

BATCHES = 4
RAD = 2
NS_STEPS = 6
WIDTH = 2 * RAD + 1
OFFSETS = [(dx, dy) for dx in range(-RAD, RAD + 1) for dy in range(-RAD, RAD + 1)]


def matmul_full(left, right):
    return jnp.dot(left, right, precision=lax.Precision.HIGHEST, preferred_element_type=jnp.float32)


def mixing_matrix(gram_matrix, projection):
    realisation_vectors = gram_matrix.shape[0]
    identity = jnp.eye(realisation_vectors, dtype=jnp.float32)
    precision_matrix = identity + gram_matrix / (realisation_vectors - 1)
    frobenius = jnp.sqrt(jnp.sum(precision_matrix * precision_matrix))
    iterate = precision_matrix / frobenius
    inverse = identity
    for repeat in range(NS_STEPS):
        factor = 1.5 * identity - 0.5 * matmul_full(inverse, iterate)
        iterate = matmul_full(iterate, factor)
        inverse = matmul_full(factor, inverse)
    transform = inverse / jnp.sqrt(frobenius)
    weights = matmul_full(transform, matmul_full(transform, projection)) / (realisation_vectors - 1)
    return transform + weights[:, None]


def stencil_kernel(x_ref, east_ref, west_ref, edge_ref, u_ref, v_ref, d_ref, col_ref, row_ref, o_ref, s_ref, east_scr, west_scr):
    rows = x_ref.shape[3]
    lanes = x_ref.shape[4]
    east_scr[:, :, :, 0 : rows - 1, :] = x_ref[:, :, :, 1:rows, :]
    east_scr[:, :, :, rows - 1 : rows, :] = east_ref[...]
    west_scr[:, :, :, 1:rows, :] = x_ref[:, :, :, 0 : rows - 1, :]
    west_scr[:, :, :, 0:1, :] = west_ref[...]
    centre = x_ref[...]
    east_cell = east_scr[...]
    west_cell = west_scr[...]
    edge = edge_ref[...]
    lane = lax.broadcasted_iota(jnp.int32, centre.shape, 4)
    north_cell = jnp.where(lane == lanes - 1, edge, pltpu.roll(centre, lanes - 1, 4))
    south_cell = jnp.where(lane == 0, edge, pltpu.roll(centre, 1, 4))
    u = u_ref[...][None, :, None]
    v = v_ref[...][None, :, None]
    d = d_ref[...][None, None, None]
    flux_x = jnp.maximum(u, 0.0) * (centre - west_cell) + jnp.minimum(u, 0.0) * (east_cell - centre)
    flux_y = jnp.maximum(v, 0.0) * (centre - south_cell) + jnp.minimum(v, 0.0) * (north_cell - centre)
    spread_term = d * (east_cell + west_cell + north_cell + south_cell - 4.0 * centre)
    result = centre + spread_term - flux_x - flux_y
    o_ref[...] = result
    block, rows_all = result.shape[0], result.shape[1] * result.shape[2] * rows
    flat = result.reshape(block * rows_all, lanes)
    high = flat.astype(jnp.bfloat16)
    rest = flat - high.astype(jnp.float32)
    mid = rest.astype(jnp.bfloat16)
    low = (rest - mid.astype(jnp.float32)).astype(jnp.bfloat16)
    pick = col_ref[...]
    picked = jnp.dot(high, pick, preferred_element_type=jnp.float32)
    picked = picked + jnp.dot(mid, pick, preferred_element_type=jnp.float32)
    picked = picked + jnp.dot(low, pick, preferred_element_type=jnp.float32)
    picked = picked.reshape(block, rows_all, picked.shape[-1]) * row_ref[...][None]
    s_ref[...] = jnp.sum(picked, axis=1)


def forecast_step(cells, courant_eastward, courant_northward, diffusivity, sites):
    nx = lax.axis_size("gx")
    ny = lax.axis_size("gy")
    rows, lanes = cells.shape[3], cells.shape[4]
    east_halo = lax.ppermute(cells[:, :, :, 0:1, :], "gx", [(i + 1, i) for i in range(nx - 1)])
    west_halo = lax.ppermute(cells[:, :, :, rows - 1 : rows, :], "gx", [(i, i + 1) for i in range(nx - 1)])
    lane_index = jnp.arange(lanes)
    pick = jnp.stack([lane_index == 0, lane_index == lanes - 1]).astype(jnp.float32)
    place = jnp.stack([lane_index == lanes - 1, lane_index == 0]).astype(jnp.float32)
    sides = jnp.einsum(
        "abcil,sl->sabci",
        cells, pick, precision=lax.Precision.HIGHEST, preferred_element_type=jnp.float32,
    )
    north_halo = lax.ppermute(sides[0], "gy", [(i + 1, i) for i in range(ny - 1)])
    south_halo = lax.ppermute(sides[1], "gy", [(i, i + 1) for i in range(ny - 1)])
    edge = jnp.einsum(
        "sabci,sl->abcil", jnp.stack([north_halo, south_halo]), place,
        precision=lax.Precision.HIGHEST, preferred_element_type=jnp.float32,
    )
    block = 16
    members = cells.shape[0]
    big = pl.BlockSpec((block,) + cells.shape[1:], lambda i: (i, 0, 0, 0, 0))
    thin = pl.BlockSpec((block,) + cells.shape[1:3] + (1, lanes), lambda i: (i, 0, 0, 0, 0))
    whole3 = pl.BlockSpec(courant_eastward.shape, lambda i: (0, 0, 0))
    whole2 = pl.BlockSpec(diffusivity.shape, lambda i: (0, 0))
    site_count = sites.shape[0]
    rows_all = cells.shape[1] * cells.shape[2] * rows
    col_pick = (sites[None, :] % lanes == jnp.arange(lanes)[:, None]).astype(jnp.bfloat16)
    row_pick = (sites[None, :] // lanes == jnp.arange(rows_all)[:, None]).astype(jnp.float32)
    picks = pl.BlockSpec((lanes, site_count), lambda i: (0, 0))
    return pl.pallas_call(
        stencil_kernel,
        out_shape=(
            jax.ShapeDtypeStruct(cells.shape, cells.dtype),
            jax.ShapeDtypeStruct((members, site_count), cells.dtype),
        ),
        grid=(members // block,),
        in_specs=[big, thin, thin, big, whole3, whole3, whole2, picks,
                  pl.BlockSpec((rows_all, site_count), lambda i: (0, 0))],
        out_specs=(big, pl.BlockSpec((block, site_count), lambda i: (i, 0))),
        scratch_shapes=[
            pltpu.VMEM((block,) + cells.shape[1:], cells.dtype),
            pltpu.VMEM((block,) + cells.shape[1:], cells.dtype),
        ],
    )(cells, east_halo, west_halo, edge, courant_eastward, courant_northward, diffusivity, col_pick, row_pick)


def mm(left, right):
    return jnp.dot(left, right, precision=lax.Precision.HIGHEST, preferred_element_type=jnp.float32)


def mm_nt(left, right):
    return lax.dot_general(
        left, right, (((1,), (1,)), ((), ())),
        precision=lax.Precision.HIGHEST, preferred_element_type=jnp.float32,
    )


def analysis_kernel(
    nx, ny, y_ref, scale_ref, obs_ref, w_ref, out_ref,
    slots, payload, rows_t, rows_u, total, carried, send_sem, recv_sem,
):
    me_x = lax.axis_index("gx")
    me_y = lax.axis_index("gy")
    members = y_ref.shape[1]
    slot_count = y_ref.shape[2]
    wide = payload.shape[2]
    batches = y_ref.shape[0]
    centre_k = RAD * WIDTH + RAD

    def inside(x, y):
        return (x >= 0) & (x < nx) & (y >= 0) & (y < ny)

    barrier = pltpu.get_barrier_semaphore()
    partners = jnp.int32(0)
    for dx, dy in OFFSETS:
        if dx == 0 and dy == 0:
            continue
        ok = inside(me_x - dx, me_y - dy)
        partners = partners + ok.astype(jnp.int32)

        @pl.when(ok)
        def _():
            pl.semaphore_signal(
                barrier, inc=1, device_id=(me_x - dx, me_y - dy),
                device_id_type=pl.DeviceIdType.MESH,
            )

    pl.semaphore_wait(barrier, partners)

    half = members // 2
    row = lax.broadcasted_iota(jnp.int32, (members, members), 0)
    col = lax.broadcasted_iota(jnp.int32, (members, members), 1)
    identity = (row == col).astype(jnp.float32)
    pair_row = lax.broadcasted_iota(jnp.int32, (half, members), 0)
    pair_col = lax.broadcasted_iota(jnp.int32, (half, members), 1)
    take_even = (pair_col == 2 * pair_row).astype(jnp.float32)
    take_odd = (pair_col == 2 * pair_row + 1).astype(jnp.float32)
    spread_row = lax.broadcasted_iota(jnp.int32, (members, half), 0)
    spread_col = lax.broadcasted_iota(jnp.int32, (members, half), 1)
    put_even = (spread_row == 2 * spread_col).astype(jnp.float32)
    put_odd = (spread_row == 2 * spread_col + 1).astype(jnp.float32)
    first_row = lax.broadcasted_iota(jnp.int32, (8, slot_count), 0) == 0
    carried[...] = identity
    rows_t[...] = jnp.zeros(rows_t.shape, jnp.float32)
    rows_u[...] = jnp.zeros(rows_u.shape, jnp.float32)

    def batch_step(b, _):
        par = b % 2
        sampled = mm(carried[...], y_ref[b])
        prior_mean = jnp.mean(sampled, axis=0, keepdims=True)
        scale = scale_ref[b]
        scaled_rows = scale * (sampled - prior_mean)
        innovation = scale * (obs_ref[b] - prior_mean)
        rows_t[0:members, :] = scaled_rows
        rows_u[members : 2 * members, :] = scaled_rows
        lead = mm_nt(mm(take_even, scaled_rows), rows_t[...]) + mm_nt(mm(take_odd, scaled_rows), rows_u[...])
        tail = mm_nt(jnp.where(first_row, innovation, 0.0), rows_t[...])
        payload[par, 0:half, :] = lead
        payload[par, half : half + 8, :] = tail

        copies = []
        for k, (dx, dy) in enumerate(OFFSETS):
            if dx == 0 and dy == 0:
                continue
            copy = pltpu.make_async_remote_copy(
                src_ref=payload.at[par],
                dst_ref=slots.at[par, k],
                send_sem=send_sem.at[par, k],
                recv_sem=recv_sem.at[par, k],
                device_id=(me_x - dx, me_y - dy),
                device_id_type=pl.DeviceIdType.MESH,
            )
            ok = inside(me_x - dx, me_y - dy)

            @pl.when(ok)
            def _():
                copy.start()

            copies.append((k, dx, dy, copy, ok))

        total[...] = jnp.zeros(total.shape, jnp.float32)
        for k, (dx, dy) in enumerate(OFFSETS):
            if dx == 0 and dy == 0:
                total[...] += w_ref[k] * payload[par]
        for k, dx, dy, copy, ok in copies:
            @pl.when(ok)
            def _():
                copy.wait_send()

            arrives = inside(me_x + dx, me_y + dy)

            @pl.when(arrives)
            def _():
                copy.wait_recv()
                total[...] += w_ref[k] * slots[par, k]

        summed = total[...]
        packed = summed[0:half, :]
        gram_total = mm(put_even, packed[:, 0:members]) + mm(put_odd, packed[:, members : 2 * members])
        proj_rows = summed[half : half + 8, 0:members]
        precision_matrix = identity + gram_total / (members - 1)
        squares = precision_matrix * precision_matrix
        frobenius = jnp.sqrt(jnp.sum(jnp.sum(squares, axis=1, keepdims=True), axis=0, keepdims=True))
        iterate = precision_matrix / frobenius

        def ns_step(_, pair):
            iterate, inverse = pair
            factor = 1.5 * identity - 0.5 * mm(inverse, iterate)
            both = mm(jnp.concatenate([iterate, inverse], axis=0), factor)
            return both[0:members], both[members : 2 * members]

        pair = (iterate, identity)
        for _i in range(NS_STEPS):
            pair = ns_step(_i, pair)
        iterate, inverse = pair
        transform = inverse / jnp.sqrt(frobenius)
        weights = mm_nt(mm_nt(proj_rows, transform), transform) / (members - 1)
        mixing_t = mm_nt(identity, transform) + weights[0:1, :]
        step = 1.0 / members + mixing_t - jnp.mean(mixing_t, axis=1, keepdims=True)
        carried[...] = mm(step, carried[...])
        return 0

    lax.fori_loop(0, batches, batch_step, 0)
    out_ref[...] = carried[...]


def run_analysis(y, scale, obs, weights, nx, ny):
    batches, members, slot_count = y.shape
    count = len(OFFSETS)
    wide = 2 * members
    packed_rows = members // 2 + 8
    return pl.pallas_call(
        functools.partial(analysis_kernel, nx, ny),
        out_shape=jax.ShapeDtypeStruct((members, members), jnp.float32),
        in_specs=[
            pl.BlockSpec(memory_space=pltpu.VMEM),
            pl.BlockSpec(memory_space=pltpu.VMEM),
            pl.BlockSpec(memory_space=pltpu.VMEM),
            pl.BlockSpec(memory_space=pltpu.SMEM),
        ],
        out_specs=pl.BlockSpec(memory_space=pltpu.VMEM),
        scratch_shapes=[
            pltpu.VMEM((2, count, packed_rows, wide), jnp.float32),
            pltpu.VMEM((2, packed_rows, wide), jnp.float32),
            pltpu.VMEM((wide, slot_count), jnp.float32),
            pltpu.VMEM((wide, slot_count), jnp.float32),
            pltpu.VMEM((packed_rows, wide), jnp.float32),
            pltpu.VMEM((members, members), jnp.float32),
            pltpu.SemaphoreType.DMA((2, count)),
            pltpu.SemaphoreType.DMA((2, count)),
        ],
        compiler_params=pltpu.CompilerParams(collective_id=0, has_side_effects=True),
    )(y, scale, obs, weights)


def transform_kernel(p_ref, x_ref, o_ref):
    rows = x_ref.shape[3]
    mix = p_ref[...]
    for i in range(rows):
        o_ref[:, 0, 0, i, :] = jnp.dot(mix, x_ref[:, 0, 0, i, :],
                                       precision=lax.Precision.HIGH, preferred_element_type=jnp.float32)


def apply_transform(carried, cells):
    members, levels, fields, rows, lanes = cells.shape
    block = pl.BlockSpec((members, 1, 1, rows, lanes), lambda a, b: (0, a, b, 0, 0))
    return pl.pallas_call(
        transform_kernel,
        out_shape=jax.ShapeDtypeStruct(cells.shape, cells.dtype),
        grid=(levels, fields),
        in_specs=[pl.BlockSpec((members, members), lambda a, b: (0, 0)), block],
        out_specs=block,
    )(carried, cells)


def on_device(
    background_sample,
    courant_eastward,
    courant_northward,
    diffusivity,
    sample_site,
    live_count,
    observed,
    error_variance,
    reach_mask,
):
    nx = lax.axis_size("gx")
    ny = lax.axis_size("gy")
    site_table = sample_site[0, 0]
    forecast, gathered = forecast_step(
        background_sample, courant_eastward, courant_northward, diffusivity, site_table.reshape(-1)
    )
    members = forecast.shape[0]
    counts = live_count[0, 0]
    observed_here = observed[0, 0]
    variance_here = error_variance[0, 0]
    batches, slot_count = site_table.shape
    slot_index = jnp.arange(slot_count)
    mask_index = jnp.arange(WIDTH)
    centre_one = ((mask_index[:, None] == RAD) & (mask_index[None, :] == RAD)).astype(jnp.float32)
    reach_weight = jnp.maximum(reach_mask[0, 0].astype(jnp.float32), centre_one).reshape(-1)
    all_sampled = gathered.reshape(members, batches, slot_count)
    y = jnp.transpose(all_sampled, (1, 0, 2))
    live_slot = (slot_index[None, :] < counts[:, None]).astype(jnp.float32)
    scale = (live_slot * (1.0 / jnp.sqrt(variance_here)))[:, None, :]
    carried = run_analysis(y, scale, observed_here[:, None, :], reach_weight, nx, ny)
    return apply_transform(carried, forecast)


def solution(mesh):
    in_specs = (
        P(None, None, None, "gx", "gy"),
        P(None, "gx", "gy"),
        P(None, "gx", "gy"),
        P("gx", "gy"),
        P("gx", "gy", None, None),
        P("gx", "gy", None),
        P("gx", "gy", None, None),
        P("gx", "gy", None, None),
        P("gx", "gy", None, None),
    )
    out_specs = P(None, None, None, "gx", "gy")
    return jax.shard_map(
        on_device, mesh=mesh, in_specs=in_specs, out_specs=out_specs, check_vma=False
    )
```

```python
import functools

import jax
import jax.numpy as jnp
from jax import lax
from jax.experimental import pallas as pl
from jax.experimental.pallas import tpu as pltpu
from jax.sharding import PartitionSpec as P

BATCHES = 4
RAD = 2
NS_STEPS = 6
WIDTH = 2 * RAD + 1
OFFSETS = [(dx, dy) for dx in range(-RAD, RAD + 1) for dy in range(-RAD, RAD + 1)]


def matmul_full(left, right):
    return jnp.dot(left, right, precision=lax.Precision.HIGHEST, preferred_element_type=jnp.float32)


def mixing_matrix(gram_matrix, projection):
    realisation_vectors = gram_matrix.shape[0]
    identity = jnp.eye(realisation_vectors, dtype=jnp.float32)
    precision_matrix = identity + gram_matrix / (realisation_vectors - 1)
    frobenius = jnp.sqrt(jnp.sum(precision_matrix * precision_matrix))
    iterate = precision_matrix / frobenius
    inverse = identity
    for repeat in range(NS_STEPS):
        factor = 1.5 * identity - 0.5 * matmul_full(inverse, iterate)
        iterate = matmul_full(iterate, factor)
        inverse = matmul_full(factor, inverse)
    transform = inverse / jnp.sqrt(frobenius)
    weights = matmul_full(transform, matmul_full(transform, projection)) / (realisation_vectors - 1)
    return transform + weights[:, None]


def stencil_kernel(x_ref, east_ref, west_ref, edge_ref, u_ref, v_ref, d_ref, col_ref, row_ref, o_ref, s_ref, east_scr, west_scr):
    rows = x_ref.shape[3]
    lanes = x_ref.shape[4]
    east_scr[:, :, :, 0 : rows - 1, :] = x_ref[:, :, :, 1:rows, :]
    east_scr[:, :, :, rows - 1 : rows, :] = east_ref[...]
    west_scr[:, :, :, 1:rows, :] = x_ref[:, :, :, 0 : rows - 1, :]
    west_scr[:, :, :, 0:1, :] = west_ref[...]
    centre = x_ref[...]
    east_cell = east_scr[...]
    west_cell = west_scr[...]
    edge = edge_ref[...]
    lane = lax.broadcasted_iota(jnp.int32, centre.shape, 4)
    north_cell = jnp.where(lane == lanes - 1, edge, pltpu.roll(centre, lanes - 1, 4))
    south_cell = jnp.where(lane == 0, edge, pltpu.roll(centre, 1, 4))
    u = u_ref[...][None, :, None]
    v = v_ref[...][None, :, None]
    d = d_ref[...][None, None, None]
    flux_x = jnp.maximum(u, 0.0) * (centre - west_cell) + jnp.minimum(u, 0.0) * (east_cell - centre)
    flux_y = jnp.maximum(v, 0.0) * (centre - south_cell) + jnp.minimum(v, 0.0) * (north_cell - centre)
    spread_term = d * (east_cell + west_cell + north_cell + south_cell - 4.0 * centre)
    result = centre + spread_term - flux_x - flux_y
    o_ref[...] = result
    block, rows_all = result.shape[0], result.shape[1] * result.shape[2] * rows
    flat = result.reshape(block * rows_all, lanes)
    high = flat.astype(jnp.bfloat16)
    rest = flat - high.astype(jnp.float32)
    mid = rest.astype(jnp.bfloat16)
    low = (rest - mid.astype(jnp.float32)).astype(jnp.bfloat16)
    pick = col_ref[...]
    picked = jnp.dot(high, pick, preferred_element_type=jnp.float32)
    picked = picked + jnp.dot(mid, pick, preferred_element_type=jnp.float32)
    picked = picked + jnp.dot(low, pick, preferred_element_type=jnp.float32)
    picked = picked.reshape(block, rows_all, picked.shape[-1]) * row_ref[...][None]
    s_ref[...] = jnp.sum(picked, axis=1)


def forecast_step(cells, courant_eastward, courant_northward, diffusivity, sites):
    nx = lax.axis_size("gx")
    ny = lax.axis_size("gy")
    rows, lanes = cells.shape[3], cells.shape[4]
    east_halo = lax.ppermute(cells[:, :, :, 0:1, :], "gx", [(i + 1, i) for i in range(nx - 1)])
    west_halo = lax.ppermute(cells[:, :, :, rows - 1 : rows, :], "gx", [(i, i + 1) for i in range(nx - 1)])
    lane_index = jnp.arange(lanes)
    pick = jnp.stack([lane_index == 0, lane_index == lanes - 1]).astype(jnp.float32)
    place = jnp.stack([lane_index == lanes - 1, lane_index == 0]).astype(jnp.float32)
    sides = jnp.einsum(
        "abcil,sl->sabci",
        cells, pick, precision=lax.Precision.HIGHEST, preferred_element_type=jnp.float32,
    )
    north_halo = lax.ppermute(sides[0], "gy", [(i + 1, i) for i in range(ny - 1)])
    south_halo = lax.ppermute(sides[1], "gy", [(i, i + 1) for i in range(ny - 1)])
    edge = jnp.einsum(
        "sabci,sl->abcil", jnp.stack([north_halo, south_halo]), place,
        precision=lax.Precision.HIGHEST, preferred_element_type=jnp.float32,
    )
    block = 8
    members = cells.shape[0]
    big = pl.BlockSpec((block,) + cells.shape[1:], lambda i: (i, 0, 0, 0, 0))
    thin = pl.BlockSpec((block,) + cells.shape[1:3] + (1, lanes), lambda i: (i, 0, 0, 0, 0))
    whole3 = pl.BlockSpec(courant_eastward.shape, lambda i: (0, 0, 0))
    whole2 = pl.BlockSpec(diffusivity.shape, lambda i: (0, 0))
    site_count = sites.shape[0]
    rows_all = cells.shape[1] * cells.shape[2] * rows
    col_pick = (sites[None, :] % lanes == jnp.arange(lanes)[:, None]).astype(jnp.bfloat16)
    row_pick = (sites[None, :] // lanes == jnp.arange(rows_all)[:, None]).astype(jnp.float32)
    picks = pl.BlockSpec((lanes, site_count), lambda i: (0, 0))
    return pl.pallas_call(
        stencil_kernel,
        out_shape=(
            jax.ShapeDtypeStruct(cells.shape, cells.dtype),
            jax.ShapeDtypeStruct((members, site_count), cells.dtype),
        ),
        grid=(members // block,),
        in_specs=[big, thin, thin, big, whole3, whole3, whole2, picks,
                  pl.BlockSpec((rows_all, site_count), lambda i: (0, 0))],
        out_specs=(big, pl.BlockSpec((block, site_count), lambda i: (i, 0))),
        scratch_shapes=[
            pltpu.VMEM((block,) + cells.shape[1:], cells.dtype),
            pltpu.VMEM((block,) + cells.shape[1:], cells.dtype),
        ],
    )(cells, east_halo, west_halo, edge, courant_eastward, courant_northward, diffusivity, col_pick, row_pick)


def mm(left, right):
    return jnp.dot(left, right, precision=lax.Precision.HIGHEST, preferred_element_type=jnp.float32)


def mm_nt(left, right):
    return lax.dot_general(
        left, right, (((1,), (1,)), ((), ())),
        precision=lax.Precision.HIGHEST, preferred_element_type=jnp.float32,
    )


def analysis_kernel(
    nx, ny, y_ref, scale_ref, obs_ref, w_ref, out_ref,
    slots, payload, rows_t, rows_u, total, carried, send_sem, recv_sem,
):
    me_x = lax.axis_index("gx")
    me_y = lax.axis_index("gy")
    members = y_ref.shape[1]
    slot_count = y_ref.shape[2]
    wide = payload.shape[2]
    batches = y_ref.shape[0]
    centre_k = RAD * WIDTH + RAD

    def inside(x, y):
        return (x >= 0) & (x < nx) & (y >= 0) & (y < ny)

    barrier = pltpu.get_barrier_semaphore()
    partners = jnp.int32(0)
    for dx, dy in OFFSETS:
        if dx == 0 and dy == 0:
            continue
        ok = inside(me_x - dx, me_y - dy)
        partners = partners + ok.astype(jnp.int32)

        @pl.when(ok)
        def _():
            pl.semaphore_signal(
                barrier, inc=1, device_id=(me_x - dx, me_y - dy),
                device_id_type=pl.DeviceIdType.MESH,
            )

    pl.semaphore_wait(barrier, partners)

    half = members // 2
    row = lax.broadcasted_iota(jnp.int32, (members, members), 0)
    col = lax.broadcasted_iota(jnp.int32, (members, members), 1)
    identity = (row == col).astype(jnp.float32)
    pair_row = lax.broadcasted_iota(jnp.int32, (half, members), 0)
    pair_col = lax.broadcasted_iota(jnp.int32, (half, members), 1)
    take_even = (pair_col == 2 * pair_row).astype(jnp.float32)
    take_odd = (pair_col == 2 * pair_row + 1).astype(jnp.float32)
    spread_row = lax.broadcasted_iota(jnp.int32, (members, half), 0)
    spread_col = lax.broadcasted_iota(jnp.int32, (members, half), 1)
    put_even = (spread_row == 2 * spread_col).astype(jnp.float32)
    put_odd = (spread_row == 2 * spread_col + 1).astype(jnp.float32)
    first_row = lax.broadcasted_iota(jnp.int32, (8, slot_count), 0) == 0
    carried[...] = identity
    rows_t[...] = jnp.zeros(rows_t.shape, jnp.float32)
    rows_u[...] = jnp.zeros(rows_u.shape, jnp.float32)

    def batch_step(b, _):
        par = b % 2
        sampled = mm(carried[...], y_ref[b])
        prior_mean = jnp.mean(sampled, axis=0, keepdims=True)
        scale = scale_ref[b]
        scaled_rows = scale * (sampled - prior_mean)
        innovation = scale * (obs_ref[b] - prior_mean)
        rows_t[0:members, :] = scaled_rows
        rows_u[members : 2 * members, :] = scaled_rows
        lead = mm_nt(mm(take_even, scaled_rows), rows_t[...]) + mm_nt(mm(take_odd, scaled_rows), rows_u[...])
        tail = mm_nt(jnp.where(first_row, innovation, 0.0), rows_t[...])
        payload[par, 0:half, :] = lead
        payload[par, half : half + 8, :] = tail

        copies = []
        for k, (dx, dy) in enumerate(OFFSETS):
            if dx == 0 and dy == 0:
                continue
            copy = pltpu.make_async_remote_copy(
                src_ref=payload.at[par],
                dst_ref=slots.at[par, k],
                send_sem=send_sem.at[par, k],
                recv_sem=recv_sem.at[par, k],
                device_id=(me_x - dx, me_y - dy),
                device_id_type=pl.DeviceIdType.MESH,
            )
            ok = inside(me_x - dx, me_y - dy)

            @pl.when(ok)
            def _():
                copy.start()

            copies.append((k, dx, dy, copy, ok))

        total[...] = jnp.zeros(total.shape, jnp.float32)
        for k, (dx, dy) in enumerate(OFFSETS):
            if dx == 0 and dy == 0:
                total[...] += w_ref[k] * payload[par]
        for k, dx, dy, copy, ok in copies:
            @pl.when(ok)
            def _():
                copy.wait_send()

            arrives = inside(me_x + dx, me_y + dy)

            @pl.when(arrives)
            def _():
                copy.wait_recv()
                total[...] += w_ref[k] * slots[par, k]

        summed = total[...]
        packed = summed[0:half, :]
        gram_total = mm(put_even, packed[:, 0:members]) + mm(put_odd, packed[:, members : 2 * members])
        proj_rows = summed[half : half + 8, 0:members]
        precision_matrix = identity + gram_total / (members - 1)
        squares = precision_matrix * precision_matrix
        frobenius = jnp.sqrt(jnp.sum(jnp.sum(squares, axis=1, keepdims=True), axis=0, keepdims=True))
        iterate = precision_matrix / frobenius

        def ns_step(_, pair):
            iterate, inverse = pair
            factor = 1.5 * identity - 0.5 * mm(inverse, iterate)
            both = mm(jnp.concatenate([iterate, inverse], axis=0), factor)
            return both[0:members], both[members : 2 * members]

        pair = (iterate, identity)
        for _i in range(NS_STEPS):
            pair = ns_step(_i, pair)
        iterate, inverse = pair
        transform = inverse / jnp.sqrt(frobenius)
        weights = mm_nt(mm_nt(proj_rows, transform), transform) / (members - 1)
        mixing_t = mm_nt(identity, transform) + weights[0:1, :]
        step = 1.0 / members + mixing_t - jnp.mean(mixing_t, axis=1, keepdims=True)
        carried[...] = mm(step, carried[...])
        return 0

    lax.fori_loop(0, batches, batch_step, 0)
    out_ref[...] = carried[...]


def run_analysis(y, scale, obs, weights, nx, ny):
    batches, members, slot_count = y.shape
    count = len(OFFSETS)
    wide = 2 * members
    packed_rows = members // 2 + 8
    return pl.pallas_call(
        functools.partial(analysis_kernel, nx, ny),
        out_shape=jax.ShapeDtypeStruct((members, members), jnp.float32),
        in_specs=[
            pl.BlockSpec(memory_space=pltpu.VMEM),
            pl.BlockSpec(memory_space=pltpu.VMEM),
            pl.BlockSpec(memory_space=pltpu.VMEM),
            pl.BlockSpec(memory_space=pltpu.SMEM),
        ],
        out_specs=pl.BlockSpec(memory_space=pltpu.VMEM),
        scratch_shapes=[
            pltpu.VMEM((2, count, packed_rows, wide), jnp.float32),
            pltpu.VMEM((2, packed_rows, wide), jnp.float32),
            pltpu.VMEM((wide, slot_count), jnp.float32),
            pltpu.VMEM((wide, slot_count), jnp.float32),
            pltpu.VMEM((packed_rows, wide), jnp.float32),
            pltpu.VMEM((members, members), jnp.float32),
            pltpu.SemaphoreType.DMA((2, count)),
            pltpu.SemaphoreType.DMA((2, count)),
        ],
        compiler_params=pltpu.CompilerParams(collective_id=0, has_side_effects=True),
    )(y, scale, obs, weights)


def transform_kernel(p_ref, x_ref, o_ref):
    rows = x_ref.shape[3]
    mix = p_ref[...]
    for i in range(rows):
        o_ref[:, 0, 0, i, :] = jnp.dot(mix, x_ref[:, 0, 0, i, :],
                                       precision=lax.Precision.HIGHEST, preferred_element_type=jnp.float32)


def apply_transform(carried, cells):
    members, levels, fields, rows, lanes = cells.shape
    block = pl.BlockSpec((members, 1, 1, rows, lanes), lambda a, b: (0, a, b, 0, 0))
    return pl.pallas_call(
        transform_kernel,
        out_shape=jax.ShapeDtypeStruct(cells.shape, cells.dtype),
        grid=(levels, fields),
        in_specs=[pl.BlockSpec((members, members), lambda a, b: (0, 0)), block],
        out_specs=block,
    )(carried, cells)


def on_device(
    background_sample,
    courant_eastward,
    courant_northward,
    diffusivity,
    sample_site,
    live_count,
    observed,
    error_variance,
    reach_mask,
):
    nx = lax.axis_size("gx")
    ny = lax.axis_size("gy")
    site_table = sample_site[0, 0]
    forecast, gathered = forecast_step(
        background_sample, courant_eastward, courant_northward, diffusivity, site_table.reshape(-1)
    )
    members = forecast.shape[0]
    counts = live_count[0, 0]
    observed_here = observed[0, 0]
    variance_here = error_variance[0, 0]
    batches, slot_count = site_table.shape
    slot_index = jnp.arange(slot_count)
    mask_index = jnp.arange(WIDTH)
    centre_one = ((mask_index[:, None] == RAD) & (mask_index[None, :] == RAD)).astype(jnp.float32)
    reach_weight = jnp.maximum(reach_mask[0, 0].astype(jnp.float32), centre_one).reshape(-1)
    all_sampled = gathered.reshape(members, batches, slot_count)
    y = jnp.transpose(all_sampled, (1, 0, 2))
    live_slot = (slot_index[None, :] < counts[:, None]).astype(jnp.float32)
    scale = (live_slot * (1.0 / jnp.sqrt(variance_here)))[:, None, :]
    carried = run_analysis(y, scale, observed_here[:, None, :], reach_weight, nx, ny)
    return apply_transform(carried, forecast)


def solution(mesh):
    in_specs = (
        P(None, None, None, "gx", "gy"),
        P(None, "gx", "gy"),
        P(None, "gx", "gy"),
        P("gx", "gy"),
        P("gx", "gy", None, None),
        P("gx", "gy", None),
        P("gx", "gy", None, None),
        P("gx", "gy", None, None),
        P("gx", "gy", None, None),
    )
    out_specs = P(None, None, None, "gx", "gy")
    return jax.shard_map(
        on_device, mesh=mesh, in_specs=in_specs, out_specs=out_specs, check_vma=False
    )
```

```python
import functools

import jax
import jax.numpy as jnp
from jax import lax
from jax.experimental import pallas as pl
from jax.experimental.pallas import tpu as pltpu
from jax.sharding import PartitionSpec as P

BATCHES = 4
RAD = 2
NS_STEPS = 6
WIDTH = 2 * RAD + 1
OFFSETS = [(dx, dy) for dx in range(-RAD, RAD + 1) for dy in range(-RAD, RAD + 1)]


def matmul_full(left, right):
    return jnp.dot(left, right, precision=lax.Precision.HIGHEST, preferred_element_type=jnp.float32)


def mixing_matrix(gram_matrix, projection):
    realisation_vectors = gram_matrix.shape[0]
    identity = jnp.eye(realisation_vectors, dtype=jnp.float32)
    precision_matrix = identity + gram_matrix / (realisation_vectors - 1)
    frobenius = jnp.sqrt(jnp.sum(precision_matrix * precision_matrix))
    iterate = precision_matrix / frobenius
    inverse = identity
    for repeat in range(NS_STEPS):
        factor = 1.5 * identity - 0.5 * matmul_full(inverse, iterate)
        iterate = matmul_full(iterate, factor)
        inverse = matmul_full(factor, inverse)
    transform = inverse / jnp.sqrt(frobenius)
    weights = matmul_full(transform, matmul_full(transform, projection)) / (realisation_vectors - 1)
    return transform + weights[:, None]


def stencil_kernel(x_ref, east_ref, west_ref, edge_ref, u_ref, v_ref, d_ref, col_ref, row_ref, o_ref, s_ref, east_scr, west_scr):
    rows = x_ref.shape[3]
    lanes = x_ref.shape[4]
    east_scr[:, :, :, 0 : rows - 1, :] = x_ref[:, :, :, 1:rows, :]
    east_scr[:, :, :, rows - 1 : rows, :] = east_ref[...]
    west_scr[:, :, :, 1:rows, :] = x_ref[:, :, :, 0 : rows - 1, :]
    west_scr[:, :, :, 0:1, :] = west_ref[...]
    centre = x_ref[...]
    east_cell = east_scr[...]
    west_cell = west_scr[...]
    edge = edge_ref[...]
    lane = lax.broadcasted_iota(jnp.int32, centre.shape, 4)
    north_cell = jnp.where(lane == lanes - 1, edge, pltpu.roll(centre, lanes - 1, 4))
    south_cell = jnp.where(lane == 0, edge, pltpu.roll(centre, 1, 4))
    u = u_ref[...][None, :, None]
    v = v_ref[...][None, :, None]
    d = d_ref[...][None, None, None]
    flux_x = jnp.maximum(u, 0.0) * (centre - west_cell) + jnp.minimum(u, 0.0) * (east_cell - centre)
    flux_y = jnp.maximum(v, 0.0) * (centre - south_cell) + jnp.minimum(v, 0.0) * (north_cell - centre)
    spread_term = d * (east_cell + west_cell + north_cell + south_cell - 4.0 * centre)
    result = centre + spread_term - flux_x - flux_y
    o_ref[...] = result
    block, rows_all = result.shape[0], result.shape[1] * result.shape[2] * rows
    flat = result.reshape(block * rows_all, lanes)
    high = flat.astype(jnp.bfloat16)
    rest = flat - high.astype(jnp.float32)
    mid = rest.astype(jnp.bfloat16)
    low = (rest - mid.astype(jnp.float32)).astype(jnp.bfloat16)
    pick = col_ref[...]
    picked = jnp.dot(high, pick, preferred_element_type=jnp.float32)
    picked = picked + jnp.dot(mid, pick, preferred_element_type=jnp.float32)
    picked = picked + jnp.dot(low, pick, preferred_element_type=jnp.float32)
    picked = picked.reshape(block, rows_all, picked.shape[-1]) * row_ref[...][None]
    s_ref[...] = jnp.sum(picked, axis=1)


def forecast_step(cells, courant_eastward, courant_northward, diffusivity, sites):
    nx = lax.axis_size("gx")
    ny = lax.axis_size("gy")
    rows, lanes = cells.shape[3], cells.shape[4]
    east_halo = lax.ppermute(cells[:, :, :, 0:1, :], "gx", [(i + 1, i) for i in range(nx - 1)])
    west_halo = lax.ppermute(cells[:, :, :, rows - 1 : rows, :], "gx", [(i, i + 1) for i in range(nx - 1)])
    lane_index = jnp.arange(lanes)
    pick = jnp.stack([lane_index == 0, lane_index == lanes - 1]).astype(jnp.float32)
    place = jnp.stack([lane_index == lanes - 1, lane_index == 0]).astype(jnp.float32)
    sides = jnp.einsum(
        "abcil,sl->sabci",
        cells, pick, precision=lax.Precision.HIGHEST, preferred_element_type=jnp.float32,
    )
    north_halo = lax.ppermute(sides[0], "gy", [(i + 1, i) for i in range(ny - 1)])
    south_halo = lax.ppermute(sides[1], "gy", [(i, i + 1) for i in range(ny - 1)])
    edge = jnp.einsum(
        "sabci,sl->abcil", jnp.stack([north_halo, south_halo]), place,
        precision=lax.Precision.HIGHEST, preferred_element_type=jnp.float32,
    )
    block = 8
    members = cells.shape[0]
    big = pl.BlockSpec((block,) + cells.shape[1:], lambda i: (i, 0, 0, 0, 0))
    thin = pl.BlockSpec((block,) + cells.shape[1:3] + (1, lanes), lambda i: (i, 0, 0, 0, 0))
    whole3 = pl.BlockSpec(courant_eastward.shape, lambda i: (0, 0, 0))
    whole2 = pl.BlockSpec(diffusivity.shape, lambda i: (0, 0))
    site_count = sites.shape[0]
    rows_all = cells.shape[1] * cells.shape[2] * rows
    col_pick = (sites[None, :] % lanes == jnp.arange(lanes)[:, None]).astype(jnp.bfloat16)
    row_pick = (sites[None, :] // lanes == jnp.arange(rows_all)[:, None]).astype(jnp.float32)
    picks = pl.BlockSpec((lanes, site_count), lambda i: (0, 0))
    return pl.pallas_call(
        stencil_kernel,
        out_shape=(
            jax.ShapeDtypeStruct(cells.shape, cells.dtype),
            jax.ShapeDtypeStruct((members, site_count), cells.dtype),
        ),
        grid=(members // block,),
        in_specs=[big, thin, thin, big, whole3, whole3, whole2, picks,
                  pl.BlockSpec((rows_all, site_count), lambda i: (0, 0))],
        out_specs=(big, pl.BlockSpec((block, site_count), lambda i: (i, 0))),
        scratch_shapes=[
            pltpu.VMEM((block,) + cells.shape[1:], cells.dtype),
            pltpu.VMEM((block,) + cells.shape[1:], cells.dtype),
        ],
    )(cells, east_halo, west_halo, edge, courant_eastward, courant_northward, diffusivity, col_pick, row_pick)


def mm(left, right):
    return jnp.dot(left, right, precision=lax.Precision.HIGHEST, preferred_element_type=jnp.float32)


def mm_nt(left, right):
    return lax.dot_general(
        left, right, (((1,), (1,)), ((), ())),
        precision=lax.Precision.HIGHEST, preferred_element_type=jnp.float32,
    )


def analysis_kernel(
    nx, ny, y_ref, scale_ref, obs_ref, w_ref, out_ref,
    slots, payload, rows_t, rows_u, total, carried, send_sem, recv_sem,
):
    me_x = lax.axis_index("gx")
    me_y = lax.axis_index("gy")
    members = y_ref.shape[1]
    slot_count = y_ref.shape[2]
    wide = payload.shape[2]
    batches = y_ref.shape[0]
    centre_k = RAD * WIDTH + RAD

    def inside(x, y):
        return (x >= 0) & (x < nx) & (y >= 0) & (y < ny)

    barrier = pltpu.get_barrier_semaphore()
    partners = jnp.int32(0)
    for dx, dy in OFFSETS:
        if dx == 0 and dy == 0:
            continue
        ok = inside(me_x - dx, me_y - dy)
        partners = partners + ok.astype(jnp.int32)

        @pl.when(ok)
        def _():
            pl.semaphore_signal(
                barrier, inc=1, device_id=(me_x - dx, me_y - dy),
                device_id_type=pl.DeviceIdType.MESH,
            )

    pl.semaphore_wait(barrier, partners)

    half = members // 2
    row = lax.broadcasted_iota(jnp.int32, (members, members), 0)
    col = lax.broadcasted_iota(jnp.int32, (members, members), 1)
    identity = (row == col).astype(jnp.float32)
    pair_row = lax.broadcasted_iota(jnp.int32, (half, members), 0)
    pair_col = lax.broadcasted_iota(jnp.int32, (half, members), 1)
    take_even = (pair_col == 2 * pair_row).astype(jnp.float32)
    take_odd = (pair_col == 2 * pair_row + 1).astype(jnp.float32)
    spread_row = lax.broadcasted_iota(jnp.int32, (members, half), 0)
    spread_col = lax.broadcasted_iota(jnp.int32, (members, half), 1)
    put_even = (spread_row == 2 * spread_col).astype(jnp.float32)
    put_odd = (spread_row == 2 * spread_col + 1).astype(jnp.float32)
    first_row = lax.broadcasted_iota(jnp.int32, (8, slot_count), 0) == 0
    carried[...] = identity
    rows_t[...] = jnp.zeros(rows_t.shape, jnp.float32)
    rows_u[...] = jnp.zeros(rows_u.shape, jnp.float32)

    def batch_step(b, _):
        par = b % 2
        sampled = mm(carried[...], y_ref[b])
        prior_mean = jnp.mean(sampled, axis=0, keepdims=True)
        scale = scale_ref[b]
        scaled_rows = scale * (sampled - prior_mean)
        innovation = scale * (obs_ref[b] - prior_mean)
        rows_t[0:members, :] = scaled_rows
        rows_u[members : 2 * members, :] = scaled_rows
        lead = mm_nt(mm(take_even, scaled_rows), rows_t[...]) + mm_nt(mm(take_odd, scaled_rows), rows_u[...])
        tail = mm_nt(jnp.where(first_row, innovation, 0.0), rows_t[...])
        payload[par, 0:half, :] = lead
        payload[par, half : half + 8, :] = tail

        copies = []
        for k, (dx, dy) in sorted(enumerate(OFFSETS), key=lambda item: -abs(item[1][0]) - abs(item[1][1])):
            if dx == 0 and dy == 0:
                continue
            copy = pltpu.make_async_remote_copy(
                src_ref=payload.at[par],
                dst_ref=slots.at[par, k],
                send_sem=send_sem.at[par, k],
                recv_sem=recv_sem.at[par, k],
                device_id=(me_x - dx, me_y - dy),
                device_id_type=pl.DeviceIdType.MESH,
            )
            ok = inside(me_x - dx, me_y - dy)

            @pl.when(ok)
            def _():
                copy.start()

            copies.append((k, dx, dy, copy, ok))

        total[...] = jnp.zeros(total.shape, jnp.float32)
        for k, (dx, dy) in enumerate(OFFSETS):
            if dx == 0 and dy == 0:
                total[...] += w_ref[k] * payload[par]
        for k, dx, dy, copy, ok in sorted(copies, key=lambda item: item[0]):
            arrives = inside(me_x + dx, me_y + dy)

            @pl.when(arrives)
            def _():
                copy.wait_recv()
                total[...] += w_ref[k] * slots[par, k]

        for k, dx, dy, copy, ok in copies:
            @pl.when(ok)
            def _():
                copy.wait_send()

        summed = total[...]
        packed = summed[0:half, :]
        gram_total = mm(put_even, packed[:, 0:members]) + mm(put_odd, packed[:, members : 2 * members])
        proj_rows = summed[half : half + 8, 0:members]
        precision_matrix = identity + gram_total / (members - 1)
        squares = precision_matrix * precision_matrix
        frobenius = jnp.sqrt(jnp.sum(jnp.sum(squares, axis=1, keepdims=True), axis=0, keepdims=True))
        iterate = precision_matrix / frobenius

        def ns_step(_, pair):
            iterate, inverse = pair
            factor = 1.5 * identity - 0.5 * mm(inverse, iterate)
            both = mm(jnp.concatenate([iterate, inverse], axis=0), factor)
            return both[0:members], both[members : 2 * members]

        pair = (iterate, identity)
        for _i in range(NS_STEPS):
            pair = ns_step(_i, pair)
        iterate, inverse = pair
        transform = inverse / jnp.sqrt(frobenius)
        weights = mm_nt(mm_nt(proj_rows, transform), transform) / (members - 1)
        mixing_t = mm_nt(identity, transform) + weights[0:1, :]
        step = 1.0 / members + mixing_t - jnp.mean(mixing_t, axis=1, keepdims=True)
        carried[...] = mm(step, carried[...])
        return 0

    lax.fori_loop(0, batches, batch_step, 0)
    out_ref[...] = carried[...]


def run_analysis(y, scale, obs, weights, nx, ny):
    batches, members, slot_count = y.shape
    count = len(OFFSETS)
    wide = 2 * members
    packed_rows = members // 2 + 8
    return pl.pallas_call(
        functools.partial(analysis_kernel, nx, ny),
        out_shape=jax.ShapeDtypeStruct((members, members), jnp.float32),
        in_specs=[
            pl.BlockSpec(memory_space=pltpu.VMEM),
            pl.BlockSpec(memory_space=pltpu.VMEM),
            pl.BlockSpec(memory_space=pltpu.VMEM),
            pl.BlockSpec(memory_space=pltpu.SMEM),
        ],
        out_specs=pl.BlockSpec(memory_space=pltpu.VMEM),
        scratch_shapes=[
            pltpu.VMEM((2, count, packed_rows, wide), jnp.float32),
            pltpu.VMEM((2, packed_rows, wide), jnp.float32),
            pltpu.VMEM((wide, slot_count), jnp.float32),
            pltpu.VMEM((wide, slot_count), jnp.float32),
            pltpu.VMEM((packed_rows, wide), jnp.float32),
            pltpu.VMEM((members, members), jnp.float32),
            pltpu.SemaphoreType.DMA((2, count)),
            pltpu.SemaphoreType.DMA((2, count)),
        ],
        compiler_params=pltpu.CompilerParams(collective_id=0, has_side_effects=True),
    )(y, scale, obs, weights)


def transform_kernel(p_ref, x_ref, o_ref):
    rows = x_ref.shape[3]
    mix = p_ref[...]
    for i in range(rows):
        o_ref[:, 0, 0, i, :] = jnp.dot(mix, x_ref[:, 0, 0, i, :],
                                       precision=lax.Precision.HIGH, preferred_element_type=jnp.float32)


def apply_transform(carried, cells):
    members, levels, fields, rows, lanes = cells.shape
    block = pl.BlockSpec((members, 1, 1, rows, lanes), lambda a, b: (0, a, b, 0, 0))
    return pl.pallas_call(
        transform_kernel,
        out_shape=jax.ShapeDtypeStruct(cells.shape, cells.dtype),
        grid=(levels, fields),
        in_specs=[pl.BlockSpec((members, members), lambda a, b: (0, 0)), block],
        out_specs=block,
    )(carried, cells)


def on_device(
    background_sample,
    courant_eastward,
    courant_northward,
    diffusivity,
    sample_site,
    live_count,
    observed,
    error_variance,
    reach_mask,
):
    nx = lax.axis_size("gx")
    ny = lax.axis_size("gy")
    site_table = sample_site[0, 0]
    forecast, gathered = forecast_step(
        background_sample, courant_eastward, courant_northward, diffusivity, site_table.reshape(-1)
    )
    members = forecast.shape[0]
    counts = live_count[0, 0]
    observed_here = observed[0, 0]
    variance_here = error_variance[0, 0]
    batches, slot_count = site_table.shape
    slot_index = jnp.arange(slot_count)
    mask_index = jnp.arange(WIDTH)
    centre_one = ((mask_index[:, None] == RAD) & (mask_index[None, :] == RAD)).astype(jnp.float32)
    reach_weight = jnp.maximum(reach_mask[0, 0].astype(jnp.float32), centre_one).reshape(-1)
    all_sampled = gathered.reshape(members, batches, slot_count)
    y = jnp.transpose(all_sampled, (1, 0, 2))
    live_slot = (slot_index[None, :] < counts[:, None]).astype(jnp.float32)
    scale = (live_slot * (1.0 / jnp.sqrt(variance_here)))[:, None, :]
    carried = run_analysis(y, scale, observed_here[:, None, :], reach_weight, nx, ny)
    return apply_transform(carried, forecast)


def solution(mesh):
    in_specs = (
        P(None, None, None, "gx", "gy"),
        P(None, "gx", "gy"),
        P(None, "gx", "gy"),
        P("gx", "gy"),
        P("gx", "gy", None, None),
        P("gx", "gy", None),
        P("gx", "gy", None, None),
        P("gx", "gy", None, None),
        P("gx", "gy", None, None),
    )
    out_specs = P(None, None, None, "gx", "gy")
    return jax.shard_map(
        on_device, mesh=mesh, in_specs=in_specs, out_specs=out_specs, check_vma=False
    )
```

```python
import functools

import jax
import jax.numpy as jnp
from jax import lax
from jax.experimental import pallas as pl
from jax.experimental.pallas import tpu as pltpu
from jax.sharding import PartitionSpec as P

BATCHES = 4
RAD = 2
NS_STEPS = 6
WIDTH = 2 * RAD + 1
OFFSETS = [(dx, dy) for dx in range(-RAD, RAD + 1) for dy in range(-RAD, RAD + 1)]


def matmul_full(left, right):
    return jnp.dot(left, right, precision=lax.Precision.HIGHEST, preferred_element_type=jnp.float32)


def mixing_matrix(gram_matrix, projection):
    realisation_vectors = gram_matrix.shape[0]
    identity = jnp.eye(realisation_vectors, dtype=jnp.float32)
    precision_matrix = identity + gram_matrix / (realisation_vectors - 1)
    frobenius = jnp.sqrt(jnp.sum(precision_matrix * precision_matrix))
    iterate = precision_matrix / frobenius
    inverse = identity
    for repeat in range(NS_STEPS):
        factor = 1.5 * identity - 0.5 * matmul_full(inverse, iterate)
        iterate = matmul_full(iterate, factor)
        inverse = matmul_full(factor, inverse)
    transform = inverse / jnp.sqrt(frobenius)
    weights = matmul_full(transform, matmul_full(transform, projection)) / (realisation_vectors - 1)
    return transform + weights[:, None]


def stencil_kernel(x_ref, east_ref, west_ref, edge_ref, u_ref, v_ref, d_ref, col_ref, row_ref, o_ref, s_ref, east_scr, west_scr):
    rows = x_ref.shape[3]
    lanes = x_ref.shape[4]
    east_scr[:, :, :, 0 : rows - 1, :] = x_ref[:, :, :, 1:rows, :]
    east_scr[:, :, :, rows - 1 : rows, :] = east_ref[...]
    west_scr[:, :, :, 1:rows, :] = x_ref[:, :, :, 0 : rows - 1, :]
    west_scr[:, :, :, 0:1, :] = west_ref[...]
    centre = x_ref[...]
    east_cell = east_scr[...]
    west_cell = west_scr[...]
    edge = edge_ref[...]
    lane = lax.broadcasted_iota(jnp.int32, centre.shape, 4)
    north_cell = jnp.where(lane == lanes - 1, edge, pltpu.roll(centre, lanes - 1, 4))
    south_cell = jnp.where(lane == 0, edge, pltpu.roll(centre, 1, 4))
    u = u_ref[...][None, :, None]
    v = v_ref[...][None, :, None]
    d = d_ref[...][None, None, None]
    flux_x = jnp.maximum(u, 0.0) * (centre - west_cell) + jnp.minimum(u, 0.0) * (east_cell - centre)
    flux_y = jnp.maximum(v, 0.0) * (centre - south_cell) + jnp.minimum(v, 0.0) * (north_cell - centre)
    spread_term = d * (east_cell + west_cell + north_cell + south_cell - 4.0 * centre)
    result = centre + spread_term - flux_x - flux_y
    o_ref[...] = result
    block, rows_all = result.shape[0], result.shape[1] * result.shape[2] * rows
    flat = result.reshape(block * rows_all, lanes)
    high = flat.astype(jnp.bfloat16)
    rest = flat - high.astype(jnp.float32)
    mid = rest.astype(jnp.bfloat16)
    low = (rest - mid.astype(jnp.float32)).astype(jnp.bfloat16)
    pick = col_ref[...]
    picked = jnp.dot(high, pick, preferred_element_type=jnp.float32)
    picked = picked + jnp.dot(mid, pick, preferred_element_type=jnp.float32)
    picked = picked + jnp.dot(low, pick, preferred_element_type=jnp.float32)
    picked = picked.reshape(block, rows_all, picked.shape[-1]) * row_ref[...][None]
    s_ref[...] = jnp.sum(picked, axis=1)


def forecast_step(cells, courant_eastward, courant_northward, diffusivity, sites):
    nx = lax.axis_size("gx")
    ny = lax.axis_size("gy")
    rows, lanes = cells.shape[3], cells.shape[4]
    east_halo = lax.ppermute(cells[:, :, :, 0:1, :], "gx", [(i + 1, i) for i in range(nx - 1)])
    west_halo = lax.ppermute(cells[:, :, :, rows - 1 : rows, :], "gx", [(i, i + 1) for i in range(nx - 1)])
    lane_index = jnp.arange(lanes)
    pick = jnp.stack([lane_index == 0, lane_index == lanes - 1]).astype(jnp.float32)
    place = jnp.stack([lane_index == lanes - 1, lane_index == 0]).astype(jnp.float32)
    sides = jnp.einsum(
        "abcil,sl->sabci",
        cells, pick, precision=lax.Precision.HIGHEST, preferred_element_type=jnp.float32,
    )
    north_halo = lax.ppermute(sides[0], "gy", [(i + 1, i) for i in range(ny - 1)])
    south_halo = lax.ppermute(sides[1], "gy", [(i, i + 1) for i in range(ny - 1)])
    edge = jnp.einsum(
        "sabci,sl->abcil", jnp.stack([north_halo, south_halo]), place,
        precision=lax.Precision.HIGHEST, preferred_element_type=jnp.float32,
    )
    block = 8
    members = cells.shape[0]
    big = pl.BlockSpec((block,) + cells.shape[1:], lambda i: (i, 0, 0, 0, 0))
    thin = pl.BlockSpec((block,) + cells.shape[1:3] + (1, lanes), lambda i: (i, 0, 0, 0, 0))
    whole3 = pl.BlockSpec(courant_eastward.shape, lambda i: (0, 0, 0))
    whole2 = pl.BlockSpec(diffusivity.shape, lambda i: (0, 0))
    site_count = sites.shape[0]
    rows_all = cells.shape[1] * cells.shape[2] * rows
    col_pick = (sites[None, :] % lanes == jnp.arange(lanes)[:, None]).astype(jnp.bfloat16)
    row_pick = (sites[None, :] // lanes == jnp.arange(rows_all)[:, None]).astype(jnp.float32)
    picks = pl.BlockSpec((lanes, site_count), lambda i: (0, 0))
    return pl.pallas_call(
        stencil_kernel,
        out_shape=(
            jax.ShapeDtypeStruct(cells.shape, cells.dtype),
            jax.ShapeDtypeStruct((members, site_count), cells.dtype),
        ),
        grid=(members // block,),
        in_specs=[big, thin, thin, big, whole3, whole3, whole2, picks,
                  pl.BlockSpec((rows_all, site_count), lambda i: (0, 0))],
        out_specs=(big, pl.BlockSpec((block, site_count), lambda i: (i, 0))),
        scratch_shapes=[
            pltpu.VMEM((block,) + cells.shape[1:], cells.dtype),
            pltpu.VMEM((block,) + cells.shape[1:], cells.dtype),
        ],
    )(cells, east_halo, west_halo, edge, courant_eastward, courant_northward, diffusivity, col_pick, row_pick)


def mm(left, right):
    return jnp.dot(left, right, precision=lax.Precision.HIGHEST, preferred_element_type=jnp.float32)


def mm_nt(left, right):
    return lax.dot_general(
        left, right, (((1,), (1,)), ((), ())),
        precision=lax.Precision.HIGHEST, preferred_element_type=jnp.float32,
    )


def analysis_kernel(
    nx, ny, y_ref, scale_ref, obs_ref, w_ref, out_ref,
    slots, payload, rows_t, rows_u, total, carried, send_sem, recv_sem,
):
    me_x = lax.axis_index("gx")
    me_y = lax.axis_index("gy")
    members = y_ref.shape[1]
    slot_count = y_ref.shape[2]
    wide = payload.shape[2]
    batches = y_ref.shape[0]
    centre_k = RAD * WIDTH + RAD

    def inside(x, y):
        return (x >= 0) & (x < nx) & (y >= 0) & (y < ny)

    barrier = pltpu.get_barrier_semaphore()
    partners = jnp.int32(0)
    for dx, dy in OFFSETS:
        if dx == 0 and dy == 0:
            continue
        ok = inside(me_x - dx, me_y - dy)
        partners = partners + ok.astype(jnp.int32)

        @pl.when(ok)
        def _():
            pl.semaphore_signal(
                barrier, inc=1, device_id=(me_x - dx, me_y - dy),
                device_id_type=pl.DeviceIdType.MESH,
            )

    pl.semaphore_wait(barrier, partners)

    half = members // 2
    row = lax.broadcasted_iota(jnp.int32, (members, members), 0)
    col = lax.broadcasted_iota(jnp.int32, (members, members), 1)
    identity = (row == col).astype(jnp.float32)
    pair_row = lax.broadcasted_iota(jnp.int32, (half, members), 0)
    pair_col = lax.broadcasted_iota(jnp.int32, (half, members), 1)
    take_even = (pair_col == 2 * pair_row).astype(jnp.float32)
    take_odd = (pair_col == 2 * pair_row + 1).astype(jnp.float32)
    spread_row = lax.broadcasted_iota(jnp.int32, (members, half), 0)
    spread_col = lax.broadcasted_iota(jnp.int32, (members, half), 1)
    put_even = (spread_row == 2 * spread_col).astype(jnp.float32)
    put_odd = (spread_row == 2 * spread_col + 1).astype(jnp.float32)
    first_row = lax.broadcasted_iota(jnp.int32, (8, slot_count), 0) == 0
    carried[...] = identity
    rows_t[...] = jnp.zeros(rows_t.shape, jnp.float32)
    rows_u[...] = jnp.zeros(rows_u.shape, jnp.float32)

    def batch_step(b, _):
        par = b % 2
        sampled = mm(carried[...], y_ref[b])
        prior_mean = jnp.mean(sampled, axis=0, keepdims=True)
        scale = scale_ref[b]
        scaled_rows = scale * (sampled - prior_mean)
        innovation = scale * (obs_ref[b] - prior_mean)
        rows_t[0:members, :] = scaled_rows
        rows_u[members : 2 * members, :] = scaled_rows
        lead = mm_nt(mm(take_even, scaled_rows), rows_t[...]) + mm_nt(mm(take_odd, scaled_rows), rows_u[...])
        tail = mm_nt(jnp.where(first_row, innovation, 0.0), rows_t[...])
        payload[par, 0:half, :] = lead
        payload[par, half : half + 8, :] = tail

        copies = []
        for k, (dx, dy) in sorted(enumerate(OFFSETS), key=lambda item: abs(item[1][0]) + abs(item[1][1])):
            if dx == 0 and dy == 0:
                continue
            copy = pltpu.make_async_remote_copy(
                src_ref=payload.at[par],
                dst_ref=slots.at[par, k],
                send_sem=send_sem.at[par, k],
                recv_sem=recv_sem.at[par, k],
                device_id=(me_x - dx, me_y - dy),
                device_id_type=pl.DeviceIdType.MESH,
            )
            ok = inside(me_x - dx, me_y - dy)

            @pl.when(ok)
            def _():
                copy.start()

            copies.append((k, dx, dy, copy, ok))

        total[...] = jnp.zeros(total.shape, jnp.float32)
        for k, (dx, dy) in enumerate(OFFSETS):
            if dx == 0 and dy == 0:
                total[...] += w_ref[k] * payload[par]
        for k, dx, dy, copy, ok in sorted(copies, key=lambda item: item[0]):
            @pl.when(ok)
            def _():
                copy.wait_send()

            arrives = inside(me_x + dx, me_y + dy)

            @pl.when(arrives)
            def _():
                copy.wait_recv()
                total[...] += w_ref[k] * slots[par, k]

        summed = total[...]
        packed = summed[0:half, :]
        gram_total = mm(put_even, packed[:, 0:members]) + mm(put_odd, packed[:, members : 2 * members])
        proj_rows = summed[half : half + 8, 0:members]
        precision_matrix = identity + gram_total / (members - 1)
        squares = precision_matrix * precision_matrix
        frobenius = jnp.sqrt(jnp.sum(jnp.sum(squares, axis=1, keepdims=True), axis=0, keepdims=True))
        iterate = precision_matrix / frobenius

        def ns_step(_, pair):
            iterate, inverse = pair
            factor = 1.5 * identity - 0.5 * mm(inverse, iterate)
            both = mm(jnp.concatenate([iterate, inverse], axis=0), factor)
            return both[0:members], both[members : 2 * members]

        pair = (iterate, identity)
        for _i in range(NS_STEPS):
            pair = ns_step(_i, pair)
        iterate, inverse = pair
        transform = inverse / jnp.sqrt(frobenius)
        weights = mm_nt(mm_nt(proj_rows, transform), transform) / (members - 1)
        mixing_t = mm_nt(identity, transform) + weights[0:1, :]
        step = 1.0 / members + mixing_t - jnp.mean(mixing_t, axis=1, keepdims=True)
        carried[...] = mm(step, carried[...])
        return 0

    lax.fori_loop(0, batches, batch_step, 0)
    out_ref[...] = carried[...]


def run_analysis(y, scale, obs, weights, nx, ny):
    batches, members, slot_count = y.shape
    count = len(OFFSETS)
    wide = 2 * members
    packed_rows = members // 2 + 8
    return pl.pallas_call(
        functools.partial(analysis_kernel, nx, ny),
        out_shape=jax.ShapeDtypeStruct((members, members), jnp.float32),
        in_specs=[
            pl.BlockSpec(memory_space=pltpu.VMEM),
            pl.BlockSpec(memory_space=pltpu.VMEM),
            pl.BlockSpec(memory_space=pltpu.VMEM),
            pl.BlockSpec(memory_space=pltpu.SMEM),
        ],
        out_specs=pl.BlockSpec(memory_space=pltpu.VMEM),
        scratch_shapes=[
            pltpu.VMEM((2, count, packed_rows, wide), jnp.float32),
            pltpu.VMEM((2, packed_rows, wide), jnp.float32),
            pltpu.VMEM((wide, slot_count), jnp.float32),
            pltpu.VMEM((wide, slot_count), jnp.float32),
            pltpu.VMEM((packed_rows, wide), jnp.float32),
            pltpu.VMEM((members, members), jnp.float32),
            pltpu.SemaphoreType.DMA((2, count)),
            pltpu.SemaphoreType.DMA((2, count)),
        ],
        compiler_params=pltpu.CompilerParams(collective_id=0, has_side_effects=True),
    )(y, scale, obs, weights)


def transform_kernel(p_ref, x_ref, o_ref):
    rows = x_ref.shape[3]
    mix = p_ref[...]
    for i in range(rows):
        o_ref[:, 0, 0, i, :] = jnp.dot(mix, x_ref[:, 0, 0, i, :],
                                       precision=lax.Precision.HIGH, preferred_element_type=jnp.float32)


def apply_transform(carried, cells):
    members, levels, fields, rows, lanes = cells.shape
    block = pl.BlockSpec((members, 1, 1, rows, lanes), lambda a, b: (0, a, b, 0, 0))
    return pl.pallas_call(
        transform_kernel,
        out_shape=jax.ShapeDtypeStruct(cells.shape, cells.dtype),
        grid=(levels, fields),
        in_specs=[pl.BlockSpec((members, members), lambda a, b: (0, 0)), block],
        out_specs=block,
    )(carried, cells)


def on_device(
    background_sample,
    courant_eastward,
    courant_northward,
    diffusivity,
    sample_site,
    live_count,
    observed,
    error_variance,
    reach_mask,
):
    nx = lax.axis_size("gx")
    ny = lax.axis_size("gy")
    site_table = sample_site[0, 0]
    forecast, gathered = forecast_step(
        background_sample, courant_eastward, courant_northward, diffusivity, site_table.reshape(-1)
    )
    members = forecast.shape[0]
    counts = live_count[0, 0]
    observed_here = observed[0, 0]
    variance_here = error_variance[0, 0]
    batches, slot_count = site_table.shape
    slot_index = jnp.arange(slot_count)
    mask_index = jnp.arange(WIDTH)
    centre_one = ((mask_index[:, None] == RAD) & (mask_index[None, :] == RAD)).astype(jnp.float32)
    reach_weight = jnp.maximum(reach_mask[0, 0].astype(jnp.float32), centre_one).reshape(-1)
    all_sampled = gathered.reshape(members, batches, slot_count)
    y = jnp.transpose(all_sampled, (1, 0, 2))
    live_slot = (slot_index[None, :] < counts[:, None]).astype(jnp.float32)
    scale = (live_slot * (1.0 / jnp.sqrt(variance_here)))[:, None, :]
    carried = run_analysis(y, scale, observed_here[:, None, :], reach_weight, nx, ny)
    return apply_transform(carried, forecast)


def solution(mesh):
    in_specs = (
        P(None, None, None, "gx", "gy"),
        P(None, "gx", "gy"),
        P(None, "gx", "gy"),
        P("gx", "gy"),
        P("gx", "gy", None, None),
        P("gx", "gy", None),
        P("gx", "gy", None, None),
        P("gx", "gy", None, None),
        P("gx", "gy", None, None),
    )
    out_specs = P(None, None, None, "gx", "gy")
    return jax.shard_map(
        on_device, mesh=mesh, in_specs=in_specs, out_specs=out_specs, check_vma=False
    )
```

```python
import functools

import jax
import jax.numpy as jnp
from jax import lax
from jax.experimental import pallas as pl
from jax.experimental.pallas import tpu as pltpu
from jax.sharding import PartitionSpec as P

BATCHES = 4
RAD = 2
NS_STEPS = 6
WIDTH = 2 * RAD + 1
OFFSETS = [(dx, dy) for dx in range(-RAD, RAD + 1) for dy in range(-RAD, RAD + 1)]


def matmul_full(left, right):
    return jnp.dot(left, right, precision=lax.Precision.HIGHEST, preferred_element_type=jnp.float32)


def mixing_matrix(gram_matrix, projection):
    realisation_vectors = gram_matrix.shape[0]
    identity = jnp.eye(realisation_vectors, dtype=jnp.float32)
    precision_matrix = identity + gram_matrix / (realisation_vectors - 1)
    frobenius = jnp.sqrt(jnp.sum(precision_matrix * precision_matrix))
    iterate = precision_matrix / frobenius
    inverse = identity
    for repeat in range(NS_STEPS):
        factor = 1.5 * identity - 0.5 * matmul_full(inverse, iterate)
        iterate = matmul_full(iterate, factor)
        inverse = matmul_full(factor, inverse)
    transform = inverse / jnp.sqrt(frobenius)
    weights = matmul_full(transform, matmul_full(transform, projection)) / (realisation_vectors - 1)
    return transform + weights[:, None]


def stencil_kernel(x_ref, east_ref, west_ref, edge_ref, u_ref, v_ref, d_ref, col_ref, row_ref, o_ref, s_ref, east_scr, west_scr):
    rows = x_ref.shape[3]
    lanes = x_ref.shape[4]
    east_scr[:, :, :, 0 : rows - 1, :] = x_ref[:, :, :, 1:rows, :]
    east_scr[:, :, :, rows - 1 : rows, :] = east_ref[...]
    west_scr[:, :, :, 1:rows, :] = x_ref[:, :, :, 0 : rows - 1, :]
    west_scr[:, :, :, 0:1, :] = west_ref[...]
    centre = x_ref[...]
    east_cell = east_scr[...]
    west_cell = west_scr[...]
    edge = edge_ref[...]
    lane = lax.broadcasted_iota(jnp.int32, centre.shape, 4)
    north_cell = jnp.where(lane == lanes - 1, edge, pltpu.roll(centre, lanes - 1, 4))
    south_cell = jnp.where(lane == 0, edge, pltpu.roll(centre, 1, 4))
    u = u_ref[...][None, :, None]
    v = v_ref[...][None, :, None]
    d = d_ref[...][None, None, None]
    flux_x = jnp.maximum(u, 0.0) * (centre - west_cell) + jnp.minimum(u, 0.0) * (east_cell - centre)
    flux_y = jnp.maximum(v, 0.0) * (centre - south_cell) + jnp.minimum(v, 0.0) * (north_cell - centre)
    spread_term = d * (east_cell + west_cell + north_cell + south_cell - 4.0 * centre)
    result = centre + spread_term - flux_x - flux_y
    o_ref[...] = result
    block, rows_all = result.shape[0], result.shape[1] * result.shape[2] * rows
    flat = result.reshape(block * rows_all, lanes)
    high = flat.astype(jnp.bfloat16)
    rest = flat - high.astype(jnp.float32)
    mid = rest.astype(jnp.bfloat16)
    low = (rest - mid.astype(jnp.float32)).astype(jnp.bfloat16)
    pick = col_ref[...]
    picked = jnp.dot(high, pick, preferred_element_type=jnp.float32)
    picked = picked + jnp.dot(mid, pick, preferred_element_type=jnp.float32)
    picked = picked + jnp.dot(low, pick, preferred_element_type=jnp.float32)
    picked = picked.reshape(block, rows_all, picked.shape[-1]) * row_ref[...][None]
    s_ref[...] = jnp.sum(picked, axis=1)


def forecast_step(cells, courant_eastward, courant_northward, diffusivity, sites):
    nx = lax.axis_size("gx")
    ny = lax.axis_size("gy")
    rows, lanes = cells.shape[3], cells.shape[4]
    east_halo = lax.ppermute(cells[:, :, :, 0:1, :], "gx", [(i + 1, i) for i in range(nx - 1)])
    west_halo = lax.ppermute(cells[:, :, :, rows - 1 : rows, :], "gx", [(i, i + 1) for i in range(nx - 1)])
    lane_index = jnp.arange(lanes)
    pick = jnp.stack([lane_index == 0, lane_index == lanes - 1]).astype(jnp.float32)
    place = jnp.stack([lane_index == lanes - 1, lane_index == 0]).astype(jnp.float32)
    sides = jnp.einsum(
        "abcil,sl->sabci",
        cells, pick, precision=lax.Precision.HIGHEST, preferred_element_type=jnp.float32,
    )
    north_halo = lax.ppermute(sides[0], "gy", [(i + 1, i) for i in range(ny - 1)])
    south_halo = lax.ppermute(sides[1], "gy", [(i, i + 1) for i in range(ny - 1)])
    edge = jnp.einsum(
        "sabci,sl->abcil", jnp.stack([north_halo, south_halo]), place,
        precision=lax.Precision.HIGHEST, preferred_element_type=jnp.float32,
    )
    block = 8
    members = cells.shape[0]
    big = pl.BlockSpec((block,) + cells.shape[1:], lambda i: (i, 0, 0, 0, 0))
    thin = pl.BlockSpec((block,) + cells.shape[1:3] + (1, lanes), lambda i: (i, 0, 0, 0, 0))
    whole3 = pl.BlockSpec(courant_eastward.shape, lambda i: (0, 0, 0))
    whole2 = pl.BlockSpec(diffusivity.shape, lambda i: (0, 0))
    site_count = sites.shape[0]
    rows_all = cells.shape[1] * cells.shape[2] * rows
    col_pick = (sites[None, :] % lanes == jnp.arange(lanes)[:, None]).astype(jnp.bfloat16)
    row_pick = (sites[None, :] // lanes == jnp.arange(rows_all)[:, None]).astype(jnp.float32)
    picks = pl.BlockSpec((lanes, site_count), lambda i: (0, 0))
    return pl.pallas_call(
        stencil_kernel,
        out_shape=(
            jax.ShapeDtypeStruct(cells.shape, cells.dtype),
            jax.ShapeDtypeStruct((members, site_count), cells.dtype),
        ),
        grid=(members // block,),
        in_specs=[big, thin, thin, big, whole3, whole3, whole2, picks,
                  pl.BlockSpec((rows_all, site_count), lambda i: (0, 0))],
        out_specs=(big, pl.BlockSpec((block, site_count), lambda i: (i, 0))),
        scratch_shapes=[
            pltpu.VMEM((block,) + cells.shape[1:], cells.dtype),
            pltpu.VMEM((block,) + cells.shape[1:], cells.dtype),
        ],
    )(cells, east_halo, west_halo, edge, courant_eastward, courant_northward, diffusivity, col_pick, row_pick)


def mm(left, right):
    return jnp.dot(left, right, precision=lax.Precision.HIGHEST, preferred_element_type=jnp.float32)


def mm_nt(left, right):
    return lax.dot_general(
        left, right, (((1,), (1,)), ((), ())),
        precision=lax.Precision.HIGHEST, preferred_element_type=jnp.float32,
    )


def analysis_kernel(
    nx, ny, y_ref, scale_ref, obs_ref, w_ref, out_ref,
    slots, payload, rows_t, rows_u, total, carried, send_sem, recv_sem,
):
    me_x = lax.axis_index("gx")
    me_y = lax.axis_index("gy")
    members = y_ref.shape[1]
    slot_count = y_ref.shape[2]
    wide = payload.shape[2]
    batches = y_ref.shape[0]
    centre_k = RAD * WIDTH + RAD

    def inside(x, y):
        return (x >= 0) & (x < nx) & (y >= 0) & (y < ny)

    barrier = pltpu.get_barrier_semaphore()
    partners = jnp.int32(0)
    for dx, dy in OFFSETS:
        if dx == 0 and dy == 0:
            continue
        ok = inside(me_x - dx, me_y - dy)
        partners = partners + ok.astype(jnp.int32)

        @pl.when(ok)
        def _():
            pl.semaphore_signal(
                barrier, inc=1, device_id=(me_x - dx, me_y - dy),
                device_id_type=pl.DeviceIdType.MESH,
            )

    pl.semaphore_wait(barrier, partners)

    half = members // 2
    row = lax.broadcasted_iota(jnp.int32, (members, members), 0)
    col = lax.broadcasted_iota(jnp.int32, (members, members), 1)
    identity = (row == col).astype(jnp.float32)
    pair_row = lax.broadcasted_iota(jnp.int32, (half, members), 0)
    pair_col = lax.broadcasted_iota(jnp.int32, (half, members), 1)
    take_even = (pair_col == 2 * pair_row).astype(jnp.float32)
    take_odd = (pair_col == 2 * pair_row + 1).astype(jnp.float32)
    spread_row = lax.broadcasted_iota(jnp.int32, (members, half), 0)
    spread_col = lax.broadcasted_iota(jnp.int32, (members, half), 1)
    put_even = (spread_row == 2 * spread_col).astype(jnp.float32)
    put_odd = (spread_row == 2 * spread_col + 1).astype(jnp.float32)
    first_row = lax.broadcasted_iota(jnp.int32, (8, slot_count), 0) == 0
    carried[...] = identity
    rows_t[...] = jnp.zeros(rows_t.shape, jnp.float32)
    rows_u[...] = jnp.zeros(rows_u.shape, jnp.float32)

    def batch_step(b, _):
        par = b % 2
        sampled = mm(carried[...], y_ref[b])
        prior_mean = jnp.mean(sampled, axis=0, keepdims=True)
        scale = scale_ref[b]
        scaled_rows = scale * (sampled - prior_mean)
        innovation = scale * (obs_ref[b] - prior_mean)
        rows_t[0:members, :] = scaled_rows
        rows_u[members : 2 * members, :] = scaled_rows
        lead = mm_nt(mm(take_even, scaled_rows), rows_t[...]) + mm_nt(mm(take_odd, scaled_rows), rows_u[...])
        tail = mm_nt(jnp.where(first_row, innovation, 0.0), rows_t[...])
        payload[par, 0:half, :] = lead
        payload[par, half : half + 8, :] = tail

        copies = []
        for k, (dx, dy) in enumerate(OFFSETS):
            if dx == 0 and dy == 0:
                continue
            copy = pltpu.make_async_remote_copy(
                src_ref=payload.at[par],
                dst_ref=slots.at[par, k],
                send_sem=send_sem.at[par, k],
                recv_sem=recv_sem.at[par, k],
                device_id=(me_x - dx, me_y - dy),
                device_id_type=pl.DeviceIdType.MESH,
            )
            ok = inside(me_x - dx, me_y - dy)

            @pl.when(ok)
            def _():
                copy.start()

            copies.append((k, dx, dy, copy, ok))

        total[...] = jnp.zeros(total.shape, jnp.float32)
        for k, (dx, dy) in enumerate(OFFSETS):
            if dx == 0 and dy == 0:
                total[...] += w_ref[k] * payload[par]
        for k, dx, dy, copy, ok in copies:
            @pl.when(ok)
            def _():
                copy.wait_send()

            arrives = inside(me_x + dx, me_y + dy)

            @pl.when(arrives)
            def _():
                copy.wait_recv()
                total[...] += w_ref[k] * slots[par, k]

        summed = total[...]
        packed = summed[0:half, :]
        gram_total = mm(put_even, packed[:, 0:members]) + mm(put_odd, packed[:, members : 2 * members])
        proj_rows = summed[half : half + 8, 0:members]
        precision_matrix = identity + gram_total / (members - 1)
        squares = precision_matrix * precision_matrix
        frobenius = jnp.sqrt(jnp.sum(jnp.sum(squares, axis=1, keepdims=True), axis=0, keepdims=True))
        iterate = precision_matrix / frobenius

        def ns_step(_, pair):
            iterate, inverse = pair
            factor = 1.5 * identity - 0.5 * mm(inverse, iterate)
            both = mm(jnp.concatenate([iterate, inverse], axis=0), factor)
            return both[0:members], both[members : 2 * members]

        pair = (iterate, identity)
        for _i in range(NS_STEPS):
            pair = ns_step(_i, pair)
        iterate, inverse = pair
        transform = inverse / jnp.sqrt(frobenius)
        weights = mm_nt(mm_nt(proj_rows, transform), transform) / (members - 1)
        mixing_t = mm_nt(identity, transform) + weights[0:1, :]
        step = 1.0 / members + mixing_t - jnp.mean(mixing_t, axis=1, keepdims=True)
        carried[...] = mm(step, carried[...])
        return 0

    lax.fori_loop(0, batches, batch_step, 0)
    out_ref[...] = carried[...]


def run_analysis(y, scale, obs, weights, nx, ny):
    batches, members, slot_count = y.shape
    count = len(OFFSETS)
    wide = 2 * members
    packed_rows = members // 2 + 8
    return pl.pallas_call(
        functools.partial(analysis_kernel, nx, ny),
        out_shape=jax.ShapeDtypeStruct((members, members), jnp.float32),
        in_specs=[
            pl.BlockSpec(memory_space=pltpu.VMEM),
            pl.BlockSpec(memory_space=pltpu.VMEM),
            pl.BlockSpec(memory_space=pltpu.VMEM),
            pl.BlockSpec(memory_space=pltpu.SMEM),
        ],
        out_specs=pl.BlockSpec(memory_space=pltpu.VMEM),
        scratch_shapes=[
            pltpu.VMEM((2, count, packed_rows, wide), jnp.float32),
            pltpu.VMEM((2, packed_rows, wide), jnp.float32),
            pltpu.VMEM((wide, slot_count), jnp.float32),
            pltpu.VMEM((wide, slot_count), jnp.float32),
            pltpu.VMEM((packed_rows, wide), jnp.float32),
            pltpu.VMEM((members, members), jnp.float32),
            pltpu.SemaphoreType.DMA((2, count)),
            pltpu.SemaphoreType.DMA((2, count)),
        ],
        compiler_params=pltpu.CompilerParams(collective_id=0, has_side_effects=True),
    )(y, scale, obs, weights)


def transform_kernel(p_ref, x_ref, o_ref):
    rows = x_ref.shape[3]
    mix = p_ref[...]
    for f in range(x_ref.shape[2]):
        for i in range(rows):
            o_ref[:, 0, f, i, :] = jnp.dot(mix, x_ref[:, 0, f, i, :],
                                           precision=lax.Precision.HIGH, preferred_element_type=jnp.float32)


def apply_transform(carried, cells):
    members, levels, fields, rows, lanes = cells.shape
    block = pl.BlockSpec((members, 1, 2, rows, lanes), lambda a, b: (0, a, b, 0, 0))
    return pl.pallas_call(
        transform_kernel,
        out_shape=jax.ShapeDtypeStruct(cells.shape, cells.dtype),
        grid=(levels, fields // 2),
        in_specs=[pl.BlockSpec((members, members), lambda a, b: (0, 0)), block],
        out_specs=block,
    )(carried, cells)


def on_device(
    background_sample,
    courant_eastward,
    courant_northward,
    diffusivity,
    sample_site,
    live_count,
    observed,
    error_variance,
    reach_mask,
):
    nx = lax.axis_size("gx")
    ny = lax.axis_size("gy")
    site_table = sample_site[0, 0]
    forecast, gathered = forecast_step(
        background_sample, courant_eastward, courant_northward, diffusivity, site_table.reshape(-1)
    )
    members = forecast.shape[0]
    counts = live_count[0, 0]
    observed_here = observed[0, 0]
    variance_here = error_variance[0, 0]
    batches, slot_count = site_table.shape
    slot_index = jnp.arange(slot_count)
    mask_index = jnp.arange(WIDTH)
    centre_one = ((mask_index[:, None] == RAD) & (mask_index[None, :] == RAD)).astype(jnp.float32)
    reach_weight = jnp.maximum(reach_mask[0, 0].astype(jnp.float32), centre_one).reshape(-1)
    all_sampled = gathered.reshape(members, batches, slot_count)
    y = jnp.transpose(all_sampled, (1, 0, 2))
    live_slot = (slot_index[None, :] < counts[:, None]).astype(jnp.float32)
    scale = (live_slot * (1.0 / jnp.sqrt(variance_here)))[:, None, :]
    carried = run_analysis(y, scale, observed_here[:, None, :], reach_weight, nx, ny)
    return apply_transform(carried, forecast)


def solution(mesh):
    in_specs = (
        P(None, None, None, "gx", "gy"),
        P(None, "gx", "gy"),
        P(None, "gx", "gy"),
        P("gx", "gy"),
        P("gx", "gy", None, None),
        P("gx", "gy", None),
        P("gx", "gy", None, None),
        P("gx", "gy", None, None),
        P("gx", "gy", None, None),
    )
    out_specs = P(None, None, None, "gx", "gy")
    return jax.shard_map(
        on_device, mesh=mesh, in_specs=in_specs, out_specs=out_specs, check_vma=False
    )
```
